32 devices in a mesh: ground: 16 (over z, x, core), pair: 2 (over y).
Axes of the slice: x: 2, y: 2, z: 4, core: 2. Of those that a mesh axis runs over, the one named last changes fastest.
Arguments:
- coregistered_sweeps: bfloat16 [2, 16, 512, 2, 512], P('pair', 'ground'), may hold values from -6 to 6
- shard_opening_height: int32 [1024], P('ground'), may hold values from 0 to 496
- shard_goal_patch: int32 [1024, 1], P('ground'), may hold values from 0 to 15; in each aligned block of 64 rows (0 to 63, 64 to 127, ...) at most 8 rows name the same one
- shard_patch_place: int32 [1024], P('ground'), may hold values from 0 to 31
Outputs:
- filtered: float32 [2, 1, 16, 2, 64, 64], P('pair', None, 'ground')
The draws below stay inside these ranges and needn't reach their ends.
Inputs may be any that keep to these rules, and one draw needn't show every extreme that they name: `shard_goal_patch`: among the 64 pieces of the bursts of one ground index, at most 8 name the same ground tile.
All inputs are finite; a program needn't handle non-finite values.
Results may differ from the reference program's by a relative error of at most 0.0023.
Values may be sent and summed in bfloat16 or wider, within the bound.
A program may use at most 320 MiB of HBM per device.

```python
import math
import jax
import jax.numpy as jnp
import numpy as np
from jax import lax

LOOK_ROWS = 4
LOOK_COLS = 16
SWEEP_HEIGHT = 512
SHARD_HEIGHT = 16
PIECE_DEV = 64
TILE_ROWS = 256
TILE_COLS = 1024
SWEEP_WIDTH = 512
PATCH_SHARD_LEVEL = 16
SLOTS = 32
SHARD_OVERALL = 1024
CAP = 8
PAIR_DEV = 1
N_GROUND = 16
N_PAIR = 2


def plant(entries, key, low, high):
    place = [jax.random.randint(jax.random.fold_in(key, axis), (), 0, length) for axis, length in enumerate(entries.shape)]
    widest = entries.shape.index(max(entries.shape))
    next_to = place[:widest] + [(place[widest] + 1) % entries.shape[widest]] + place[widest + 1:]
    return entries.at[tuple(place)].set(low).at[tuple(next_to)].set(high)


def levels(key, shape, cuts, least, high):
    def one(axis_at, parts):
        steps = jax.random.uniform(jax.random.fold_in(jax.random.fold_in(key, 6), axis_at), (parts,), jnp.float32, least / len(cuts), high / len(cuts))
        return jnp.repeat(jnp.exp(steps), shape[axis_at] // parts).reshape((-1,) + (1,) * (len(shape) - axis_at - 1))

    gain = one(*cuts[0])
    for cut in cuts[1:]:
        gain = gain * one(*cut)
    return gain


def assign_block(stream_key, own, number, rows, amount, top, bound, lean):
    order = jax.random.permutation(stream_key, amount)
    heavy_load, common = load_shares(amount, rows * top, bound, lean, True), load_shares(amount, rows * top, bound, lean, False)
    places = jnp.arange(amount)

    def named(sizes, rotation):
        used = int((sizes > 0).sum())
        fixed = max(1, used // 4)
        moved = fixed + (places - fixed + rotation * (used - fixed)) % max(1, amount - fixed)
        return jnp.zeros((amount,), jnp.int32).at[order[jnp.where(places < fixed, places, moved)]].set(jnp.asarray(sizes, jnp.int32))

    sizes = jnp.where(number % 4 == 0, named(heavy_load, number // 4), named(common, number - number // 4 - 1))
    mixed = jax.random.permutation(jax.random.fold_in(own, 3), amount)
    source_of, receiver = mixed[0:amount // 2 * 2:2], mixed[1:amount // 2 * 2:2]
    margin = jnp.minimum(sizes[source_of] - 1, bound - sizes[receiver]) // 2
    margin = jnp.where((source_of == order[0]) | (receiver == order[0]) | (sizes[receiver] == 0), 0, jnp.maximum(margin, 0))
    moved = jax.random.randint(jax.random.fold_in(own, 4), (amount // 2,), 0, 1 << 20) % (margin + 1)
    sizes = sizes.at[source_of].add(-moved).at[receiver].add(moved)
    members = jnp.searchsorted(jnp.cumsum(sizes), jnp.arange(rows * top), side="right").astype(jnp.int32)
    listing = members.reshape(top, rows).T
    listing = listing[jax.random.permutation(jax.random.fold_in(own, 1), rows)]
    rotation = jax.random.randint(jax.random.fold_in(own, 2), (rows, 1), 0, top)
    return jnp.take_along_axis(listing, (jnp.arange(top)[None, :] + rotation) % top, axis=1)


def load_shares(number_of, total, most, lean, full):
    portions = [(1 << 20) // math.isqrt(rank ** lean) + 1 for rank in range(1, number_of + 1)]
    largest = most if full else min(most, max(-(-total // number_of), total * portions[0] // sum(portions)))
    least = 1 if total - largest >= number_of - 1 else 0
    given, surplus = [largest] + [least] * (number_of - 1), total - largest - least * (number_of - 1)
    while surplus > 0:
        candidates = [i for i in range(1, number_of) if given[i] < largest] or [i for i in range(1, number_of) if given[i] < most]
        pool, left = sum([portions[i] for i in candidates]), surplus
        for i in candidates:
            extra = min(most - given[i], max(1, left * portions[i] // pool), surplus)
            given[i] = given[i] + extra
            surplus = surplus - extra
    return np.array(given)


def bell_draw(stream_key, shape, scale, limit, split=(), kind=jnp.bfloat16):
    drawn = scale * jax.random.normal(stream_key, shape, jnp.float32)
    if split:
        drawn = drawn * levels(stream_key, shape, split, -0.22, 0.18)
    return jnp.clip(drawn, -limit, limit).astype(kind)


def setup_inputs(seed: int = 0) -> dict:
    streams_of = jax.random.split(jax.random.key(seed), 5)
    coregistered_sweeps = bell_draw(streams_of[0], (N_PAIR, N_GROUND, SWEEP_HEIGHT, 2, SWEEP_WIDTH), 1.0, 6.0, ((0, 2), (1, 16)))
    shard_opening_height = plant(jax.random.randint(streams_of[1], (SHARD_OVERALL,), 0, SWEEP_HEIGHT - SHARD_HEIGHT + 1), jax.random.fold_in(streams_of[1], 1), 0, SWEEP_HEIGHT - SHARD_HEIGHT).astype(jnp.int32)
    shard_goal_patch_keys = jax.random.split(jax.random.fold_in(streams_of[2], 1), SHARD_OVERALL // PIECE_DEV)
    shard_goal_patch_turns = jax.random.permutation(jax.random.fold_in(streams_of[2], 3), SHARD_OVERALL // PIECE_DEV)
    shard_goal_patch = jax.vmap(lambda own, number: assign_block(jax.random.fold_in(streams_of[2], 2), own, number, PIECE_DEV, N_GROUND, 1, CAP, 2))(shard_goal_patch_keys, shard_goal_patch_turns).reshape((SHARD_OVERALL, 1))
    shard_patch_place = plant(jax.random.randint(streams_of[3], (SHARD_OVERALL,), 0, SLOTS), jax.random.fold_in(streams_of[3], 1), 0, SLOTS - 1).astype(jnp.int32)
    return {"coregistered_sweeps": coregistered_sweeps, "shard_opening_height": shard_opening_height, "shard_goal_patch": shard_goal_patch, "shard_patch_place": shard_patch_place}


def multilook(reference_tiles, secondary_tiles):
    first = reference_tiles.astype(jnp.float32)
    second = secondary_tiles.astype(jnp.float32)
    real_part = first[..., 0, :] * second[..., 0, :] + first[..., 1, :] * second[..., 1, :]
    imag_part = first[..., 1, :] * second[..., 0, :] - first[..., 0, :] * second[..., 1, :]
    joined = jnp.stack([real_part, imag_part], axis=-3)
    leading = joined.shape[:-2]
    row_count = joined.shape[-2]
    col_count = joined.shape[-1]
    boxes = joined.reshape(leading + (row_count // LOOK_ROWS, LOOK_ROWS, col_count // LOOK_COLS, LOOK_COLS))
    return jnp.mean(boxes, axis=(-3, -1))


def goldstein(looked):
    field = looked[..., 0, :, :] + 1j * looked[..., 1, :, :]
    spectrum = jnp.fft.fft2(field)
    weight = (spectrum.real ** 2 + spectrum.imag ** 2 + 1e-6) ** 0.25
    weight = weight / jnp.mean(weight, axis=(-2, -1), keepdims=True)
    result = jnp.fft.ifft2(spectrum * weight)
    return jnp.stack([result.real, result.imag], axis=-3).astype(jnp.float32)


def reference(coregistered_sweeps, shard_opening_height, shard_goal_patch, shard_patch_place):
    provider = (jnp.arange(SHARD_OVERALL) // PIECE_DEV).astype(jnp.int32)
    sweep_height_offset = shard_opening_height[:, None] + jnp.arange(SHARD_HEIGHT, dtype=jnp.int32)[None, :]
    slot_key = shard_goal_patch[:, 0] * SLOTS + shard_patch_place
    counts = jax.ops.segment_sum(jnp.ones((SHARD_OVERALL,), jnp.float32), slot_key, num_segments=N_GROUND * SLOTS)
    divisor = jnp.maximum(counts, 1.0)

    def compose_earth_patches(radar_pass):
        shards = radar_pass[provider[:, None], sweep_height_offset].astype(jnp.float32)
        totals = jax.ops.segment_sum(shards, slot_key, num_segments=N_GROUND * SLOTS)
        smoothed_pixel_mean = (totals / divisor[:, None, None, None]).astype(jnp.bfloat16)
        refolded_patches = smoothed_pixel_mean.reshape(N_GROUND, PATCH_SHARD_LEVEL, 2, SHARD_HEIGHT, 2, SWEEP_WIDTH)
        return refolded_patches.transpose(0, 1, 3, 4, 2, 5).reshape(N_GROUND, TILE_ROWS, 2, TILE_COLS)

    earth_patch_pile = lax.map(compose_earth_patches, coregistered_sweeps)

    def per_acquisition(index):
        secondary = earth_patch_pile[index]
        order = jnp.arange(PAIR_DEV, dtype=jnp.int32)
        partners = (order + (order >= index).astype(jnp.int32)).astype(jnp.int32)

        def per_pair(other):
            return goldstein(multilook(earth_patch_pile[other], secondary))

        return lax.map(per_pair, partners)

    return lax.map(per_acquisition, jnp.arange(N_PAIR, dtype=jnp.int32))
```

```python
import functools
import math

import jax
import jax.numpy as jnp
import numpy as np
from jax import lax
from jax.experimental import pallas as pl
from jax.experimental.pallas import tpu as pltpu
from jax.sharding import PartitionSpec as P

LOOK_ROWS = 4
LOOK_COLS = 16
SHARD_HEIGHT = 16
TILE_ROWS = 256
TILE_COLS = 1024
SWEEP_WIDTH = 512
PATCH_SHARD_LEVEL = 16
SLOTS = 32


def multilook(reference_tiles, secondary_tiles):
    first = reference_tiles.astype(jnp.float32)
    second = secondary_tiles.astype(jnp.float32)
    real_part = first[..., 0, :] * second[..., 0, :] + first[..., 1, :] * second[..., 1, :]
    imag_part = first[..., 1, :] * second[..., 0, :] - first[..., 0, :] * second[..., 1, :]
    joined = jnp.stack([real_part, imag_part], axis=-3)
    leading = joined.shape[:-2]
    row_count = joined.shape[-2]
    col_count = joined.shape[-1]
    boxes = joined.reshape(
        leading + (row_count // LOOK_ROWS, LOOK_ROWS, col_count // LOOK_COLS, LOOK_COLS)
    )
    return jnp.mean(boxes, axis=(-3, -1))


def on_left(matrix, field):
    return jnp.einsum("ij,...jk->...ik", matrix, field, precision=lax.Precision.HIGHEST)


def on_right(field, matrix):
    return jnp.einsum("...ij,jk->...ik", field, matrix, precision=lax.Precision.HIGHEST)


def goldstein(looked):
    length = looked.shape[-1]
    positions = jnp.arange(length, dtype=jnp.int32)
    phase = positions[:, None] * positions[None, :] % length
    angle = phase.astype(jnp.float32) * (2.0 * math.pi / length)
    cosine = jnp.cos(angle)
    sine = jnp.sin(angle)
    real_in = looked[..., 0, :, :]
    imag_in = looked[..., 1, :, :]
    half_real = on_left(cosine, real_in) + on_left(sine, imag_in)
    half_imag = on_left(cosine, imag_in) - on_left(sine, real_in)
    spec_real = on_right(half_real, cosine) + on_right(half_imag, sine)
    spec_imag = on_right(half_imag, cosine) - on_right(half_real, sine)
    weight = (spec_real * spec_real + spec_imag * spec_imag + 1e-06) ** 0.25
    weight = weight / jnp.mean(weight, axis=(-2, -1), keepdims=True)
    spec_real = spec_real * weight
    spec_imag = spec_imag * weight
    back_real = on_left(cosine, spec_real) - on_left(sine, spec_imag)
    back_imag = on_left(cosine, spec_imag) + on_left(sine, spec_real)
    out_real = on_right(back_real, cosine) - on_right(back_imag, sine)
    out_imag = on_right(back_imag, cosine) + on_right(back_real, sine)
    scale = 1.0 / (length * length)
    return jnp.stack([out_real * scale, out_imag * scale], axis=-3)


def partners_of(index, pair_width):
    order = jnp.arange(pair_width, dtype=jnp.int32)
    return order + (order >= index).astype(jnp.int32)


def local(coregistered_sweeps, shard_opening_height, shard_goal_patch, shard_patch_place):
    earth_patch_total_size = lax.axis_size("ground")
    pair_count = lax.axis_size("pair")
    piece_count = shard_opening_height.shape[0]
    place_allowance = max(
        2, (2 * piece_count + earth_patch_total_size - 1) // earth_patch_total_size
    )
    sweep_resident = coregistered_sweeps[0, 0]
    target = shard_goal_patch[:, 0]
    hits = (target[:, None] == jnp.arange(earth_patch_total_size, dtype=jnp.int32)[None, :]).astype(
        jnp.int32
    )
    order = jnp.arange(piece_count, dtype=jnp.int32)
    before = (order[None, :] < order[:, None]).astype(jnp.bfloat16)
    earlier = jnp.dot(before, hits.astype(jnp.bfloat16), preferred_element_type=jnp.float32).astype(jnp.int32)
    rank = jnp.sum(earlier * hits, axis=1)
    position = target * place_allowance + rank
    matches = (
        position[None, :]
        == jnp.arange(earth_patch_total_size * place_allowance, dtype=jnp.int32)[:, None]
    ).astype(jnp.int32)
    tiles_filled = jnp.sum(matches, axis=1) > 0
    sweep_height_offset = (
        jnp.sum(matches * shard_opening_height[None, :], axis=1)[:, None] + jnp.arange(SHARD_HEIGHT, dtype=jnp.int32)[None, :]
    )
    wanted = jnp.where(tiles_filled[:, None], sweep_height_offset, -1).reshape(-1)
    picked = wanted[:, None] == jnp.arange(sweep_resident.shape[0], dtype=jnp.int32)[None, :]
    pieces_to_send = jnp.dot(
        picked.astype(jnp.bfloat16),
        sweep_resident.reshape(sweep_resident.shape[0], -1),
        preferred_element_type=jnp.float32,
    ).astype(jnp.bfloat16)
    labels = jnp.sum(matches * (shard_patch_place + 1)[None, :], axis=1).astype(jnp.bfloat16)
    received_pieces, arrived_labels = (
        lax.all_to_all(
            pieces_to_send.reshape(
                earth_patch_total_size, place_allowance, SHARD_HEIGHT, 2, SWEEP_WIDTH
            ),
            "ground",
            split_axis=0,
            concat_axis=0,
            tiled=True,
        ),
        lax.all_to_all(
            labels.reshape(earth_patch_total_size, place_allowance),
            "ground",
            split_axis=0,
            concat_axis=0,
            tiled=True,
        ),
    )
    pieces_flattened = received_pieces.reshape(
        earth_patch_total_size * place_allowance, SHARD_HEIGHT * 2 * SWEEP_WIDTH
    )
    slot_labels = (jnp.arange(SLOTS, dtype=jnp.int32) + 1).astype(jnp.bfloat16)
    selector = arrived_labels.reshape(-1)[None, :] == slot_labels[:, None]
    totals = jnp.dot(
        selector.astype(jnp.bfloat16), pieces_flattened, preferred_element_type=jnp.float32
    )
    counts = jnp.sum(selector.astype(jnp.float32), axis=1)
    smoothed_pixel_mean = (totals / jnp.maximum(counts, 1.0)[:, None]).astype(jnp.bfloat16)
    ground_tile = (
        smoothed_pixel_mean.reshape(PATCH_SHARD_LEVEL, 2, SHARD_HEIGHT, 2, SWEEP_WIDTH)
        .transpose(0, 2, 3, 1, 4)
        .reshape(TILE_ROWS, 2, TILE_COLS)
    )
    pair_width = pair_count - 1
    own_refs = partners_of(lax.axis_index("pair"), pair_width)
    piece = lax.all_gather(ground_tile[None], "pair", axis=0, tiled=True)
    looked_piece = multilook(piece, ground_tile[None])
    indices = jnp.arange(piece.shape[0], dtype=jnp.int32)
    selection = (own_refs[:, None] == indices[None, :]).astype(jnp.float32)
    looked = jnp.einsum("kn,nabc->kabc", selection, looked_piece, precision=lax.Precision.HIGHEST)
    return goldstein(looked)[None, :, None]


CAP_VMEM = 48 * 1024 * 1024
MESH = pl.DeviceIdType.MESH
EXACT = lax.Precision.HIGHEST
COLS = 16
LANES = 128


def fused_kernel(
    sweep_hbm, opening_hbm, goal_hbm, place_hbm, part_hbm, widen_hbm, row_dft_hbm, left_hbm, back_hbm,
    out,
    sweep, ints, part, widen, row_dft, left, back_mat, outgoing, arrived, meta_out, meta, tops, rows, gathered,
    looked_out, looked_in, load_sem, part_sem, send_sem, recv_sem, meta_send, meta_recv, top_sem, own_sem,
    look_send, look_recv,
):
    me = lax.axis_index("ground")
    mine = lax.axis_index("pair")
    tile_count = meta.shape[0]
    level_count = tile_count // 4
    level = me // 4
    spot = lax.rem(me, 4)
    self_id = me * 2 + mine
    device_count = 2 * tile_count
    barrier = pltpu.get_barrier_semaphore()

    def greet(step, carry):
        pl.semaphore_signal(
            barrier, inc=1,
            device_id={"ground": lax.rem(me + step // 2, tile_count), "pair": lax.rem(mine + step, 2)},
            device_id_type=MESH,
        )
        return carry

    loads = [
        pltpu.make_async_copy(source, sink, load_sem.at[at])
        for at, (source, sink) in enumerate(
            [
                (sweep_hbm, sweep),
                (opening_hbm, ints.at[0]),
                (goal_hbm, ints.at[1]),
                (place_hbm, ints.at[2]),
                (widen_hbm, widen),
                (row_dft_hbm, row_dft),
                (left_hbm, left),
                (back_hbm, back_mat),
            ]
        )
    ]
    for copy in loads[:4]:
        copy.start()

    def spot_of(step):
        return lax.rem(spot // 2 + step // 2, 2) * 2 + lax.rem(spot + step, 2)

    parts = [
        pltpu.make_async_copy(part_hbm.at[spot_of(step)], part.at[step], part_sem.at[step]) for step in range(4)
    ]
    for copy in parts:
        copy.start()
    for copy in loads[4:]:
        copy.start()
    lax.fori_loop(1, device_count, greet, 0)

    def block(step, far, other):
        level_to = lax.rem(level + far, level_count)
        ground = level_to * 4 + spot_of(step)
        return ground, pltpu.make_async_remote_copy(
            src_ref=outgoing.at[step, other, level_to],
            dst_ref=arrived.at[me, mine],
            send_sem=send_sem.at[ground, other],
            recv_sem=recv_sem.at[me, mine],
            device_id={"ground": ground, "pair": other},
            device_id_type=MESH,
        )

    def arrival(source, other):
        return pltpu.make_async_remote_copy(
            src_ref=outgoing.at[0, 0, 0],
            dst_ref=arrived.at[source, other],
            send_sem=send_sem.at[source, other],
            recv_sem=recv_sem.at[source, other],
            device_id={"ground": source, "pair": other},
            device_id_type=MESH,
        )

    own_block = pltpu.make_async_copy(outgoing.at[0, mine, level], arrived.at[me, mine], own_sem.at[0])
    own_meta = pltpu.make_async_copy(meta_out, meta.at[me], own_sem.at[1])

    def label(target, source):
        return pltpu.make_async_remote_copy(
            src_ref=meta_out,
            dst_ref=meta.at[source],
            send_sem=meta_send.at[target],
            recv_sem=meta_recv.at[source],
            device_id={"ground": target, "pair": mine},
            device_id_type=MESH,
        )

    for copy in loads[1:4]:
        copy.wait()
    meta_out[...] = jnp.concatenate([ints[0] * 2, ints[1] * SLOTS + ints[2]], axis=1)
    own_meta.start()
    loads[0].wait()

    for step in range(4):
        parts[step].wait()
        for at in range(level_count):
            wide = jnp.concatenate(
                [
                    sweep[row * 64:(row + 1) * 64, :, at * LANES:(at + 1) * LANES].reshape(LANES, LANES)
                    for row in range(8)
                ],
                axis=1,
            )
            moved = jnp.dot(wide, part[step], preferred_element_type=jnp.float32).astype(jnp.bfloat16)
            outgoing[step, 0, at] = moved[:, :LANES]
            outgoing[step, 1, at] = moved[:, LANES:]
        if step == 0:
            pl.semaphore_wait(barrier, device_count - 1)

            def tell(shift, carry):
                label(lax.rem(me + shift, tile_count), me).start()
                return carry

            lax.fori_loop(1, tile_count, tell, 0)
        for far in (2, 1, 3, 0):
            if step == 0 and far == 0:
                block(step, far, 1 - mine)[1].start()
                own_block.start()
            else:
                for other in range(2):
                    block(step, far, other)[1].start()

    own_meta.wait()

    def told(shift, carry):
        source = lax.rem(me + shift, tile_count)
        label(source, source).wait_recv()
        return carry

    lax.fori_loop(1, tile_count, told, 0)
    to_scalars = pltpu.make_async_copy(meta, tops, top_sem)
    to_scalars.start()
    for copy in loads[4:]:
        copy.wait()
    to_scalars.wait()

    lane8 = lax.broadcasted_iota(jnp.int32, (8, LANES), 1)
    piece_count = 64
    key_rows = []
    for step in range(4):
        for far in range(level_count):
            source = lax.rem(level + far, level_count) * 4 + spot_of(step)
            for other in range(2):
                if step == 0 and far == 0:
                    continue
                arrival(source, other).wait_recv()
            if step == 0 and far == 0:
                arrival(source, 1 - mine).wait_recv()
                own_block.wait()
            both = jnp.concatenate([arrived[source, 0], arrived[source, 1]], axis=1)
            position = step * level_count + far
            for quarter in range(4):
                spread = jnp.dot(both, widen[quarter], preferred_element_type=jnp.float32)
                rows[quarter * 256:quarter * 256 + LANES] = spread[:, :LANES]
                rows[quarter * 256 + LANES:quarter * 256 + 256] = spread[:, LANES:]

            def take(group, carry):
                for inner in range(8):
                    piece = group * 8 + inner
                    top = tops[source, 0, piece]
                    value = rows[pl.ds(top, 8), :]
                    for shift in range(1, 4):
                        value = jnp.where(lane8 < shift * 32, value, rows[pl.ds(top + 8 * shift, 8), :])
                    gathered[pl.ds(position * piece_count + piece, 8, stride=tile_count * piece_count), :] = value
                return carry

            lax.fori_loop(0, piece_count // 8, take, 0)
            line = meta[source]
            key_rows.append(line if position % 2 else pltpu.roll(line, 64, 1))

    lane1 = lax.broadcasted_iota(jnp.int32, (1, LANES), 1)
    keys = jnp.concatenate(
        [jnp.where(lane1 < 64, key_rows[2 * at], key_rows[2 * at + 1]) for at in range(tile_count // 2)], axis=1
    )
    slots = lax.broadcasted_iota(jnp.int32, (tile_count * SLOTS, tile_count * piece_count), 0)
    chosen = jnp.where(slots == keys, 1.0, 0.0).astype(jnp.bfloat16)
    count = jnp.dot(
        chosen, jnp.ones((tile_count * piece_count, LANES), jnp.bfloat16), preferred_element_type=jnp.float32
    )
    scale = 1.0 / jnp.maximum(count, 1.0)
    same = jnp.zeros((tile_count * SLOTS, LANES), jnp.float32)
    cross = same
    for pair_row in range(4):
        at = pair_row * 2 * tile_count * piece_count
        wide = jnp.concatenate(
            [
                gathered[at:at + tile_count * piece_count],
                gathered[at + tile_count * piece_count:at + 2 * tile_count * piece_count],
            ],
            axis=1,
        ).astype(jnp.bfloat16)
        total = jnp.dot(chosen, wide, preferred_element_type=jnp.float32)
        real = (total[:, :LANES] * scale).astype(jnp.bfloat16).astype(jnp.float32)
        imag = (total[:, LANES:] * scale).astype(jnp.bfloat16).astype(jnp.float32)
        real_other = pltpu.roll(real, LANES - COLS, 1)
        imag_other = pltpu.roll(imag, LANES - COLS, 1)
        same = same + real * real_other + imag * imag_other
        cross = cross + imag_other * real - real_other * imag
    lane = lax.broadcasted_iota(jnp.int32, same.shape, 1)
    merged = jnp.where(lane % 32 < COLS, same, pltpu.roll(cross, COLS, 1))
    row8 = lax.broadcasted_iota(jnp.int32, (8, LANES), 0)
    pool = jnp.where(lane8 // COLS == (row8 % 4) * 2 + row8 // 4, 1.0 / (LOOK_ROWS * LOOK_COLS), 0.0)
    pooled = lax.dot_general(
        pool, merged, (((1,), (1,)), ((), ())), precision=EXACT, preferred_element_type=jnp.float32
    )
    for group in range(tile_count // 4):
        piece = pooled[:, group * LANES:(group + 1) * LANES]
        turned = piece
        for shift in range(1, 4):
            moved = pltpu.roll(pltpu.roll(piece, LANES - 32 * shift, 1), 2 * shift, 0)
            turned = jnp.where((row8 // 2 - lane8 // 32 + 4) % 4 == shift, moved, turned)
        for inner in range(4):
            looked_out[group * 4 + inner] = turned[2 * inner:2 * inner + 2]

    def show(target, other):
        return pltpu.make_async_remote_copy(
            src_ref=looked_out.at[target],
            dst_ref=looked_in.at[self_id],
            send_sem=look_send.at[target, other],
            recv_sem=look_recv.at[self_id],
            device_id={"ground": target, "pair": other},
            device_id_type=MESH,
        )

    def shown(source, other):
        return pltpu.make_async_remote_copy(
            src_ref=looked_out.at[source],
            dst_ref=looked_in.at[source * 2 + other],
            send_sem=look_send.at[source, other],
            recv_sem=look_recv.at[source * 2 + other],
            device_id={"ground": source, "pair": other},
            device_id_type=MESH,
        )

    def partner(step):
        return lax.rem(me + step // 2, tile_count), lax.rem(mine + step, 2)

    def show_one(step, carry):
        show(*partner(step)).start()
        return carry

    lax.fori_loop(1, device_count, show_one, 0)
    own_look = pltpu.make_async_copy(looked_out.at[me], looked_in.at[self_id], own_sem.at[0])
    own_look.start()

    def sent(step, carry):
        ground, other = partner(step)
        pltpu.make_async_remote_copy(
            src_ref=outgoing.at[0, 0, 0],
            dst_ref=arrived.at[me, mine],
            send_sem=send_sem.at[ground, other],
            recv_sem=recv_sem.at[me, mine],
            device_id={"ground": ground, "pair": other},
            device_id_type=MESH,
        ).wait_send()
        return carry

    lax.fori_loop(1, device_count, sent, 0)

    def told_out(shift, carry):
        label(lax.rem(me + shift, tile_count), me).wait_send()
        return carry

    lax.fori_loop(1, tile_count, told_out, 0)

    def shown_one(step, carry):
        shown(*partner(step)).wait_recv()
        return carry

    lax.fori_loop(1, device_count, shown_one, 0)
    own_look.wait()

    def dot(a, b):
        return jnp.dot(a, b, precision=EXACT, preferred_element_type=jnp.float32)

    flip = 1.0 - 2.0 * mine.astype(jnp.float32)
    lanes = lax.broadcasted_iota(jnp.int32, (device_count, LANES), 1)
    sign = jnp.where(lanes < 64, 1.0, flip)
    field = jnp.concatenate([looked_in[:, 0, :] * sign, looked_in[:, 1, :] * sign], axis=1)
    field = dot(field, row_dft[...])
    field = jnp.concatenate([field[:, :LANES], field[:, LANES:]], axis=0)
    length = left.shape[1]
    turn = jnp.where(lax.broadcasted_iota(jnp.int32, (length, 2 * length), 1) < length, 1.0, -1.0)
    both = dot(left[...], field)
    spectrum = both[:length] + turn * pltpu.roll(both[length:], length, 1)
    power = spectrum * spectrum
    power = power + pltpu.roll(power, length, 1)
    weight = jnp.sqrt(jnp.sqrt(power + 1e-06))
    mean = jnp.sum(weight) * (1.0 / (2 * length * length))
    spectrum = spectrum * (weight / mean)
    both = dot(left[...], spectrum)
    back = both[:length] - turn * pltpu.roll(both[length:], length, 1)
    result = lax.dot_general(
        back_mat[...], back, (((1,), (1,)), ((), ())), precision=EXACT, preferred_element_type=jnp.float32
    ) * (1.0 / (length * length))
    out[0] = result[:length]
    out[1] = result[length:]

    def shown_out(step, carry):
        show(*partner(step)).wait_send()
        return carry

    lax.fori_loop(1, device_count, shown_out, 0)


def constants():
    row = np.arange(1024)
    col = np.arange(256)
    lane, group = row % 128, row // 128
    part = np.stack(
        [
            (lane[:, None] // 32 == spot)
            & (col[None, :] // 128 == lane[:, None] // 16 % 2)
            & (col[None, :] % 128 // 16 == group[:, None])
            & (col[None, :] % 16 == lane[:, None] % 16)
            for spot in range(4)
        ]
    ).astype(jnp.bfloat16)
    row = np.arange(256)
    widen = np.stack(
        [
            (row[:, None] // 128 == col[None, :] // 16 % 2)
            & (row[:, None] % 128 // 16 == 2 * quarter + col[None, :] // 128)
            & (row[:, None] % 16 == col[None, :] % 16)
            for quarter in range(4)
        ]
    ).astype(jnp.bfloat16)
    low, high, slot = row // 128, row % 128 // 32, row % 32
    kind, box = (2 * high + low) // 4, (2 * high + low) % 4
    line = slot // 2 * 4 + box
    out_side, out_kind, frequency = col // 128, col // 64 % 2, col % 64
    angle = (line[:, None] * frequency[None, :] % 64) * (2.0 * math.pi / 64)
    mixed = np.where(
        kind[:, None] == out_kind[None, :],
        np.cos(angle),
        np.where(kind[:, None] == 0, -np.sin(angle), np.sin(angle)),
    )
    row_dft = np.where(slot[:, None] % 2 == out_side[None, :], mixed, 0.0)
    column = np.arange(64)
    angle = (column[:, None] * column[None, :] % 64) * (2.0 * math.pi / 64)
    cosine, sine = np.cos(angle), np.sin(angle)
    left = np.concatenate([cosine, sine], 0)
    back = np.block([[cosine, -sine], [sine, cosine]])
    return (part, widen) + tuple(x.astype(np.float32) for x in (row_dft, left, back))


def local_pair(coregistered_sweeps, shard_opening_height, shard_goal_patch, shard_patch_place):
    tile_count = lax.axis_size("ground")
    tables = constants()
    vmem = pl.BlockSpec(memory_space=pltpu.VMEM)
    anyplace = pl.BlockSpec(memory_space=pl.ANY)
    dma = pltpu.SemaphoreType.DMA
    filtered = pl.pallas_call(
        fused_kernel,
        out_shape=jax.ShapeDtypeStruct((2, 64, 64), jnp.float32),
        in_specs=[anyplace] * 9,
        out_specs=vmem,
        scratch_shapes=[
            pltpu.VMEM((512, 2, 512), jnp.bfloat16),
            pltpu.VMEM((3, 1, 64), jnp.int32),
            pltpu.VMEM((4, 1024, 256), jnp.bfloat16),
            pltpu.VMEM((4, 256, 256), jnp.bfloat16),
            pltpu.VMEM((256, 256), jnp.float32),
            pltpu.VMEM((128, 64), jnp.float32),
            pltpu.VMEM((128, 128), jnp.float32),
            pltpu.VMEM((4, 2, 4, 128, 128), jnp.bfloat16),
            pltpu.VMEM((tile_count, 2, 128, 128), jnp.bfloat16),
            pltpu.VMEM((1, 128), jnp.int32),
            pltpu.VMEM((tile_count, 1, 128), jnp.int32),
            pltpu.SMEM((tile_count, 1, 128), jnp.int32),
            pltpu.VMEM((1024, 128), jnp.float32),
            pltpu.VMEM((8 * tile_count * 64, 128), jnp.float32),
            pltpu.VMEM((tile_count, 2, 128), jnp.float32),
            pltpu.VMEM((2 * tile_count, 2, 128), jnp.float32),
            dma((8,)),
            dma((4,)),
            dma((tile_count, 2)),
            dma((tile_count, 2)),
            dma((tile_count,)),
            dma((tile_count,)),
            dma,
            dma((2,)),
            dma((tile_count, 2)),
            dma((2 * tile_count,)),
        ],
        compiler_params=pltpu.CompilerParams(
            collective_id=0, has_side_effects=True, vmem_limit_bytes=CAP_VMEM
        ),
    )(
        coregistered_sweeps[0, 0],
        shard_opening_height.reshape(1, -1),
        shard_goal_patch.reshape(1, -1),
        shard_patch_place.reshape(1, -1),
        *tables,
    )
    return filtered[None, None, None]


def solution(mesh):
    placed = (P("pair", "ground", None, None, None), P("ground"), P("ground", None), P("ground"))
    return jax.shard_map(
        local_pair if dict(mesh.shape) == {"ground": 16, "pair": 2} else local,
        mesh=mesh,
        in_specs=placed,
        out_specs=P("pair", None, "ground", None, None, None),
        check_vma=False,
    )
```

```python
import functools
import math

import jax
import jax.numpy as jnp
import numpy as np
from jax import lax
from jax.experimental import pallas as pl
from jax.experimental.pallas import tpu as pltpu
from jax.sharding import PartitionSpec as P

LOOK_ROWS = 4
LOOK_COLS = 16
SHARD_HEIGHT = 16
TILE_ROWS = 256
TILE_COLS = 1024
SWEEP_WIDTH = 512
PATCH_SHARD_LEVEL = 16
SLOTS = 32


def multilook(reference_tiles, secondary_tiles):
    first = reference_tiles.astype(jnp.float32)
    second = secondary_tiles.astype(jnp.float32)
    real_part = first[..., 0, :] * second[..., 0, :] + first[..., 1, :] * second[..., 1, :]
    imag_part = first[..., 1, :] * second[..., 0, :] - first[..., 0, :] * second[..., 1, :]
    joined = jnp.stack([real_part, imag_part], axis=-3)
    leading = joined.shape[:-2]
    row_count = joined.shape[-2]
    col_count = joined.shape[-1]
    boxes = joined.reshape(
        leading + (row_count // LOOK_ROWS, LOOK_ROWS, col_count // LOOK_COLS, LOOK_COLS)
    )
    return jnp.mean(boxes, axis=(-3, -1))


def on_left(matrix, field):
    return jnp.einsum("ij,...jk->...ik", matrix, field, precision=lax.Precision.HIGHEST)


def on_right(field, matrix):
    return jnp.einsum("...ij,jk->...ik", field, matrix, precision=lax.Precision.HIGHEST)


def goldstein(looked):
    length = looked.shape[-1]
    positions = jnp.arange(length, dtype=jnp.int32)
    phase = positions[:, None] * positions[None, :] % length
    angle = phase.astype(jnp.float32) * (2.0 * math.pi / length)
    cosine = jnp.cos(angle)
    sine = jnp.sin(angle)
    real_in = looked[..., 0, :, :]
    imag_in = looked[..., 1, :, :]
    half_real = on_left(cosine, real_in) + on_left(sine, imag_in)
    half_imag = on_left(cosine, imag_in) - on_left(sine, real_in)
    spec_real = on_right(half_real, cosine) + on_right(half_imag, sine)
    spec_imag = on_right(half_imag, cosine) - on_right(half_real, sine)
    weight = (spec_real * spec_real + spec_imag * spec_imag + 1e-06) ** 0.25
    weight = weight / jnp.mean(weight, axis=(-2, -1), keepdims=True)
    spec_real = spec_real * weight
    spec_imag = spec_imag * weight
    back_real = on_left(cosine, spec_real) - on_left(sine, spec_imag)
    back_imag = on_left(cosine, spec_imag) + on_left(sine, spec_real)
    out_real = on_right(back_real, cosine) - on_right(back_imag, sine)
    out_imag = on_right(back_imag, cosine) + on_right(back_real, sine)
    scale = 1.0 / (length * length)
    return jnp.stack([out_real * scale, out_imag * scale], axis=-3)


def partners_of(index, pair_width):
    order = jnp.arange(pair_width, dtype=jnp.int32)
    return order + (order >= index).astype(jnp.int32)


def local(coregistered_sweeps, shard_opening_height, shard_goal_patch, shard_patch_place):
    earth_patch_total_size = lax.axis_size("ground")
    pair_count = lax.axis_size("pair")
    piece_count = shard_opening_height.shape[0]
    place_allowance = max(
        2, (2 * piece_count + earth_patch_total_size - 1) // earth_patch_total_size
    )
    sweep_resident = coregistered_sweeps[0, 0]
    target = shard_goal_patch[:, 0]
    hits = (target[:, None] == jnp.arange(earth_patch_total_size, dtype=jnp.int32)[None, :]).astype(
        jnp.int32
    )
    order = jnp.arange(piece_count, dtype=jnp.int32)
    before = (order[None, :] < order[:, None]).astype(jnp.bfloat16)
    earlier = jnp.dot(before, hits.astype(jnp.bfloat16), preferred_element_type=jnp.float32).astype(jnp.int32)
    rank = jnp.sum(earlier * hits, axis=1)
    position = target * place_allowance + rank
    matches = (
        position[None, :]
        == jnp.arange(earth_patch_total_size * place_allowance, dtype=jnp.int32)[:, None]
    ).astype(jnp.int32)
    tiles_filled = jnp.sum(matches, axis=1) > 0
    sweep_height_offset = (
        jnp.sum(matches * shard_opening_height[None, :], axis=1)[:, None] + jnp.arange(SHARD_HEIGHT, dtype=jnp.int32)[None, :]
    )
    wanted = jnp.where(tiles_filled[:, None], sweep_height_offset, -1).reshape(-1)
    picked = wanted[:, None] == jnp.arange(sweep_resident.shape[0], dtype=jnp.int32)[None, :]
    pieces_to_send = jnp.dot(
        picked.astype(jnp.bfloat16),
        sweep_resident.reshape(sweep_resident.shape[0], -1),
        preferred_element_type=jnp.float32,
    ).astype(jnp.bfloat16)
    labels = jnp.sum(matches * (shard_patch_place + 1)[None, :], axis=1).astype(jnp.bfloat16)
    received_pieces, arrived_labels = (
        lax.all_to_all(
            pieces_to_send.reshape(
                earth_patch_total_size, place_allowance, SHARD_HEIGHT, 2, SWEEP_WIDTH
            ),
            "ground",
            split_axis=0,
            concat_axis=0,
            tiled=True,
        ),
        lax.all_to_all(
            labels.reshape(earth_patch_total_size, place_allowance),
            "ground",
            split_axis=0,
            concat_axis=0,
            tiled=True,
        ),
    )
    pieces_flattened = received_pieces.reshape(
        earth_patch_total_size * place_allowance, SHARD_HEIGHT * 2 * SWEEP_WIDTH
    )
    slot_labels = (jnp.arange(SLOTS, dtype=jnp.int32) + 1).astype(jnp.bfloat16)
    selector = arrived_labels.reshape(-1)[None, :] == slot_labels[:, None]
    totals = jnp.dot(
        selector.astype(jnp.bfloat16), pieces_flattened, preferred_element_type=jnp.float32
    )
    counts = jnp.sum(selector.astype(jnp.float32), axis=1)
    smoothed_pixel_mean = (totals / jnp.maximum(counts, 1.0)[:, None]).astype(jnp.bfloat16)
    ground_tile = (
        smoothed_pixel_mean.reshape(PATCH_SHARD_LEVEL, 2, SHARD_HEIGHT, 2, SWEEP_WIDTH)
        .transpose(0, 2, 3, 1, 4)
        .reshape(TILE_ROWS, 2, TILE_COLS)
    )
    pair_width = pair_count - 1
    own_refs = partners_of(lax.axis_index("pair"), pair_width)
    piece = lax.all_gather(ground_tile[None], "pair", axis=0, tiled=True)
    looked_piece = multilook(piece, ground_tile[None])
    indices = jnp.arange(piece.shape[0], dtype=jnp.int32)
    selection = (own_refs[:, None] == indices[None, :]).astype(jnp.float32)
    looked = jnp.einsum("kn,nabc->kabc", selection, looked_piece, precision=lax.Precision.HIGHEST)
    return goldstein(looked)[None, :, None]


CAP_VMEM = 58 * 1024 * 1024
MESH = pl.DeviceIdType.MESH
EXACT = lax.Precision.HIGHEST
COLS = 16
LANES = 128


def fused_kernel(
    sweep_hbm, opening_hbm, goal_hbm, place_hbm, part_hbm, widen_hbm, row_dft_hbm, left_hbm, back_hbm,
    out,
    sweep, ints, part, widen, row_dft, left, back_mat, outgoing, arrived, meta_out, meta, tops, rows, gathered,
    chosen, scale, sums, looked_out, looked_in,
    load_sem, part_sem, send_sem, recv_sem, meta_send, meta_recv, top_sem, look_send, look_recv, gate,
):
    me = lax.axis_index("ground")
    mine = lax.axis_index("pair")
    tile_count = meta.shape[0]
    piece_count = ints.shape[2]
    device_count = 2 * tile_count
    level_count = tile_count // 4
    level = me // 4
    spot = lax.rem(me, 4)
    self_id = me * 2 + mine
    barrier = pltpu.get_barrier_semaphore()

    loads = [
        pltpu.make_async_copy(source, sink, load_sem.at[at])
        for at, (source, sink) in enumerate(
            [
                (sweep_hbm, sweep),
                (opening_hbm, ints.at[0]),
                (goal_hbm, ints.at[1]),
                (place_hbm, ints.at[2]),
                (widen_hbm, widen),
                (row_dft_hbm, row_dft),
                (left_hbm, left),
                (back_hbm, back_mat),
            ]
        )
    ]

    def spot_of(step):
        return lax.rem(spot // 2 + step // 2, 2) * 2 + lax.rem(spot + step, 2)

    parts = [
        pltpu.make_async_copy(part_hbm.at[spot_of(step)], part.at[step], part_sem.at[step]) for step in range(4)
    ]
    for copy in [loads[0], parts[0]] + loads[1:4] + parts[1:] + loads[4:]:
        copy.start()

    above = device_count - 8 * level

    def greet(step, carry):
        number = 8 * level + lax.rem(self_id - 8 * level + step, above)
        pl.semaphore_signal(
            barrier, inc=1, device_id={"ground": number // 2, "pair": lax.rem(number, 2)}, device_id_type=MESH
        )
        return carry

    lax.fori_loop(1, above, greet, 0)

    def block(step, plane, other):
        return pltpu.make_async_remote_copy(
            src_ref=outgoing.at[(step * 2 + other) * level_count + plane],
            dst_ref=arrived.at[me, mine],
            send_sem=send_sem,
            recv_sem=recv_sem.at[me],
            device_id={"ground": plane * 4 + spot_of(step), "pair": other},
            device_id_type=MESH,
        )

    def label(target):
        return pltpu.make_async_remote_copy(
            src_ref=meta_out,
            dst_ref=meta.at[me],
            send_sem=meta_send,
            recv_sem=meta_recv,
            device_id={"ground": target, "pair": mine},
            device_id_type=MESH,
        )

    def labels(plane):
        for step in range(4):
            label(plane * 4 + spot_of(step)).start()

    for copy in loads[1:4]:
        copy.wait()
    meta_out[...] = jnp.concatenate([ints[0] * 2, ints[1] * SLOTS + ints[2]], axis=1)
    meta[me] = meta_out[...]
    loads[0].wait()

    for step in range(4):
        parts[step].wait()
        for at in range(level_count):
            wide = jnp.concatenate(
                [
                    sweep[row * 64:(row + 1) * 64, :, at * LANES:(at + 1) * LANES].reshape(LANES, LANES)
                    for row in range(8)
                ],
                axis=1,
            )
            moved = jnp.dot(wide, part[step], preferred_element_type=jnp.float32).astype(jnp.bfloat16)
            outgoing[step * 2 * level_count + at] = moved[:, :LANES]
            outgoing[(step * 2 + 1) * level_count + at] = moved[:, LANES:]
        if step == 0:
            pl.semaphore_wait(barrier, 8 * level + 7)

            def admit(number, carry):
                pl.semaphore_signal(
                    gate.at[level], inc=1, device_id={"ground": number // 2, "pair": lax.rem(number, 2)},
                    device_id_type=MESH,
                )
                return carry

            lax.fori_loop(0, 8 * level, admit, 0)
        for plane in range(level_count - 1):

            @pl.when(plane < level)
            def _():
                if step == 0:
                    labels(plane)
                for other in range(2):
                    block(step, plane, other).start()

        if step == 0:
            for turn in range(1, 4):
                label(level * 4 + spot_of(turn)).start()
            block(step, level, 1 - mine).start()
            arrived[me, mine] = outgoing[mine * level_count + level]
        else:
            for other in range(2):
                block(step, level, other).start()
        if step >= 1:
            for plane in range(1, level_count):

                @pl.when(plane == level + 1)
                def _():
                    if step == 1:
                        pl.semaphore_wait(gate.at[plane], 8)
                        labels(plane)
                        for other in range(2):
                            block(0, plane, other).start()
                    for other in range(2):
                        block(step, plane, other).start()

    for plane in range(2, level_count):

        @pl.when(plane > level + 1)
        def _():
            pl.semaphore_wait(gate.at[plane], 8)
            labels(plane)
            for turn in range(4):
                for other in range(2):
                    block(turn, plane, other).start()

    pltpu.make_async_remote_copy(
        src_ref=meta.at[pl.ds(0, tile_count - 1)],
        dst_ref=meta.at[pl.ds(0, tile_count - 1)],
        send_sem=meta_send,
        recv_sem=meta_recv,
        device_id={"ground": me, "pair": 1 - mine},
        device_id_type=MESH,
    ).wait()
    to_scalars = pltpu.make_async_copy(meta, tops, top_sem)
    to_scalars.start()
    for copy in loads[4:]:
        copy.wait()

    near = level + 1 - 2 * lax.rem(level, 2)
    cross = 2 - 2 * (level // 2)
    order = [(level, step) for step in range(4)] + [(near, step) for step in range(4)]
    order += [(cross + side, step) for step in range(4) for side in range(2)]
    sources = [plane * 4 + spot_of(step) for plane, step in order]

    lane1 = lax.broadcasted_iota(jnp.int32, (1, LANES), 1)
    width = tile_count * piece_count
    for at in range(tile_count // 2):
        keys = jnp.where(lane1 < 64, pltpu.roll(meta[sources[2 * at]], 64, 1), meta[sources[2 * at + 1]])
        slots = lax.broadcasted_iota(jnp.int32, (tile_count * SLOTS, LANES), 0)
        chosen[:, at * LANES:(at + 1) * LANES] = jnp.where(slots == keys, 1.0, 0.0).astype(jnp.bfloat16)
    count = jnp.dot(chosen[...], jnp.ones((width, LANES), jnp.bfloat16), preferred_element_type=jnp.float32)
    scale[...] = 1.0 / jnp.maximum(count, 1.0)
    to_scalars.wait()

    lane8 = lax.broadcasted_iota(jnp.int32, (8, LANES), 1)
    early = 12 * piece_count

    def columns(pair_row, first, last):
        return jnp.concatenate(
            [gathered[(2 * pair_row + part) * width + first:(2 * pair_row + part) * width + last] for part in range(2)],
            axis=1,
        ).astype(jnp.bfloat16)

    for position, source in enumerate(sources):
        if position == 0:
            pltpu.make_async_remote_copy(
                src_ref=outgoing.at[0],
                dst_ref=arrived.at[me, 1 - mine],
                send_sem=send_sem,
                recv_sem=recv_sem.at[me],
                device_id={"ground": me, "pair": 1 - mine},
                device_id_type=MESH,
            ).wait_recv()
        else:
            pltpu.make_async_remote_copy(
                src_ref=arrived.at[source],
                dst_ref=arrived.at[source],
                send_sem=send_sem,
                recv_sem=recv_sem.at[source],
                device_id={"ground": source, "pair": mine},
                device_id_type=MESH,
            ).wait_recv()
        both = jnp.concatenate([arrived[source, 0], arrived[source, 1]], axis=1)
        for quarter in range(4):
            spread = jnp.dot(both, widen[quarter], preferred_element_type=jnp.float32)
            rows[quarter * 256:quarter * 256 + LANES] = spread[:, :LANES]
            rows[quarter * 256 + LANES:quarter * 256 + 256] = spread[:, LANES:]

        def take(group, carry):
            for inner in range(8):
                piece = group * 8 + inner
                top = tops[source, 0, piece]
                value = rows[pl.ds(top, 8), :]
                for shift in range(1, 4):
                    value = jnp.where(lane8 < shift * 32, value, rows[pl.ds(top + 8 * shift, 8), :])
                gathered[pl.ds(position * piece_count + piece, 8, stride=width), :] = value
            return carry

        lax.fori_loop(0, piece_count // 8, take, 0)
        if position == 11:
            for pair_row in range(4):
                sums[pair_row] = jnp.dot(
                    chosen[:, :early], columns(pair_row, 0, early), preferred_element_type=jnp.float32
                )

    same = jnp.zeros((tile_count * SLOTS, LANES), jnp.float32)
    crossed = same
    for pair_row in range(4):
        total = sums[pair_row] + jnp.dot(
            chosen[:, early:], columns(pair_row, early, width), preferred_element_type=jnp.float32
        )
        real = (total[:, :LANES] * scale[...]).astype(jnp.bfloat16).astype(jnp.float32)
        imag = (total[:, LANES:] * scale[...]).astype(jnp.bfloat16).astype(jnp.float32)
        real_other = pltpu.roll(real, LANES - COLS, 1)
        imag_other = pltpu.roll(imag, LANES - COLS, 1)
        same = same + real * real_other + imag * imag_other
        crossed = crossed + imag_other * real - real_other * imag
    lane = lax.broadcasted_iota(jnp.int32, same.shape, 1)
    merged = jnp.where(lane % 32 < COLS, same, pltpu.roll(crossed, COLS, 1))
    high = merged.astype(jnp.bfloat16)
    low = (merged - high.astype(jnp.float32)).astype(jnp.bfloat16)
    row8 = lax.broadcasted_iota(jnp.int32, (8, LANES), 0)
    pool = jnp.where(lane8 // COLS == (row8 % 4) * 2 + row8 // 4, 1.0 / (LOOK_ROWS * LOOK_COLS), 0.0)
    pool = pool.astype(jnp.bfloat16)
    pooled = lax.dot_general(
        jnp.concatenate([pool, pool], axis=1),
        jnp.concatenate([high, low], axis=1),
        (((1,), (1,)), ((), ())),
        preferred_element_type=jnp.float32,
    )
    for group in range(tile_count // 4):
        piece = pooled[:, group * LANES:(group + 1) * LANES]
        turned = piece
        for shift in range(1, 4):
            moved = pltpu.roll(pltpu.roll(piece, LANES - 32 * shift, 1), 2 * shift, 0)
            turned = jnp.where((row8 // 2 - lane8 // 32 + 4) % 4 == shift, moved, turned)
        for inner in range(4):
            looked_out[group * 4 + inner] = turned[2 * inner:2 * inner + 2]

    for step in range(1, device_count):
        target = lax.rem(me + step // 2, tile_count)
        pltpu.make_async_remote_copy(
            src_ref=looked_out.at[target],
            dst_ref=looked_in.at[self_id],
            send_sem=look_send,
            recv_sem=look_recv,
            device_id={"ground": target, "pair": lax.rem(mine + step, 2)},
            device_id_type=MESH,
        ).start()
    looked_in[self_id] = looked_out[me]
    pltpu.make_async_remote_copy(
        src_ref=outgoing.at[pl.ds(0, device_count - 1)],
        dst_ref=outgoing.at[pl.ds(0, device_count - 1)],
        send_sem=send_sem,
        recv_sem=recv_sem.at[0],
        device_id={"ground": me, "pair": 1 - mine},
        device_id_type=MESH,
    ).wait_send()
    pltpu.make_async_remote_copy(
        src_ref=looked_in.at[pl.ds(0, device_count - 1)],
        dst_ref=looked_in.at[pl.ds(0, device_count - 1)],
        send_sem=look_send,
        recv_sem=look_recv,
        device_id={"ground": me, "pair": 1 - mine},
        device_id_type=MESH,
    ).wait()

    def dot(a, b):
        return jnp.dot(a, b, precision=EXACT, preferred_element_type=jnp.float32)

    flip = 1.0 - 2.0 * mine.astype(jnp.float32)
    lanes = lax.broadcasted_iota(jnp.int32, (device_count, LANES), 1)
    sign = jnp.where(lanes < 64, 1.0, flip)
    field = jnp.concatenate([looked_in[:, 0, :] * sign, looked_in[:, 1, :] * sign], axis=1)
    field = dot(field, row_dft[...])
    field = jnp.concatenate([field[:, :LANES], field[:, LANES:]], axis=0)
    length = left.shape[1]
    turn = jnp.where(lax.broadcasted_iota(jnp.int32, (length, 2 * length), 1) < length, 1.0, -1.0)
    both = dot(left[...], field)
    spectrum = both[:length] + turn * pltpu.roll(both[length:], length, 1)
    power = spectrum * spectrum
    power = power + pltpu.roll(power, length, 1)
    weight = jnp.sqrt(jnp.sqrt(power + 1e-06))
    mean = jnp.sum(weight) * (1.0 / (2 * length * length))
    spectrum = spectrum * (weight / mean)
    both = dot(left[...], spectrum)
    back = both[:length] - turn * pltpu.roll(both[length:], length, 1)
    result = lax.dot_general(
        back_mat[...], back, (((1,), (1,)), ((), ())), precision=EXACT, preferred_element_type=jnp.float32
    ) * (1.0 / (length * length))
    out[0] = result[:length]
    out[1] = result[length:]


def constants():
    row = np.arange(1024)
    col = np.arange(256)
    lane, group = row % 128, row // 128
    part = np.stack(
        [
            (lane[:, None] // 32 == spot)
            & (col[None, :] // 128 == lane[:, None] // 16 % 2)
            & (col[None, :] % 128 // 16 == group[:, None])
            & (col[None, :] % 16 == lane[:, None] % 16)
            for spot in range(4)
        ]
    ).astype(jnp.bfloat16)
    row = np.arange(256)
    widen = np.stack(
        [
            (row[:, None] // 128 == col[None, :] // 16 % 2)
            & (row[:, None] % 128 // 16 == 2 * quarter + col[None, :] // 128)
            & (row[:, None] % 16 == col[None, :] % 16)
            for quarter in range(4)
        ]
    ).astype(jnp.bfloat16)
    low, high, slot = row // 128, row % 128 // 32, row % 32
    kind, box = (2 * high + low) // 4, (2 * high + low) % 4
    line = slot // 2 * 4 + box
    out_side, out_kind, frequency = col // 128, col // 64 % 2, col % 64
    angle = (line[:, None] * frequency[None, :] % 64) * (2.0 * math.pi / 64)
    mixed = np.where(
        kind[:, None] == out_kind[None, :],
        np.cos(angle),
        np.where(kind[:, None] == 0, -np.sin(angle), np.sin(angle)),
    )
    row_dft = np.where(slot[:, None] % 2 == out_side[None, :], mixed, 0.0)
    column = np.arange(64)
    angle = (column[:, None] * column[None, :] % 64) * (2.0 * math.pi / 64)
    cosine, sine = np.cos(angle), np.sin(angle)
    left = np.concatenate([cosine, sine], 0)
    back = np.block([[cosine, -sine], [sine, cosine]])
    return (part, widen) + tuple(x.astype(np.float32) for x in (row_dft, left, back))


def local_pair(coregistered_sweeps, shard_opening_height, shard_goal_patch, shard_patch_place):
    tile_count = lax.axis_size("ground")
    level_count = tile_count // 4
    tables = constants()
    vmem = pl.BlockSpec(memory_space=pltpu.VMEM)
    anyplace = pl.BlockSpec(memory_space=pltpu.HBM)
    dma = pltpu.SemaphoreType.DMA
    filtered = pl.pallas_call(
        fused_kernel,
        out_shape=jax.ShapeDtypeStruct((2, 64, 64), jnp.float32),
        in_specs=[anyplace] * 9,
        out_specs=vmem,
        scratch_shapes=[
            pltpu.VMEM((512, 2, 512), jnp.bfloat16),
            pltpu.VMEM((3, 1, 64), jnp.int32),
            pltpu.VMEM((4, 1024, 256), jnp.bfloat16),
            pltpu.VMEM((4, 256, 256), jnp.bfloat16),
            pltpu.VMEM((256, 256), jnp.float32),
            pltpu.VMEM((128, 64), jnp.float32),
            pltpu.VMEM((128, 128), jnp.float32),
            pltpu.VMEM((2 * tile_count, 128, 128), jnp.bfloat16),
            pltpu.VMEM((tile_count, 2, 128, 128), jnp.bfloat16),
            pltpu.VMEM((1, 128), jnp.int32),
            pltpu.VMEM((tile_count, 1, 128), jnp.int32),
            pltpu.SMEM((tile_count, 1, 128), jnp.int32),
            pltpu.VMEM((1024, 128), jnp.float32),
            pltpu.VMEM((8 * tile_count * 64, 128), jnp.float32),
            pltpu.VMEM((tile_count * SLOTS, tile_count * 64), jnp.bfloat16),
            pltpu.VMEM((tile_count * SLOTS, 128), jnp.float32),
            pltpu.VMEM((4, tile_count * SLOTS, 256), jnp.float32),
            pltpu.VMEM((tile_count, 2, 128), jnp.float32),
            pltpu.VMEM((2 * tile_count, 2, 128), jnp.float32),
            dma((8,)),
            dma((4,)),
            dma,
            dma((tile_count,)),
            dma,
            dma,
            dma,
            dma,
            dma,
            pltpu.SemaphoreType.REGULAR((level_count,)),
        ],
        compiler_params=pltpu.CompilerParams(
            collective_id=0, has_side_effects=True, vmem_limit_bytes=CAP_VMEM
        ),
    )(
        coregistered_sweeps[0, 0],
        shard_opening_height.reshape(1, -1),
        shard_goal_patch.reshape(1, -1),
        shard_patch_place.reshape(1, -1),
        *tables,
    )
    return filtered[None, None, None]


def solution(mesh):
    placed = (P("pair", "ground", None, None, None), P("ground"), P("ground", None), P("ground"))
    return jax.shard_map(
        local_pair if dict(mesh.shape) == {"ground": 16, "pair": 2} else local,
        mesh=mesh,
        in_specs=placed,
        out_specs=P("pair", None, "ground", None, None, None),
        check_vma=False,
    )
```

```python
import functools
import math

import jax
import jax.numpy as jnp
import numpy as np
from jax import lax
from jax.experimental import pallas as pl
from jax.experimental.pallas import tpu as pltpu
from jax.sharding import PartitionSpec as P

LOOK_ROWS = 4
LOOK_COLS = 16
SHARD_HEIGHT = 16
TILE_ROWS = 256
TILE_COLS = 1024
SWEEP_WIDTH = 512
PATCH_SHARD_LEVEL = 16
SLOTS = 32


def multilook(reference_tiles, secondary_tiles):
    first = reference_tiles.astype(jnp.float32)
    second = secondary_tiles.astype(jnp.float32)
    real_part = first[..., 0, :] * second[..., 0, :] + first[..., 1, :] * second[..., 1, :]
    imag_part = first[..., 1, :] * second[..., 0, :] - first[..., 0, :] * second[..., 1, :]
    joined = jnp.stack([real_part, imag_part], axis=-3)
    leading = joined.shape[:-2]
    row_count = joined.shape[-2]
    col_count = joined.shape[-1]
    boxes = joined.reshape(
        leading + (row_count // LOOK_ROWS, LOOK_ROWS, col_count // LOOK_COLS, LOOK_COLS)
    )
    return jnp.mean(boxes, axis=(-3, -1))


def on_left(matrix, field):
    return jnp.einsum("ij,...jk->...ik", matrix, field, precision=lax.Precision.HIGHEST)


def on_right(field, matrix):
    return jnp.einsum("...ij,jk->...ik", field, matrix, precision=lax.Precision.HIGHEST)


def goldstein(looked):
    length = looked.shape[-1]
    positions = jnp.arange(length, dtype=jnp.int32)
    phase = positions[:, None] * positions[None, :] % length
    angle = phase.astype(jnp.float32) * (2.0 * math.pi / length)
    cosine = jnp.cos(angle)
    sine = jnp.sin(angle)
    real_in = looked[..., 0, :, :]
    imag_in = looked[..., 1, :, :]
    half_real = on_left(cosine, real_in) + on_left(sine, imag_in)
    half_imag = on_left(cosine, imag_in) - on_left(sine, real_in)
    spec_real = on_right(half_real, cosine) + on_right(half_imag, sine)
    spec_imag = on_right(half_imag, cosine) - on_right(half_real, sine)
    weight = (spec_real * spec_real + spec_imag * spec_imag + 1e-06) ** 0.25
    weight = weight / jnp.mean(weight, axis=(-2, -1), keepdims=True)
    spec_real = spec_real * weight
    spec_imag = spec_imag * weight
    back_real = on_left(cosine, spec_real) - on_left(sine, spec_imag)
    back_imag = on_left(cosine, spec_imag) + on_left(sine, spec_real)
    out_real = on_right(back_real, cosine) - on_right(back_imag, sine)
    out_imag = on_right(back_imag, cosine) + on_right(back_real, sine)
    scale = 1.0 / (length * length)
    return jnp.stack([out_real * scale, out_imag * scale], axis=-3)


def partners_of(index, pair_width):
    order = jnp.arange(pair_width, dtype=jnp.int32)
    return order + (order >= index).astype(jnp.int32)


def local(coregistered_sweeps, shard_opening_height, shard_goal_patch, shard_patch_place):
    earth_patch_total_size = lax.axis_size("ground")
    pair_count = lax.axis_size("pair")
    piece_count = shard_opening_height.shape[0]
    place_allowance = max(
        2, (2 * piece_count + earth_patch_total_size - 1) // earth_patch_total_size
    )
    sweep_resident = coregistered_sweeps[0, 0]
    target = shard_goal_patch[:, 0]
    hits = (target[:, None] == jnp.arange(earth_patch_total_size, dtype=jnp.int32)[None, :]).astype(
        jnp.int32
    )
    order = jnp.arange(piece_count, dtype=jnp.int32)
    before = (order[None, :] < order[:, None]).astype(jnp.bfloat16)
    earlier = jnp.dot(before, hits.astype(jnp.bfloat16), preferred_element_type=jnp.float32).astype(jnp.int32)
    rank = jnp.sum(earlier * hits, axis=1)
    position = target * place_allowance + rank
    matches = (
        position[None, :]
        == jnp.arange(earth_patch_total_size * place_allowance, dtype=jnp.int32)[:, None]
    ).astype(jnp.int32)
    tiles_filled = jnp.sum(matches, axis=1) > 0
    sweep_height_offset = (
        jnp.sum(matches * shard_opening_height[None, :], axis=1)[:, None] + jnp.arange(SHARD_HEIGHT, dtype=jnp.int32)[None, :]
    )
    wanted = jnp.where(tiles_filled[:, None], sweep_height_offset, -1).reshape(-1)
    picked = wanted[:, None] == jnp.arange(sweep_resident.shape[0], dtype=jnp.int32)[None, :]
    pieces_to_send = jnp.dot(
        picked.astype(jnp.bfloat16),
        sweep_resident.reshape(sweep_resident.shape[0], -1),
        preferred_element_type=jnp.float32,
    ).astype(jnp.bfloat16)
    labels = jnp.sum(matches * (shard_patch_place + 1)[None, :], axis=1).astype(jnp.bfloat16)
    received_pieces, arrived_labels = (
        lax.all_to_all(
            pieces_to_send.reshape(
                earth_patch_total_size, place_allowance, SHARD_HEIGHT, 2, SWEEP_WIDTH
            ),
            "ground",
            split_axis=0,
            concat_axis=0,
            tiled=True,
        ),
        lax.all_to_all(
            labels.reshape(earth_patch_total_size, place_allowance),
            "ground",
            split_axis=0,
            concat_axis=0,
            tiled=True,
        ),
    )
    pieces_flattened = received_pieces.reshape(
        earth_patch_total_size * place_allowance, SHARD_HEIGHT * 2 * SWEEP_WIDTH
    )
    slot_labels = (jnp.arange(SLOTS, dtype=jnp.int32) + 1).astype(jnp.bfloat16)
    selector = arrived_labels.reshape(-1)[None, :] == slot_labels[:, None]
    totals = jnp.dot(
        selector.astype(jnp.bfloat16), pieces_flattened, preferred_element_type=jnp.float32
    )
    counts = jnp.sum(selector.astype(jnp.float32), axis=1)
    smoothed_pixel_mean = (totals / jnp.maximum(counts, 1.0)[:, None]).astype(jnp.bfloat16)
    ground_tile = (
        smoothed_pixel_mean.reshape(PATCH_SHARD_LEVEL, 2, SHARD_HEIGHT, 2, SWEEP_WIDTH)
        .transpose(0, 2, 3, 1, 4)
        .reshape(TILE_ROWS, 2, TILE_COLS)
    )
    pair_width = pair_count - 1
    own_refs = partners_of(lax.axis_index("pair"), pair_width)
    piece = lax.all_gather(ground_tile[None], "pair", axis=0, tiled=True)
    looked_piece = multilook(piece, ground_tile[None])
    indices = jnp.arange(piece.shape[0], dtype=jnp.int32)
    selection = (own_refs[:, None] == indices[None, :]).astype(jnp.float32)
    looked = jnp.einsum("kn,nabc->kabc", selection, looked_piece, precision=lax.Precision.HIGHEST)
    return goldstein(looked)[None, :, None]


CAP_VMEM = 58 * 1024 * 1024
MESH = pl.DeviceIdType.MESH
EXACT = lax.Precision.HIGHEST
COLS = 16
LANES = 128


def fused_kernel(
    sweep_hbm, opening_hbm, goal_hbm, place_hbm, part_hbm, widen_hbm, row_dft_hbm, left_hbm, back_hbm,
    out,
    sweep, ints, part, widen, row_dft, left, back_mat, outgoing, arrived, meta_out, meta, tops, rows, gathered,
    chosen, scale, sums, looked_out, looked_in,
    load_sem, part_sem, send_sem, recv_sem, meta_send, meta_recv, top_sem, look_send, look_recv, gate,
):
    me = lax.axis_index("ground")
    mine = lax.axis_index("pair")
    tile_count = meta.shape[0]
    piece_count = ints.shape[2]
    device_count = 2 * tile_count
    level_count = tile_count // 4
    level = me // 4
    spot = lax.rem(me, 4)
    self_id = me * 2 + mine
    barrier = pltpu.get_barrier_semaphore()

    loads = [
        pltpu.make_async_copy(source, sink, load_sem.at[at])
        for at, (source, sink) in enumerate(
            [
                (sweep_hbm, sweep),
                (opening_hbm, ints.at[0]),
                (goal_hbm, ints.at[1]),
                (place_hbm, ints.at[2]),
                (widen_hbm, widen),
                (row_dft_hbm, row_dft),
                (left_hbm, left),
                (back_hbm, back_mat),
            ]
        )
    ]

    def spot_of(step):
        return lax.rem(spot // 2 + step // 2, 2) * 2 + lax.rem(spot + step, 2)

    parts = [
        pltpu.make_async_copy(part_hbm.at[spot_of(step)], part.at[step], part_sem.at[step]) for step in range(4)
    ]
    for copy in [loads[0], parts[0]] + loads[1:4] + parts[1:] + loads[4:]:
        copy.start()

    above = device_count - 8 * level

    def greet(step, carry):
        number = 8 * level + lax.rem(self_id - 8 * level + step, above)
        pl.semaphore_signal(
            barrier, inc=1, device_id={"ground": number // 2, "pair": lax.rem(number, 2)}, device_id_type=MESH
        )
        return carry

    lax.fori_loop(1, above, greet, 0)
    pl.semaphore_wait(barrier, 8 * level + 7)
    for plane in range(level_count - 1):

        @pl.when(plane < level)
        def _():
            pl.semaphore_signal(
                gate.at[level], inc=1, device_id={"ground": plane * 4 + spot, "pair": mine}, device_id_type=MESH
            )

    def block(step, plane, other):
        return pltpu.make_async_remote_copy(
            src_ref=outgoing.at[(step * 2 + other) * level_count + plane],
            dst_ref=arrived.at[me, mine],
            send_sem=send_sem,
            recv_sem=recv_sem.at[me],
            device_id={"ground": plane * 4 + spot_of(step), "pair": other},
            device_id_type=MESH,
        )

    def label(target):
        return pltpu.make_async_remote_copy(
            src_ref=meta_out,
            dst_ref=meta.at[me],
            send_sem=meta_send,
            recv_sem=meta_recv,
            device_id={"ground": target, "pair": mine},
            device_id_type=MESH,
        )

    def labels(plane):
        for step in range(4):
            label(plane * 4 + spot_of(step)).start()

    for copy in loads[1:4]:
        copy.wait()
    meta_out[...] = jnp.concatenate([ints[0] * 2, ints[1] * SLOTS + ints[2]], axis=1)
    meta[me] = meta_out[...]
    loads[0].wait()

    for step in range(4):
        parts[step].wait()
        for at in range(level_count):
            wide = jnp.concatenate(
                [
                    sweep[row * 64:(row + 1) * 64, :, at * LANES:(at + 1) * LANES].reshape(LANES, LANES)
                    for row in range(8)
                ],
                axis=1,
            )
            moved = jnp.dot(wide, part[step], preferred_element_type=jnp.float32).astype(jnp.bfloat16)
            outgoing[step * 2 * level_count + at] = moved[:, :LANES]
            outgoing[(step * 2 + 1) * level_count + at] = moved[:, LANES:]
        for plane in range(level_count - 1):

            @pl.when(plane < level)
            def _():
                if step == 0:
                    labels(plane)
                for other in range(2):
                    block(step, plane, other).start()

        if step == 0:
            for turn in range(1, 4):
                label(level * 4 + spot_of(turn)).start()
            block(step, level, 1 - mine).start()
            arrived[me, mine] = outgoing[mine * level_count + level]
        else:
            for other in range(2):
                block(step, level, other).start()
        for plane in range(1, level_count):

            @pl.when(plane > level)
            def _():
                opening_step = 0 if plane < level_count - 1 else 1
                if step == opening_step:
                    pl.semaphore_wait(gate.at[plane], 1)
                    labels(plane)
                if step >= opening_step:
                    for turn in range(0 if step == opening_step else step, step + 1):
                        for other in range(2):
                            block(turn, plane, other).start()

    pltpu.make_async_remote_copy(
        src_ref=meta.at[pl.ds(0, tile_count - 1)],
        dst_ref=meta.at[pl.ds(0, tile_count - 1)],
        send_sem=meta_send,
        recv_sem=meta_recv,
        device_id={"ground": me, "pair": 1 - mine},
        device_id_type=MESH,
    ).wait()
    to_scalars = pltpu.make_async_copy(meta, tops, top_sem)
    to_scalars.start()
    for copy in loads[4:]:
        copy.wait()

    near = level + 1 - 2 * lax.rem(level, 2)
    cross = 2 - 2 * (level // 2)
    order = [(plane, step) for step in range(4) for plane in (level, near, cross, cross + 1)]
    sources = [plane * 4 + spot_of(step) for plane, step in order]

    lane1 = lax.broadcasted_iota(jnp.int32, (1, LANES), 1)
    width = tile_count * piece_count
    for at in range(tile_count // 2):
        keys = jnp.where(lane1 < 64, pltpu.roll(meta[sources[2 * at]], 64, 1), meta[sources[2 * at + 1]])
        slots = lax.broadcasted_iota(jnp.int32, (tile_count * SLOTS, LANES), 0)
        chosen[:, at * LANES:(at + 1) * LANES] = jnp.where(slots == keys, 1.0, 0.0).astype(jnp.bfloat16)
    count = jnp.dot(chosen[...], jnp.ones((width, LANES), jnp.bfloat16), preferred_element_type=jnp.float32)
    scale[...] = 1.0 / jnp.maximum(count, 1.0)
    to_scalars.wait()

    lane8 = lax.broadcasted_iota(jnp.int32, (8, LANES), 1)
    early = 12 * piece_count

    def columns(pair_row, first, last):
        return jnp.concatenate(
            [gathered[(2 * pair_row + part) * width + first:(2 * pair_row + part) * width + last] for part in range(2)],
            axis=1,
        ).astype(jnp.bfloat16)

    for position, source in enumerate(sources):
        if position == 0:
            pltpu.make_async_remote_copy(
                src_ref=outgoing.at[0],
                dst_ref=arrived.at[me, 1 - mine],
                send_sem=send_sem,
                recv_sem=recv_sem.at[me],
                device_id={"ground": me, "pair": 1 - mine},
                device_id_type=MESH,
            ).wait_recv()
        else:
            pltpu.make_async_remote_copy(
                src_ref=arrived.at[source],
                dst_ref=arrived.at[source],
                send_sem=send_sem,
                recv_sem=recv_sem.at[source],
                device_id={"ground": source, "pair": mine},
                device_id_type=MESH,
            ).wait_recv()
        both = jnp.concatenate([arrived[source, 0], arrived[source, 1]], axis=1)
        for quarter in range(4):
            spread = jnp.dot(both, widen[quarter], preferred_element_type=jnp.float32)
            rows[quarter * 256:quarter * 256 + LANES] = spread[:, :LANES]
            rows[quarter * 256 + LANES:quarter * 256 + 256] = spread[:, LANES:]

        def take(group, carry):
            for inner in range(8):
                piece = group * 8 + inner
                top = tops[source, 0, piece]
                value = rows[pl.ds(top, 8), :]
                for shift in range(1, 4):
                    value = jnp.where(lane8 < shift * 32, value, rows[pl.ds(top + 8 * shift, 8), :])
                gathered[pl.ds(position * piece_count + piece, 8, stride=width), :] = value
            return carry

        lax.fori_loop(0, piece_count // 8, take, 0)
        if position == 11:
            for pair_row in range(4):
                sums[pair_row] = jnp.dot(
                    chosen[:, :early], columns(pair_row, 0, early), preferred_element_type=jnp.float32
                )

    same = jnp.zeros((tile_count * SLOTS, LANES), jnp.float32)
    crossed = same
    for pair_row in range(4):
        total = sums[pair_row] + jnp.dot(
            chosen[:, early:], columns(pair_row, early, width), preferred_element_type=jnp.float32
        )
        real = (total[:, :LANES] * scale[...]).astype(jnp.bfloat16).astype(jnp.float32)
        imag = (total[:, LANES:] * scale[...]).astype(jnp.bfloat16).astype(jnp.float32)
        real_other = pltpu.roll(real, LANES - COLS, 1)
        imag_other = pltpu.roll(imag, LANES - COLS, 1)
        same = same + real * real_other + imag * imag_other
        crossed = crossed + imag_other * real - real_other * imag
    lane = lax.broadcasted_iota(jnp.int32, same.shape, 1)
    merged = jnp.where(lane % 32 < COLS, same, pltpu.roll(crossed, COLS, 1))
    high = merged.astype(jnp.bfloat16)
    low = (merged - high.astype(jnp.float32)).astype(jnp.bfloat16)
    row8 = lax.broadcasted_iota(jnp.int32, (8, LANES), 0)
    pool = jnp.where(lane8 // COLS == (row8 % 4) * 2 + row8 // 4, 1.0 / (LOOK_ROWS * LOOK_COLS), 0.0)
    pool = pool.astype(jnp.bfloat16)
    pooled = lax.dot_general(
        jnp.concatenate([pool, pool], axis=1),
        jnp.concatenate([high, low], axis=1),
        (((1,), (1,)), ((), ())),
        preferred_element_type=jnp.float32,
    )
    for group in range(tile_count // 4):
        piece = pooled[:, group * LANES:(group + 1) * LANES]
        turned = piece
        for shift in range(1, 4):
            moved = pltpu.roll(pltpu.roll(piece, LANES - 32 * shift, 1), 2 * shift, 0)
            turned = jnp.where((row8 // 2 - lane8 // 32 + 4) % 4 == shift, moved, turned)
        for inner in range(4):
            looked_out[group * 4 + inner] = turned[2 * inner:2 * inner + 2]

    for step in range(1, device_count):
        target = lax.rem(me + step // 2, tile_count)
        pltpu.make_async_remote_copy(
            src_ref=looked_out.at[target],
            dst_ref=looked_in.at[self_id],
            send_sem=look_send,
            recv_sem=look_recv,
            device_id={"ground": target, "pair": lax.rem(mine + step, 2)},
            device_id_type=MESH,
        ).start()
    looked_in[self_id] = looked_out[me]
    pltpu.make_async_remote_copy(
        src_ref=outgoing.at[pl.ds(0, device_count - 1)],
        dst_ref=outgoing.at[pl.ds(0, device_count - 1)],
        send_sem=send_sem,
        recv_sem=recv_sem.at[0],
        device_id={"ground": me, "pair": 1 - mine},
        device_id_type=MESH,
    ).wait_send()
    pltpu.make_async_remote_copy(
        src_ref=looked_in.at[pl.ds(0, device_count - 1)],
        dst_ref=looked_in.at[pl.ds(0, device_count - 1)],
        send_sem=look_send,
        recv_sem=look_recv,
        device_id={"ground": me, "pair": 1 - mine},
        device_id_type=MESH,
    ).wait()

    def dot(a, b):
        return jnp.dot(a, b, precision=EXACT, preferred_element_type=jnp.float32)

    flip = 1.0 - 2.0 * mine.astype(jnp.float32)
    lanes = lax.broadcasted_iota(jnp.int32, (device_count, LANES), 1)
    sign = jnp.where(lanes < 64, 1.0, flip)
    field = jnp.concatenate([looked_in[:, 0, :] * sign, looked_in[:, 1, :] * sign], axis=1)
    field = dot(field, row_dft[...])
    field = jnp.concatenate([field[:, :LANES], field[:, LANES:]], axis=0)
    length = left.shape[1]
    turn = jnp.where(lax.broadcasted_iota(jnp.int32, (length, 2 * length), 1) < length, 1.0, -1.0)
    both = dot(left[...], field)
    spectrum = both[:length] + turn * pltpu.roll(both[length:], length, 1)
    power = spectrum * spectrum
    power = power + pltpu.roll(power, length, 1)
    weight = jnp.sqrt(jnp.sqrt(power + 1e-06))
    mean = jnp.sum(weight) * (1.0 / (2 * length * length))
    spectrum = spectrum * (weight / mean)
    both = dot(left[...], spectrum)
    back = both[:length] - turn * pltpu.roll(both[length:], length, 1)
    result = lax.dot_general(
        back_mat[...], back, (((1,), (1,)), ((), ())), precision=EXACT, preferred_element_type=jnp.float32
    ) * (1.0 / (length * length))
    out[0] = result[:length]
    out[1] = result[length:]


def constants():
    row = np.arange(1024)
    col = np.arange(256)
    lane, group = row % 128, row // 128
    part = np.stack(
        [
            (lane[:, None] // 32 == spot)
            & (col[None, :] // 128 == lane[:, None] // 16 % 2)
            & (col[None, :] % 128 // 16 == group[:, None])
            & (col[None, :] % 16 == lane[:, None] % 16)
            for spot in range(4)
        ]
    ).astype(jnp.bfloat16)
    row = np.arange(256)
    widen = np.stack(
        [
            (row[:, None] // 128 == col[None, :] // 16 % 2)
            & (row[:, None] % 128 // 16 == 2 * quarter + col[None, :] // 128)
            & (row[:, None] % 16 == col[None, :] % 16)
            for quarter in range(4)
        ]
    ).astype(jnp.bfloat16)
    low, high, slot = row // 128, row % 128 // 32, row % 32
    kind, box = (2 * high + low) // 4, (2 * high + low) % 4
    line = slot // 2 * 4 + box
    out_side, out_kind, frequency = col // 128, col // 64 % 2, col % 64
    angle = (line[:, None] * frequency[None, :] % 64) * (2.0 * math.pi / 64)
    mixed = np.where(
        kind[:, None] == out_kind[None, :],
        np.cos(angle),
        np.where(kind[:, None] == 0, -np.sin(angle), np.sin(angle)),
    )
    row_dft = np.where(slot[:, None] % 2 == out_side[None, :], mixed, 0.0)
    column = np.arange(64)
    angle = (column[:, None] * column[None, :] % 64) * (2.0 * math.pi / 64)
    cosine, sine = np.cos(angle), np.sin(angle)
    left = np.concatenate([cosine, sine], 0)
    back = np.block([[cosine, -sine], [sine, cosine]])
    return (part, widen) + tuple(x.astype(np.float32) for x in (row_dft, left, back))


def local_pair(coregistered_sweeps, shard_opening_height, shard_goal_patch, shard_patch_place):
    tile_count = lax.axis_size("ground")
    level_count = tile_count // 4
    tables = constants()
    vmem = pl.BlockSpec(memory_space=pltpu.VMEM)
    anyplace = pl.BlockSpec(memory_space=pltpu.HBM)
    dma = pltpu.SemaphoreType.DMA
    filtered = pl.pallas_call(
        fused_kernel,
        out_shape=jax.ShapeDtypeStruct((2, 64, 64), jnp.float32),
        in_specs=[anyplace] * 9,
        out_specs=vmem,
        scratch_shapes=[
            pltpu.VMEM((512, 2, 512), jnp.bfloat16),
            pltpu.VMEM((3, 1, 64), jnp.int32),
            pltpu.VMEM((4, 1024, 256), jnp.bfloat16),
            pltpu.VMEM((4, 256, 256), jnp.bfloat16),
            pltpu.VMEM((256, 256), jnp.float32),
            pltpu.VMEM((128, 64), jnp.float32),
            pltpu.VMEM((128, 128), jnp.float32),
            pltpu.VMEM((2 * tile_count, 128, 128), jnp.bfloat16),
            pltpu.VMEM((tile_count, 2, 128, 128), jnp.bfloat16),
            pltpu.VMEM((1, 128), jnp.int32),
            pltpu.VMEM((tile_count, 1, 128), jnp.int32),
            pltpu.SMEM((tile_count, 1, 128), jnp.int32),
            pltpu.VMEM((1024, 128), jnp.float32),
            pltpu.VMEM((8 * tile_count * 64, 128), jnp.float32),
            pltpu.VMEM((tile_count * SLOTS, tile_count * 64), jnp.bfloat16),
            pltpu.VMEM((tile_count * SLOTS, 128), jnp.float32),
            pltpu.VMEM((4, tile_count * SLOTS, 256), jnp.float32),
            pltpu.VMEM((tile_count, 2, 128), jnp.float32),
            pltpu.VMEM((2 * tile_count, 2, 128), jnp.float32),
            dma((8,)),
            dma((4,)),
            dma,
            dma((tile_count,)),
            dma,
            dma,
            dma,
            dma,
            dma,
            pltpu.SemaphoreType.REGULAR((level_count,)),
        ],
        compiler_params=pltpu.CompilerParams(
            collective_id=0, has_side_effects=True, vmem_limit_bytes=CAP_VMEM
        ),
    )(
        coregistered_sweeps[0, 0],
        shard_opening_height.reshape(1, -1),
        shard_goal_patch.reshape(1, -1),
        shard_patch_place.reshape(1, -1),
        *tables,
    )
    return filtered[None, None, None]


def solution(mesh):
    placed = (P("pair", "ground", None, None, None), P("ground"), P("ground", None), P("ground"))
    return jax.shard_map(
        local_pair if dict(mesh.shape) == {"ground": 16, "pair": 2} else local,
        mesh=mesh,
        in_specs=placed,
        out_specs=P("pair", None, "ground", None, None, None),
        check_vma=False,
    )
```

```python
import functools
import math

import jax
import jax.numpy as jnp
import numpy as np
from jax import lax
from jax.experimental import pallas as pl
from jax.experimental.pallas import tpu as pltpu
from jax.sharding import PartitionSpec as P

LOOK_ROWS = 4
LOOK_COLS = 16
SHARD_HEIGHT = 16
TILE_ROWS = 256
TILE_COLS = 1024
SWEEP_WIDTH = 512
PATCH_SHARD_LEVEL = 16
SLOTS = 32


def multilook(reference_tiles, secondary_tiles):
    first = reference_tiles.astype(jnp.float32)
    second = secondary_tiles.astype(jnp.float32)
    real_part = first[..., 0, :] * second[..., 0, :] + first[..., 1, :] * second[..., 1, :]
    imag_part = first[..., 1, :] * second[..., 0, :] - first[..., 0, :] * second[..., 1, :]
    joined = jnp.stack([real_part, imag_part], axis=-3)
    leading = joined.shape[:-2]
    row_count = joined.shape[-2]
    col_count = joined.shape[-1]
    boxes = joined.reshape(
        leading + (row_count // LOOK_ROWS, LOOK_ROWS, col_count // LOOK_COLS, LOOK_COLS)
    )
    return jnp.mean(boxes, axis=(-3, -1))


def on_left(matrix, field):
    return jnp.einsum("ij,...jk->...ik", matrix, field, precision=lax.Precision.HIGHEST)


def on_right(field, matrix):
    return jnp.einsum("...ij,jk->...ik", field, matrix, precision=lax.Precision.HIGHEST)


def goldstein(looked):
    length = looked.shape[-1]
    positions = jnp.arange(length, dtype=jnp.int32)
    phase = positions[:, None] * positions[None, :] % length
    angle = phase.astype(jnp.float32) * (2.0 * math.pi / length)
    cosine = jnp.cos(angle)
    sine = jnp.sin(angle)
    real_in = looked[..., 0, :, :]
    imag_in = looked[..., 1, :, :]
    half_real = on_left(cosine, real_in) + on_left(sine, imag_in)
    half_imag = on_left(cosine, imag_in) - on_left(sine, real_in)
    spec_real = on_right(half_real, cosine) + on_right(half_imag, sine)
    spec_imag = on_right(half_imag, cosine) - on_right(half_real, sine)
    weight = (spec_real * spec_real + spec_imag * spec_imag + 1e-06) ** 0.25
    weight = weight / jnp.mean(weight, axis=(-2, -1), keepdims=True)
    spec_real = spec_real * weight
    spec_imag = spec_imag * weight
    back_real = on_left(cosine, spec_real) - on_left(sine, spec_imag)
    back_imag = on_left(cosine, spec_imag) + on_left(sine, spec_real)
    out_real = on_right(back_real, cosine) - on_right(back_imag, sine)
    out_imag = on_right(back_imag, cosine) + on_right(back_real, sine)
    scale = 1.0 / (length * length)
    return jnp.stack([out_real * scale, out_imag * scale], axis=-3)


def partners_of(index, pair_width):
    order = jnp.arange(pair_width, dtype=jnp.int32)
    return order + (order >= index).astype(jnp.int32)


def local(coregistered_sweeps, shard_opening_height, shard_goal_patch, shard_patch_place):
    earth_patch_total_size = lax.axis_size("ground")
    pair_count = lax.axis_size("pair")
    piece_count = shard_opening_height.shape[0]
    place_allowance = max(
        2, (2 * piece_count + earth_patch_total_size - 1) // earth_patch_total_size
    )
    sweep_resident = coregistered_sweeps[0, 0]
    target = shard_goal_patch[:, 0]
    hits = (target[:, None] == jnp.arange(earth_patch_total_size, dtype=jnp.int32)[None, :]).astype(
        jnp.int32
    )
    order = jnp.arange(piece_count, dtype=jnp.int32)
    before = (order[None, :] < order[:, None]).astype(jnp.bfloat16)
    earlier = jnp.dot(before, hits.astype(jnp.bfloat16), preferred_element_type=jnp.float32).astype(jnp.int32)
    rank = jnp.sum(earlier * hits, axis=1)
    position = target * place_allowance + rank
    matches = (
        position[None, :]
        == jnp.arange(earth_patch_total_size * place_allowance, dtype=jnp.int32)[:, None]
    ).astype(jnp.int32)
    tiles_filled = jnp.sum(matches, axis=1) > 0
    sweep_height_offset = (
        jnp.sum(matches * shard_opening_height[None, :], axis=1)[:, None] + jnp.arange(SHARD_HEIGHT, dtype=jnp.int32)[None, :]
    )
    wanted = jnp.where(tiles_filled[:, None], sweep_height_offset, -1).reshape(-1)
    picked = wanted[:, None] == jnp.arange(sweep_resident.shape[0], dtype=jnp.int32)[None, :]
    pieces_to_send = jnp.dot(
        picked.astype(jnp.bfloat16),
        sweep_resident.reshape(sweep_resident.shape[0], -1),
        preferred_element_type=jnp.float32,
    ).astype(jnp.bfloat16)
    labels = jnp.sum(matches * (shard_patch_place + 1)[None, :], axis=1).astype(jnp.bfloat16)
    received_pieces, arrived_labels = (
        lax.all_to_all(
            pieces_to_send.reshape(
                earth_patch_total_size, place_allowance, SHARD_HEIGHT, 2, SWEEP_WIDTH
            ),
            "ground",
            split_axis=0,
            concat_axis=0,
            tiled=True,
        ),
        lax.all_to_all(
            labels.reshape(earth_patch_total_size, place_allowance),
            "ground",
            split_axis=0,
            concat_axis=0,
            tiled=True,
        ),
    )
    pieces_flattened = received_pieces.reshape(
        earth_patch_total_size * place_allowance, SHARD_HEIGHT * 2 * SWEEP_WIDTH
    )
    slot_labels = (jnp.arange(SLOTS, dtype=jnp.int32) + 1).astype(jnp.bfloat16)
    selector = arrived_labels.reshape(-1)[None, :] == slot_labels[:, None]
    totals = jnp.dot(
        selector.astype(jnp.bfloat16), pieces_flattened, preferred_element_type=jnp.float32
    )
    counts = jnp.sum(selector.astype(jnp.float32), axis=1)
    smoothed_pixel_mean = (totals / jnp.maximum(counts, 1.0)[:, None]).astype(jnp.bfloat16)
    ground_tile = (
        smoothed_pixel_mean.reshape(PATCH_SHARD_LEVEL, 2, SHARD_HEIGHT, 2, SWEEP_WIDTH)
        .transpose(0, 2, 3, 1, 4)
        .reshape(TILE_ROWS, 2, TILE_COLS)
    )
    pair_width = pair_count - 1
    own_refs = partners_of(lax.axis_index("pair"), pair_width)
    piece = lax.all_gather(ground_tile[None], "pair", axis=0, tiled=True)
    looked_piece = multilook(piece, ground_tile[None])
    indices = jnp.arange(piece.shape[0], dtype=jnp.int32)
    selection = (own_refs[:, None] == indices[None, :]).astype(jnp.float32)
    looked = jnp.einsum("kn,nabc->kabc", selection, looked_piece, precision=lax.Precision.HIGHEST)
    return goldstein(looked)[None, :, None]


CAP_VMEM = 54784 * 1024
MESH = pl.DeviceIdType.MESH
EXACT = lax.Precision.HIGHEST
COLS = 16
LANES = 128


def fused_kernel(
    sweep_hbm, meta_hbm, tables,
    out,
    sweep, part, fixed, outgoing, arrived, meta_out, meta, tops, rows, gathered,
    chosen, scale, sums, looked_out, looked_in, folded,
    load_sem, part_sem, send_sem, recv_sem, meta_send, meta_recv, top_sem, look_send, look_recv, gate,
):
    me = lax.axis_index("ground")
    mine = lax.axis_index("pair")
    tile_count = meta.shape[0]
    piece_count = meta_out.shape[1] // 2
    device_count = 2 * tile_count
    level_count = tile_count // 4
    level = me // 4
    spot = lax.rem(me, 4)
    self_id = me * 2 + mine
    barrier = pltpu.get_barrier_semaphore()

    spread_rows = pl.ds(4 * 1024, fixed.shape[0])
    load_meta = pltpu.make_async_copy(meta_hbm, meta_out, load_sem.at[0])
    load_fixed = pltpu.make_async_copy(tables.at[spread_rows], fixed, load_sem.at[1])

    def spot_of(step):
        return lax.rem(spot // 2 + step // 2, 2) * 2 + lax.rem(spot + step, 2)

    parts = [
        pltpu.make_async_copy(tables.at[pl.ds(spot_of(step) * 1024, 1024)], part.at[step], part_sem.at[step])
        for step in range(4)
    ]
    load_sweep = pltpu.make_async_copy(sweep_hbm, sweep, load_sem.at[2])
    load_meta.start()
    load_sweep.start()
    for copy in parts:
        copy.start()
    load_fixed.start()

    above = device_count - 8 * level

    def greet(step, carry):
        number = 8 * level + lax.rem(self_id - 8 * level + step, above)
        pl.semaphore_signal(
            barrier, inc=1, device_id={"ground": number // 2, "pair": lax.rem(number, 2)}, device_id_type=MESH
        )
        return carry

    lax.fori_loop(1, above, greet, 0)
    pl.semaphore_wait(barrier, 8 * level + 7)
    for plane in range(level_count - 1):

        @pl.when(plane < level)
        def _():
            pl.semaphore_signal(
                gate.at[level], inc=1, device_id={"ground": plane * 4 + spot, "pair": mine}, device_id_type=MESH
            )

    def block(step, plane, other):
        return pltpu.make_async_remote_copy(
            src_ref=outgoing.at[(step * 2 + other) * level_count + plane],
            dst_ref=arrived.at[me, mine],
            send_sem=send_sem,
            recv_sem=recv_sem.at[me],
            device_id={"ground": plane * 4 + spot_of(step), "pair": other},
            device_id_type=MESH,
        )

    def label(target):
        return pltpu.make_async_remote_copy(
            src_ref=meta_out,
            dst_ref=meta.at[me],
            send_sem=meta_send,
            recv_sem=meta_recv,
            device_id={"ground": target, "pair": mine},
            device_id_type=MESH,
        )

    def labels(plane):
        for step in range(4):
            label(plane * 4 + spot_of(step)).start()

    load_meta.wait()
    meta[me] = meta_out[...]
    load_sweep.wait()

    for step in range(4):
        parts[step].wait()
        for at in range(level_count):
            if step == 0:
                for row in range(8):
                    folded[at, :, row * LANES:(row + 1) * LANES] = sweep[
                        row * 64:(row + 1) * 64, :, at * LANES:(at + 1) * LANES
                    ].reshape(LANES, LANES)
            moved = jnp.dot(folded[at], part[step], preferred_element_type=jnp.float32).astype(jnp.bfloat16)
            outgoing[step * 2 * level_count + at] = moved[:, :LANES]
            outgoing[(step * 2 + 1) * level_count + at] = moved[:, LANES:]
        for plane in range(level_count - 1):

            @pl.when(plane < level)
            def _():
                if step == 0:
                    labels(plane)
                for other in range(2):
                    block(step, plane, other).start()

        if step == 0:
            for turn in range(1, 4):
                label(level * 4 + spot_of(turn)).start()
            block(step, level, 1 - mine).start()
            arrived[me, mine] = outgoing[mine * level_count + level]
        else:
            for other in range(2):
                block(step, level, other).start()
        for plane in range(1, level_count):

            @pl.when(plane > level)
            def _():
                opening_step = 0 if plane < level_count - 1 else 1
                if step == opening_step:
                    pl.semaphore_wait(gate.at[plane], 1)
                    labels(plane)
                if step >= opening_step:
                    for turn in range(0 if step == opening_step else step, step + 1):
                        for other in range(2):
                            block(turn, plane, other).start()

    pltpu.make_async_remote_copy(
        src_ref=meta.at[pl.ds(0, tile_count - 1)],
        dst_ref=meta.at[pl.ds(0, tile_count - 1)],
        send_sem=meta_send,
        recv_sem=meta_recv,
        device_id={"ground": me, "pair": 1 - mine},
        device_id_type=MESH,
    ).wait()
    to_scalars = pltpu.make_async_copy(meta, tops, top_sem)
    to_scalars.start()
    load_fixed.wait()

    near = level + 1 - 2 * lax.rem(level, 2)
    cross = 2 - 2 * (level // 2)
    order = [(plane, step) for step in range(4) for plane in (level, near, cross, cross + 1)]
    sources = [plane * 4 + spot_of(step) for plane, step in order]

    lane1 = lax.broadcasted_iota(jnp.int32, (1, LANES), 1)
    width = tile_count * piece_count
    for at in range(tile_count // 2):
        keys = jnp.where(lane1 < 64, pltpu.roll(meta[sources[2 * at]], 64, 1), meta[sources[2 * at + 1]])
        slots = lax.broadcasted_iota(jnp.int32, (tile_count * SLOTS, LANES), 0)
        chosen[:, at * LANES:(at + 1) * LANES] = jnp.where(slots == keys, 1.0, 0.0).astype(jnp.bfloat16)
    count = jnp.dot(chosen[...], jnp.ones((width, LANES), jnp.bfloat16), preferred_element_type=jnp.float32)
    scale[...] = 1.0 / jnp.maximum(count, 1.0)
    to_scalars.wait()

    lane8 = lax.broadcasted_iota(jnp.int32, (8, LANES), 1)
    early = 12 * piece_count

    def columns(pair_row, first, last):
        return jnp.concatenate(
            [gathered[(2 * pair_row + part) * width + first:(2 * pair_row + part) * width + last] for part in range(2)],
            axis=1,
        ).astype(jnp.bfloat16)

    for position, source in enumerate(sources):
        if position == 0:
            pltpu.make_async_remote_copy(
                src_ref=outgoing.at[0],
                dst_ref=arrived.at[me, 1 - mine],
                send_sem=send_sem,
                recv_sem=recv_sem.at[me],
                device_id={"ground": me, "pair": 1 - mine},
                device_id_type=MESH,
            ).wait_recv()
        else:
            pltpu.make_async_remote_copy(
                src_ref=arrived.at[source],
                dst_ref=arrived.at[source],
                send_sem=send_sem,
                recv_sem=recv_sem.at[source],
                device_id={"ground": source, "pair": mine},
                device_id_type=MESH,
            ).wait_recv()
        both = jnp.concatenate([arrived[source, 0], arrived[source, 1]], axis=1)
        for quarter in range(4):
            spread = jnp.dot(both, fixed[quarter * 256:(quarter + 1) * 256], preferred_element_type=jnp.float32)
            rows[quarter * 256:quarter * 256 + LANES] = spread[:, :LANES]
            rows[quarter * 256 + LANES:quarter * 256 + 256] = spread[:, LANES:]

        for piece in range(piece_count):
            top = tops[source, 0, piece]
            value = rows[pl.ds(top, 8), :]
            for shift in range(1, 4):
                value = jnp.where(lane8 < shift * 32, value, rows[pl.ds(top + 8 * shift, 8), :])
            gathered[pl.ds(position * piece_count + piece, 8, stride=width), :] = value
        if position == 11:
            for pair_row in range(4):
                sums[pair_row] = jnp.dot(
                    chosen[:, :early], columns(pair_row, 0, early), preferred_element_type=jnp.float32
                )

    same = jnp.zeros((tile_count * SLOTS, LANES), jnp.float32)
    crossed = same
    for pair_row in range(4):
        total = sums[pair_row] + jnp.dot(
            chosen[:, early:], columns(pair_row, early, width), preferred_element_type=jnp.float32
        )
        real = (total[:, :LANES] * scale[...]).astype(jnp.bfloat16).astype(jnp.float32)
        imag = (total[:, LANES:] * scale[...]).astype(jnp.bfloat16).astype(jnp.float32)
        real_other = pltpu.roll(real, LANES - COLS, 1)
        imag_other = pltpu.roll(imag, LANES - COLS, 1)
        same = same + real * real_other + imag * imag_other
        crossed = crossed + imag_other * real - real_other * imag
    lane = lax.broadcasted_iota(jnp.int32, same.shape, 1)
    merged = jnp.where(lane % 32 < COLS, same, pltpu.roll(crossed, COLS, 1))
    high = merged.astype(jnp.bfloat16)
    low = (merged - high.astype(jnp.float32)).astype(jnp.bfloat16)
    row8 = lax.broadcasted_iota(jnp.int32, (8, LANES), 0)
    pool = jnp.where(lane8 // COLS == (row8 % 4) * 2 + row8 // 4, 1.0 / (LOOK_ROWS * LOOK_COLS), 0.0)
    pool = pool.astype(jnp.bfloat16)
    pooled = lax.dot_general(
        jnp.concatenate([pool, pool], axis=1),
        jnp.concatenate([high, low], axis=1),
        (((1,), (1,)), ((), ())),
        preferred_element_type=jnp.float32,
    )
    for group in range(tile_count // 4):
        piece = pooled[:, group * LANES:(group + 1) * LANES]
        turned = piece
        for shift in range(1, 4):
            moved = pltpu.roll(pltpu.roll(piece, LANES - 32 * shift, 1), 2 * shift, 0)
            turned = jnp.where((row8 // 2 - lane8 // 32 + 4) % 4 == shift, moved, turned)
        for inner in range(4):
            looked_out[group * 4 + inner] = turned[2 * inner:2 * inner + 2]

    for step in range(1, device_count):
        target = lax.rem(me + step // 2, tile_count)
        pltpu.make_async_remote_copy(
            src_ref=looked_out.at[target],
            dst_ref=looked_in.at[self_id],
            send_sem=look_send,
            recv_sem=look_recv,
            device_id={"ground": target, "pair": lax.rem(mine + step, 2)},
            device_id_type=MESH,
        ).start()
    looked_in[self_id] = looked_out[me]
    pltpu.make_async_remote_copy(
        src_ref=outgoing.at[pl.ds(0, device_count - 1)],
        dst_ref=outgoing.at[pl.ds(0, device_count - 1)],
        send_sem=send_sem,
        recv_sem=recv_sem.at[0],
        device_id={"ground": me, "pair": 1 - mine},
        device_id_type=MESH,
    ).wait_send()
    pltpu.make_async_remote_copy(
        src_ref=looked_in.at[pl.ds(0, device_count - 1)],
        dst_ref=looked_in.at[pl.ds(0, device_count - 1)],
        send_sem=look_send,
        recv_sem=look_recv,
        device_id={"ground": me, "pair": 1 - mine},
        device_id_type=MESH,
    ).wait()

    def split(value):
        first = value.astype(jnp.bfloat16)
        return first, (value - first.astype(jnp.float32)).astype(jnp.bfloat16)

    flip = 1.0 - 2.0 * mine.astype(jnp.float32)
    lanes = lax.broadcasted_iota(jnp.int32, (device_count, LANES), 1)
    sign = jnp.where(lanes < 64, 1.0, flip)
    field = jnp.concatenate([looked_in[:, 0, :] * sign, looked_in[:, 1, :] * sign], axis=1)
    first, second = split(field)
    field = jnp.dot(
        jnp.concatenate([first, second, first], axis=1), fixed[1024:1792], preferred_element_type=jnp.float32
    )
    field = jnp.concatenate([field[:, :LANES], field[:, LANES:]], axis=0)
    length = out.shape[1]
    left = fixed[1920:2048, :3 * length]
    turn = jnp.where(lax.broadcasted_iota(jnp.int32, (length, 2 * length), 1) < length, 1.0, -1.0)
    first, second = split(field)
    both = jnp.dot(
        left, jnp.concatenate([first, second, first], axis=0), preferred_element_type=jnp.float32
    )
    spectrum = both[:length] + turn * pltpu.roll(both[length:], length, 1)
    power = spectrum * spectrum
    power = power + pltpu.roll(power, length, 1)
    weight = jnp.sqrt(jnp.sqrt(power + 1e-06))
    mean = jnp.sum(weight) * (1.0 / (2 * length * length))
    spectrum = spectrum * (weight / mean)
    first, second = split(spectrum)
    both = jnp.dot(
        left, jnp.concatenate([first, second, first], axis=0), preferred_element_type=jnp.float32
    )
    back = both[:length] - turn * pltpu.roll(both[length:], length, 1)
    first, second = split(back)
    result = lax.dot_general(
        jnp.concatenate([fixed[1792:1920, :LANES], fixed[1792:1920, :LANES], fixed[1792:1920, LANES:]], axis=1),
        jnp.concatenate([first, second, first], axis=1),
        (((1,), (1,)), ((), ())),
        preferred_element_type=jnp.float32,
    ) * (1.0 / (length * length))
    out[0] = result[:length]
    out[1] = result[length:]


def constants():
    row = np.arange(1024)
    col = np.arange(256)
    lane, group = row % 128, row // 128
    part = np.stack(
        [
            (lane[:, None] // 32 == spot)
            & (col[None, :] // 128 == lane[:, None] // 16 % 2)
            & (col[None, :] % 128 // 16 == group[:, None])
            & (col[None, :] % 16 == lane[:, None] % 16)
            for spot in range(4)
        ]
    ).astype(jnp.bfloat16)
    row = np.arange(256)
    widen = np.stack(
        [
            (row[:, None] // 128 == col[None, :] // 16 % 2)
            & (row[:, None] % 128 // 16 == 2 * quarter + col[None, :] // 128)
            & (row[:, None] % 16 == col[None, :] % 16)
            for quarter in range(4)
        ]
    ).astype(jnp.bfloat16)
    low, high, slot = row // 128, row % 128 // 32, row % 32
    kind, box = (2 * high + low) // 4, (2 * high + low) % 4
    line = slot // 2 * 4 + box
    out_side, out_kind, frequency = col // 128, col // 64 % 2, col % 64
    angle = (line[:, None] * frequency[None, :] % 64) * (2.0 * math.pi / 64)
    mixed = np.where(
        kind[:, None] == out_kind[None, :],
        np.cos(angle),
        np.where(kind[:, None] == 0, -np.sin(angle), np.sin(angle)),
    )
    row_dft = np.where(slot[:, None] % 2 == out_side[None, :], mixed, 0.0)
    column = np.arange(64)
    angle = (column[:, None] * column[None, :] % 64) * (2.0 * math.pi / 64)
    cosine, sine = np.cos(angle), np.sin(angle)
    left = np.concatenate([cosine, sine], 0)
    back = np.block([[cosine, -sine], [sine, cosine]])

    def split(value):
        first = value.astype(np.float32).astype(jnp.bfloat16)
        return first, (value - first.astype(np.float64)).astype(np.float32).astype(jnp.bfloat16)

    row_high, row_low = split(row_dft)
    left_high, left_low = split(left)
    return np.concatenate(
        [
            part.reshape(-1, 256),
            widen.reshape(-1, 256),
            row_high,
            row_high,
            row_low,
            np.concatenate(split(back), 1),
            np.concatenate([left_high, left_high, left_low, np.zeros_like(left_low)], 1),
        ]
    )


def local_pair(coregistered_sweeps, shard_opening_height, shard_goal_patch, shard_patch_place):
    tile_count = lax.axis_size("ground")
    level_count = tile_count // 4
    vmem = pl.BlockSpec(memory_space=pltpu.VMEM)
    anyplace = pl.BlockSpec(memory_space=pltpu.HBM)
    dma = pltpu.SemaphoreType.DMA
    filtered = pl.pallas_call(
        fused_kernel,
        out_shape=jax.ShapeDtypeStruct((2, 64, 64), jnp.float32),
        in_specs=[anyplace] * 3,
        out_specs=vmem,
        scratch_shapes=[
            pltpu.VMEM((512, 2, 512), jnp.bfloat16),
            pltpu.VMEM((4, 1024, 256), jnp.bfloat16),
            pltpu.VMEM((2048, 256), jnp.bfloat16),
            pltpu.VMEM((2 * tile_count, 128, 128), jnp.bfloat16),
            pltpu.VMEM((tile_count, 2, 128, 128), jnp.bfloat16),
            pltpu.VMEM((1, 128), jnp.int32),
            pltpu.VMEM((tile_count, 1, 128), jnp.int32),
            pltpu.SMEM((tile_count, 1, 128), jnp.int32),
            pltpu.VMEM((1024, 128), jnp.float32),
            pltpu.VMEM((8 * tile_count * 64, 128), jnp.float32),
            pltpu.VMEM((tile_count * SLOTS, tile_count * 64), jnp.bfloat16),
            pltpu.VMEM((tile_count * SLOTS, 128), jnp.float32),
            pltpu.VMEM((4, tile_count * SLOTS, 256), jnp.float32),
            pltpu.VMEM((tile_count, 2, 128), jnp.float32),
            pltpu.VMEM((2 * tile_count, 2, 128), jnp.float32),
            pltpu.VMEM((4, 128, 1024), jnp.bfloat16),
            dma((3,)),
            dma((4,)),
            dma,
            dma((tile_count,)),
            dma,
            dma,
            dma,
            dma,
            dma,
            pltpu.SemaphoreType.REGULAR((level_count,)),
        ],
        compiler_params=pltpu.CompilerParams(
            collective_id=0, has_side_effects=True, vmem_limit_bytes=CAP_VMEM
        ),
    )(
        coregistered_sweeps[0, 0],
        jnp.concatenate(
            [shard_opening_height * 2, shard_goal_patch[:, 0] * SLOTS + shard_patch_place]
        ).reshape(1, -1),
        constants(),
    )
    return filtered[None, None, None]


def solution(mesh):
    placed = (P("pair", "ground", None, None, None), P("ground"), P("ground", None), P("ground"))
    return jax.shard_map(
        local_pair if dict(mesh.shape) == {"ground": 16, "pair": 2} else local,
        mesh=mesh,
        in_specs=placed,
        out_specs=P("pair", None, "ground", None, None, None),
        check_vma=False,
    )
```

```python
import functools
import math

import jax
import jax.numpy as jnp
import numpy as np
from jax import lax
from jax.experimental import pallas as pl
from jax.experimental.pallas import tpu as pltpu
from jax.sharding import PartitionSpec as P

LOOK_ROWS = 4
LOOK_COLS = 16
SHARD_HEIGHT = 16
TILE_ROWS = 256
TILE_COLS = 1024
SWEEP_WIDTH = 512
PATCH_SHARD_LEVEL = 16
SLOTS = 32


def multilook(reference_tiles, secondary_tiles):
    first = reference_tiles.astype(jnp.float32)
    second = secondary_tiles.astype(jnp.float32)
    real_part = first[..., 0, :] * second[..., 0, :] + first[..., 1, :] * second[..., 1, :]
    imag_part = first[..., 1, :] * second[..., 0, :] - first[..., 0, :] * second[..., 1, :]
    joined = jnp.stack([real_part, imag_part], axis=-3)
    leading = joined.shape[:-2]
    row_count = joined.shape[-2]
    col_count = joined.shape[-1]
    boxes = joined.reshape(
        leading + (row_count // LOOK_ROWS, LOOK_ROWS, col_count // LOOK_COLS, LOOK_COLS)
    )
    return jnp.mean(boxes, axis=(-3, -1))


def on_left(matrix, field):
    return jnp.einsum("ij,...jk->...ik", matrix, field, precision=lax.Precision.HIGHEST)


def on_right(field, matrix):
    return jnp.einsum("...ij,jk->...ik", field, matrix, precision=lax.Precision.HIGHEST)


def goldstein(looked):
    length = looked.shape[-1]
    positions = jnp.arange(length, dtype=jnp.int32)
    phase = positions[:, None] * positions[None, :] % length
    angle = phase.astype(jnp.float32) * (2.0 * math.pi / length)
    cosine = jnp.cos(angle)
    sine = jnp.sin(angle)
    real_in = looked[..., 0, :, :]
    imag_in = looked[..., 1, :, :]
    half_real = on_left(cosine, real_in) + on_left(sine, imag_in)
    half_imag = on_left(cosine, imag_in) - on_left(sine, real_in)
    spec_real = on_right(half_real, cosine) + on_right(half_imag, sine)
    spec_imag = on_right(half_imag, cosine) - on_right(half_real, sine)
    weight = (spec_real * spec_real + spec_imag * spec_imag + 1e-06) ** 0.25
    weight = weight / jnp.mean(weight, axis=(-2, -1), keepdims=True)
    spec_real = spec_real * weight
    spec_imag = spec_imag * weight
    back_real = on_left(cosine, spec_real) - on_left(sine, spec_imag)
    back_imag = on_left(cosine, spec_imag) + on_left(sine, spec_real)
    out_real = on_right(back_real, cosine) - on_right(back_imag, sine)
    out_imag = on_right(back_imag, cosine) + on_right(back_real, sine)
    scale = 1.0 / (length * length)
    return jnp.stack([out_real * scale, out_imag * scale], axis=-3)


def partners_of(index, pair_width):
    order = jnp.arange(pair_width, dtype=jnp.int32)
    return order + (order >= index).astype(jnp.int32)


def local(coregistered_sweeps, shard_opening_height, shard_goal_patch, shard_patch_place):
    earth_patch_total_size = lax.axis_size("ground")
    pair_count = lax.axis_size("pair")
    piece_count = shard_opening_height.shape[0]
    place_allowance = max(
        2, (2 * piece_count + earth_patch_total_size - 1) // earth_patch_total_size
    )
    sweep_resident = coregistered_sweeps[0, 0]
    target = shard_goal_patch[:, 0]
    hits = (target[:, None] == jnp.arange(earth_patch_total_size, dtype=jnp.int32)[None, :]).astype(
        jnp.int32
    )
    order = jnp.arange(piece_count, dtype=jnp.int32)
    before = (order[None, :] < order[:, None]).astype(jnp.bfloat16)
    earlier = jnp.dot(before, hits.astype(jnp.bfloat16), preferred_element_type=jnp.float32).astype(jnp.int32)
    rank = jnp.sum(earlier * hits, axis=1)
    position = target * place_allowance + rank
    matches = (
        position[None, :]
        == jnp.arange(earth_patch_total_size * place_allowance, dtype=jnp.int32)[:, None]
    ).astype(jnp.int32)
    tiles_filled = jnp.sum(matches, axis=1) > 0
    sweep_height_offset = (
        jnp.sum(matches * shard_opening_height[None, :], axis=1)[:, None] + jnp.arange(SHARD_HEIGHT, dtype=jnp.int32)[None, :]
    )
    wanted = jnp.where(tiles_filled[:, None], sweep_height_offset, -1).reshape(-1)
    picked = wanted[:, None] == jnp.arange(sweep_resident.shape[0], dtype=jnp.int32)[None, :]
    pieces_to_send = jnp.dot(
        picked.astype(jnp.bfloat16),
        sweep_resident.reshape(sweep_resident.shape[0], -1),
        preferred_element_type=jnp.float32,
    ).astype(jnp.bfloat16)
    labels = jnp.sum(matches * (shard_patch_place + 1)[None, :], axis=1).astype(jnp.bfloat16)
    received_pieces, arrived_labels = (
        lax.all_to_all(
            pieces_to_send.reshape(
                earth_patch_total_size, place_allowance, SHARD_HEIGHT, 2, SWEEP_WIDTH
            ),
            "ground",
            split_axis=0,
            concat_axis=0,
            tiled=True,
        ),
        lax.all_to_all(
            labels.reshape(earth_patch_total_size, place_allowance),
            "ground",
            split_axis=0,
            concat_axis=0,
            tiled=True,
        ),
    )
    pieces_flattened = received_pieces.reshape(
        earth_patch_total_size * place_allowance, SHARD_HEIGHT * 2 * SWEEP_WIDTH
    )
    slot_labels = (jnp.arange(SLOTS, dtype=jnp.int32) + 1).astype(jnp.bfloat16)
    selector = arrived_labels.reshape(-1)[None, :] == slot_labels[:, None]
    totals = jnp.dot(
        selector.astype(jnp.bfloat16), pieces_flattened, preferred_element_type=jnp.float32
    )
    counts = jnp.sum(selector.astype(jnp.float32), axis=1)
    smoothed_pixel_mean = (totals / jnp.maximum(counts, 1.0)[:, None]).astype(jnp.bfloat16)
    ground_tile = (
        smoothed_pixel_mean.reshape(PATCH_SHARD_LEVEL, 2, SHARD_HEIGHT, 2, SWEEP_WIDTH)
        .transpose(0, 2, 3, 1, 4)
        .reshape(TILE_ROWS, 2, TILE_COLS)
    )
    pair_width = pair_count - 1
    own_refs = partners_of(lax.axis_index("pair"), pair_width)
    piece = lax.all_gather(ground_tile[None], "pair", axis=0, tiled=True)
    looked_piece = multilook(piece, ground_tile[None])
    indices = jnp.arange(piece.shape[0], dtype=jnp.int32)
    selection = (own_refs[:, None] == indices[None, :]).astype(jnp.float32)
    looked = jnp.einsum("kn,nabc->kabc", selection, looked_piece, precision=lax.Precision.HIGHEST)
    return goldstein(looked)[None, :, None]


CAP_VMEM = 58 * 1024 * 1024
MESH = pl.DeviceIdType.MESH
EXACT = lax.Precision.HIGHEST
COLS = 16
LANES = 128


def fused_kernel(
    sweep_hbm, opening_hbm, goal_hbm, place_hbm, part_hbm, widen_hbm, row_dft_hbm, left_hbm, back_hbm,
    out,
    sweep, ints, part, widen, row_dft, left, back_mat, outgoing, arrived, meta_out, meta, tops, rows, gathered,
    chosen, scale, sums, looked_out, looked_in, folded,
    load_sem, part_sem, send_sem, recv_sem, meta_send, meta_recv, top_sem, look_send, look_recv, gate,
):
    me = lax.axis_index("ground")
    mine = lax.axis_index("pair")
    tile_count = meta.shape[0]
    piece_count = ints.shape[2]
    device_count = 2 * tile_count
    level_count = tile_count // 4
    level = me // 4
    spot = lax.rem(me, 4)
    self_id = me * 2 + mine
    barrier = pltpu.get_barrier_semaphore()

    loads = [
        pltpu.make_async_copy(source, sink, load_sem.at[at])
        for at, (source, sink) in enumerate(
            [
                (sweep_hbm, sweep),
                (opening_hbm, ints.at[0]),
                (goal_hbm, ints.at[1]),
                (place_hbm, ints.at[2]),
                (widen_hbm, widen),
                (row_dft_hbm, row_dft),
                (left_hbm, left),
                (back_hbm, back_mat),
            ]
        )
    ]

    def spot_of(step):
        return lax.rem(spot // 2 + step // 2, 2) * 2 + lax.rem(spot + step, 2)

    parts = [
        pltpu.make_async_copy(part_hbm.at[spot_of(step)], part.at[step], part_sem.at[step]) for step in range(4)
    ]
    for copy in [loads[0], parts[0]] + loads[1:4] + parts[1:] + loads[4:]:
        copy.start()

    above = device_count - 8 * level

    def greet(step, carry):
        number = 8 * level + lax.rem(self_id - 8 * level + step, above)
        pl.semaphore_signal(
            barrier, inc=1, device_id={"ground": number // 2, "pair": lax.rem(number, 2)}, device_id_type=MESH
        )
        return carry

    lax.fori_loop(1, above, greet, 0)
    pl.semaphore_wait(barrier, 8 * level + 7)
    for plane in range(level_count - 1):

        @pl.when(plane < level)
        def _():
            pl.semaphore_signal(
                gate.at[level], inc=1, device_id={"ground": plane * 4 + spot, "pair": mine}, device_id_type=MESH
            )

    def block(step, plane, other):
        return pltpu.make_async_remote_copy(
            src_ref=outgoing.at[(step * 2 + other) * level_count + plane],
            dst_ref=arrived.at[me, mine],
            send_sem=send_sem,
            recv_sem=recv_sem.at[me],
            device_id={"ground": plane * 4 + spot_of(step), "pair": other},
            device_id_type=MESH,
        )

    def label(target):
        return pltpu.make_async_remote_copy(
            src_ref=meta_out,
            dst_ref=meta.at[me],
            send_sem=meta_send,
            recv_sem=meta_recv,
            device_id={"ground": target, "pair": mine},
            device_id_type=MESH,
        )

    def labels(plane):
        for step in range(4):
            label(plane * 4 + spot_of(step)).start()

    for copy in loads[1:4]:
        copy.wait()
    meta_out[...] = jnp.concatenate([ints[0] * 2, ints[1] * SLOTS + ints[2]], axis=1)
    meta[me] = meta_out[...]
    loads[0].wait()

    for step in range(4):
        parts[step].wait()
        for at in range(level_count):
            if step == 0:
                for row in range(8):
                    folded[at, :, row * LANES:(row + 1) * LANES] = sweep[
                        row * 64:(row + 1) * 64, :, at * LANES:(at + 1) * LANES
                    ].reshape(LANES, LANES)
            moved = jnp.dot(folded[at], part[step], preferred_element_type=jnp.float32).astype(jnp.bfloat16)
            outgoing[step * 2 * level_count + at] = moved[:, :LANES]
            outgoing[(step * 2 + 1) * level_count + at] = moved[:, LANES:]
        for plane in range(level_count - 1):

            @pl.when(plane < level)
            def _():
                if step == 0:
                    labels(plane)
                for other in range(2):
                    block(step, plane, other).start()

        if step == 0:
            for turn in range(1, 4):
                label(level * 4 + spot_of(turn)).start()
            block(step, level, 1 - mine).start()
            arrived[me, mine] = outgoing[mine * level_count + level]
        else:
            for other in range(2):
                block(step, level, other).start()
        for plane in range(1, level_count):

            @pl.when(plane > level)
            def _():
                opening_step = 0 if plane < level_count - 1 else 1
                if step == opening_step:
                    pl.semaphore_wait(gate.at[plane], 1)
                    labels(plane)
                if step >= opening_step:
                    for turn in range(0 if step == opening_step else step, step + 1):
                        for other in range(2):
                            block(turn, plane, other).start()

    pltpu.make_async_remote_copy(
        src_ref=meta.at[pl.ds(0, tile_count - 1)],
        dst_ref=meta.at[pl.ds(0, tile_count - 1)],
        send_sem=meta_send,
        recv_sem=meta_recv,
        device_id={"ground": me, "pair": 1 - mine},
        device_id_type=MESH,
    ).wait()
    to_scalars = pltpu.make_async_copy(meta, tops, top_sem)
    to_scalars.start()
    for copy in loads[4:]:
        copy.wait()

    near = level + 1 - 2 * lax.rem(level, 2)
    cross = 2 - 2 * (level // 2)
    order = [(plane, step) for step in range(4) for plane in (level, near, cross, cross + 1)]
    sources = [plane * 4 + spot_of(step) for plane, step in order]

    lane1 = lax.broadcasted_iota(jnp.int32, (1, LANES), 1)
    width = tile_count * piece_count
    for at in range(tile_count // 2):
        keys = jnp.where(lane1 < 64, pltpu.roll(meta[sources[2 * at]], 64, 1), meta[sources[2 * at + 1]])
        slots = lax.broadcasted_iota(jnp.int32, (tile_count * SLOTS, LANES), 0)
        chosen[:, at * LANES:(at + 1) * LANES] = jnp.where(slots == keys, 1.0, 0.0).astype(jnp.bfloat16)
    count = jnp.dot(chosen[...], jnp.ones((width, LANES), jnp.bfloat16), preferred_element_type=jnp.float32)
    scale[...] = 1.0 / jnp.maximum(count, 1.0)
    to_scalars.wait()

    lane8 = lax.broadcasted_iota(jnp.int32, (8, LANES), 1)
    cuts = (8, 12)
    early = cuts[-1] * piece_count

    def columns(pair_row, first, last):
        return jnp.concatenate(
            [gathered[(2 * pair_row + part) * width + first:(2 * pair_row + part) * width + last] for part in range(2)],
            axis=1,
        ).astype(jnp.bfloat16)

    for position, source in enumerate(sources):
        if position == 0:
            pltpu.make_async_remote_copy(
                src_ref=outgoing.at[0],
                dst_ref=arrived.at[me, 1 - mine],
                send_sem=send_sem,
                recv_sem=recv_sem.at[me],
                device_id={"ground": me, "pair": 1 - mine},
                device_id_type=MESH,
            ).wait_recv()
        else:
            pltpu.make_async_remote_copy(
                src_ref=arrived.at[source],
                dst_ref=arrived.at[source],
                send_sem=send_sem,
                recv_sem=recv_sem.at[source],
                device_id={"ground": source, "pair": mine},
                device_id_type=MESH,
            ).wait_recv()
        both = jnp.concatenate([arrived[source, 0], arrived[source, 1]], axis=1)
        for quarter in range(4):
            spread = jnp.dot(both, widen[quarter], preferred_element_type=jnp.float32)
            rows[quarter * 256:quarter * 256 + LANES] = spread[:, :LANES]
            rows[quarter * 256 + LANES:quarter * 256 + 256] = spread[:, LANES:]

        for piece in range(piece_count):
            top = tops[source, 0, piece]
            value = rows[pl.ds(top, 8), :]
            for shift in range(1, 4):
                value = jnp.where(lane8 < shift * 32, value, rows[pl.ds(top + 8 * shift, 8), :])
            gathered[pl.ds(position * piece_count + piece, 8, stride=width), :] = value
        if position + 1 in cuts:
            last = (position + 1) * piece_count
            first = 0 if position + 1 == cuts[0] else cuts[cuts.index(position + 1) - 1] * piece_count
            for pair_row in range(4):
                part_sum = jnp.dot(
                    chosen[:, first:last], columns(pair_row, first, last), preferred_element_type=jnp.float32
                )
                sums[pair_row] = part_sum if first == 0 else sums[pair_row] + part_sum

    same = jnp.zeros((tile_count * SLOTS, LANES), jnp.float32)
    crossed = same
    for pair_row in range(4):
        total = sums[pair_row] + jnp.dot(
            chosen[:, early:], columns(pair_row, early, width), preferred_element_type=jnp.float32
        )
        real = (total[:, :LANES] * scale[...]).astype(jnp.bfloat16).astype(jnp.float32)
        imag = (total[:, LANES:] * scale[...]).astype(jnp.bfloat16).astype(jnp.float32)
        real_other = pltpu.roll(real, LANES - COLS, 1)
        imag_other = pltpu.roll(imag, LANES - COLS, 1)
        same = same + real * real_other + imag * imag_other
        crossed = crossed + imag_other * real - real_other * imag
    lane = lax.broadcasted_iota(jnp.int32, same.shape, 1)
    merged = jnp.where(lane % 32 < COLS, same, pltpu.roll(crossed, COLS, 1))
    high = merged.astype(jnp.bfloat16)
    low = (merged - high.astype(jnp.float32)).astype(jnp.bfloat16)
    row8 = lax.broadcasted_iota(jnp.int32, (8, LANES), 0)
    pool = jnp.where(lane8 // COLS == (row8 % 4) * 2 + row8 // 4, 1.0 / (LOOK_ROWS * LOOK_COLS), 0.0)
    pool = pool.astype(jnp.bfloat16)
    pooled = lax.dot_general(
        jnp.concatenate([pool, pool], axis=1),
        jnp.concatenate([high, low], axis=1),
        (((1,), (1,)), ((), ())),
        preferred_element_type=jnp.float32,
    )
    for group in range(tile_count // 4):
        piece = pooled[:, group * LANES:(group + 1) * LANES]
        turned = piece
        for shift in range(1, 4):
            moved = pltpu.roll(pltpu.roll(piece, LANES - 32 * shift, 1), 2 * shift, 0)
            turned = jnp.where((row8 // 2 - lane8 // 32 + 4) % 4 == shift, moved, turned)
        for inner in range(4):
            looked_out[group * 4 + inner] = turned[2 * inner:2 * inner + 2]

    away = level // 2
    for plane in (3 - 3 * away, 2 - away, near, level):
        for step in (3, 2, 1, 0):
            target = plane * 4 + spot_of(step)
            for other in (1 - mine, mine):
                if plane is level and step == 0 and other is mine:
                    continue
                pltpu.make_async_remote_copy(
                    src_ref=looked_out.at[target],
                    dst_ref=looked_in.at[self_id],
                    send_sem=look_send,
                    recv_sem=look_recv,
                    device_id={"ground": target, "pair": other},
                    device_id_type=MESH,
                ).start()
    looked_in[self_id] = looked_out[me]
    pltpu.make_async_remote_copy(
        src_ref=outgoing.at[pl.ds(0, device_count - 1)],
        dst_ref=outgoing.at[pl.ds(0, device_count - 1)],
        send_sem=send_sem,
        recv_sem=recv_sem.at[0],
        device_id={"ground": me, "pair": 1 - mine},
        device_id_type=MESH,
    ).wait_send()
    pltpu.make_async_remote_copy(
        src_ref=looked_in.at[pl.ds(0, device_count - 1)],
        dst_ref=looked_in.at[pl.ds(0, device_count - 1)],
        send_sem=look_send,
        recv_sem=look_recv,
        device_id={"ground": me, "pair": 1 - mine},
        device_id_type=MESH,
    ).wait()

    def split(value):
        first = value.astype(jnp.bfloat16)
        return first, (value - first.astype(jnp.float32)).astype(jnp.bfloat16)

    flip = 1.0 - 2.0 * mine.astype(jnp.float32)
    lanes = lax.broadcasted_iota(jnp.int32, (device_count, LANES), 1)
    sign = jnp.where(lanes < 64, 1.0, flip)
    field = jnp.concatenate([looked_in[:, 0, :] * sign, looked_in[:, 1, :] * sign], axis=1)
    first, second = split(field)
    field = jnp.dot(
        jnp.concatenate([first, second, first], axis=1), row_dft[...], preferred_element_type=jnp.float32
    )
    field = jnp.concatenate([field[:, :LANES], field[:, LANES:]], axis=0)
    length = out.shape[1]
    turn = jnp.where(lax.broadcasted_iota(jnp.int32, (length, 2 * length), 1) < length, 1.0, -1.0)
    first, second = split(field)
    both = jnp.dot(
        left[...], jnp.concatenate([first, second, first], axis=0), preferred_element_type=jnp.float32
    )
    spectrum = both[:length] + turn * pltpu.roll(both[length:], length, 1)
    power = spectrum * spectrum
    power = power + pltpu.roll(power, length, 1)
    weight = jnp.sqrt(jnp.sqrt(power + 1e-06))
    mean = jnp.sum(weight) * (1.0 / (2 * length * length))
    spectrum = spectrum * (weight / mean)
    first, second = split(spectrum)
    both = jnp.dot(
        left[...], jnp.concatenate([first, second, first], axis=0), preferred_element_type=jnp.float32
    )
    back = both[:length] - turn * pltpu.roll(both[length:], length, 1)
    first, second = split(back)
    result = lax.dot_general(
        back_mat[...],
        jnp.concatenate([first, second, first], axis=1),
        (((1,), (1,)), ((), ())),
        preferred_element_type=jnp.float32,
    ) * (1.0 / (length * length))
    out[0] = result[:length]
    out[1] = result[length:]


def constants():
    row = np.arange(1024)
    col = np.arange(256)
    lane, group = row % 128, row // 128
    part = np.stack(
        [
            (lane[:, None] // 32 == spot)
            & (col[None, :] // 128 == lane[:, None] // 16 % 2)
            & (col[None, :] % 128 // 16 == group[:, None])
            & (col[None, :] % 16 == lane[:, None] % 16)
            for spot in range(4)
        ]
    ).astype(jnp.bfloat16)
    row = np.arange(256)
    widen = np.stack(
        [
            (row[:, None] // 128 == col[None, :] // 16 % 2)
            & (row[:, None] % 128 // 16 == 2 * quarter + col[None, :] // 128)
            & (row[:, None] % 16 == col[None, :] % 16)
            for quarter in range(4)
        ]
    ).astype(jnp.bfloat16)
    low, high, slot = row // 128, row % 128 // 32, row % 32
    kind, box = (2 * high + low) // 4, (2 * high + low) % 4
    line = slot // 2 * 4 + box
    out_side, out_kind, frequency = col // 128, col // 64 % 2, col % 64
    angle = (line[:, None] * frequency[None, :] % 64) * (2.0 * math.pi / 64)
    mixed = np.where(
        kind[:, None] == out_kind[None, :],
        np.cos(angle),
        np.where(kind[:, None] == 0, -np.sin(angle), np.sin(angle)),
    )
    row_dft = np.where(slot[:, None] % 2 == out_side[None, :], mixed, 0.0)
    column = np.arange(64)
    angle = (column[:, None] * column[None, :] % 64) * (2.0 * math.pi / 64)
    cosine, sine = np.cos(angle), np.sin(angle)
    left = np.concatenate([cosine, sine], 0)
    back = np.block([[cosine, -sine], [sine, cosine]])

    def parts_of(value, axis):
        first = value.astype(np.float32).astype(jnp.bfloat16)
        second = (value - first.astype(np.float64)).astype(np.float32).astype(jnp.bfloat16)
        return np.concatenate([first, first, second], axis)

    return part, widen, parts_of(row_dft, 0), parts_of(left, 1), parts_of(back, 1)


def local_pair(coregistered_sweeps, shard_opening_height, shard_goal_patch, shard_patch_place):
    tile_count = lax.axis_size("ground")
    level_count = tile_count // 4
    tables = constants()
    vmem = pl.BlockSpec(memory_space=pltpu.VMEM)
    anyplace = pl.BlockSpec(memory_space=pltpu.HBM)
    dma = pltpu.SemaphoreType.DMA
    filtered = pl.pallas_call(
        fused_kernel,
        out_shape=pltpu.VMEM((2, 64, 64), jnp.float32),
        in_specs=[anyplace] * 9,
        out_specs=vmem,
        scratch_shapes=[
            pltpu.VMEM((512, 2, 512), jnp.bfloat16),
            pltpu.VMEM((3, 1, 64), jnp.int32),
            pltpu.VMEM((4, 1024, 256), jnp.bfloat16),
            pltpu.VMEM((4, 256, 256), jnp.bfloat16),
            pltpu.VMEM((3 * 256, 256), jnp.bfloat16),
            pltpu.VMEM((128, 3 * 64), jnp.bfloat16),
            pltpu.VMEM((128, 3 * 128), jnp.bfloat16),
            pltpu.VMEM((2 * tile_count, 128, 128), jnp.bfloat16),
            pltpu.VMEM((tile_count, 2, 128, 128), jnp.bfloat16),
            pltpu.VMEM((1, 128), jnp.int32),
            pltpu.VMEM((tile_count, 1, 128), jnp.int32),
            pltpu.SMEM((tile_count, 1, 128), jnp.int32),
            pltpu.VMEM((1024, 128), jnp.float32),
            pltpu.VMEM((8 * tile_count * 64, 128), jnp.float32),
            pltpu.VMEM((tile_count * SLOTS, tile_count * 64), jnp.bfloat16),
            pltpu.VMEM((tile_count * SLOTS, 128), jnp.float32),
            pltpu.VMEM((4, tile_count * SLOTS, 256), jnp.float32),
            pltpu.VMEM((tile_count, 2, 128), jnp.float32),
            pltpu.VMEM((2 * tile_count, 2, 128), jnp.float32),
            pltpu.VMEM((4, 128, 1024), jnp.bfloat16),
            dma((8,)),
            dma((4,)),
            dma,
            dma((tile_count,)),
            dma,
            dma,
            dma,
            dma,
            dma,
            pltpu.SemaphoreType.REGULAR((level_count,)),
        ],
        compiler_params=pltpu.CompilerParams(
            collective_id=0, has_side_effects=True, vmem_limit_bytes=CAP_VMEM
        ),
    )(
        coregistered_sweeps[0, 0],
        shard_opening_height.reshape(1, -1),
        shard_goal_patch.reshape(1, -1),
        shard_patch_place.reshape(1, -1),
        *tables,
    )
    return filtered[None, None, None]


def solution(mesh):
    placed = (P("pair", "ground", None, None, None), P("ground"), P("ground", None), P("ground"))
    return jax.shard_map(
        local_pair if dict(mesh.shape) == {"ground": 16, "pair": 2} else local,
        mesh=mesh,
        in_specs=placed,
        out_specs=P("pair", None, "ground", None, None, None),
        check_vma=False,
    )
```

```python
import functools
import math

import jax
import jax.numpy as jnp
import numpy as np
from jax import lax
from jax.experimental import pallas as pl
from jax.experimental.pallas import tpu as pltpu
from jax.sharding import PartitionSpec as P

LOOK_ROWS = 4
LOOK_COLS = 16
SHARD_HEIGHT = 16
TILE_ROWS = 256
TILE_COLS = 1024
SWEEP_WIDTH = 512
PATCH_SHARD_LEVEL = 16
SLOTS = 32


def multilook(reference_tiles, secondary_tiles):
    first = reference_tiles.astype(jnp.float32)
    second = secondary_tiles.astype(jnp.float32)
    real_part = first[..., 0, :] * second[..., 0, :] + first[..., 1, :] * second[..., 1, :]
    imag_part = first[..., 1, :] * second[..., 0, :] - first[..., 0, :] * second[..., 1, :]
    joined = jnp.stack([real_part, imag_part], axis=-3)
    leading = joined.shape[:-2]
    row_count = joined.shape[-2]
    col_count = joined.shape[-1]
    boxes = joined.reshape(
        leading + (row_count // LOOK_ROWS, LOOK_ROWS, col_count // LOOK_COLS, LOOK_COLS)
    )
    return jnp.mean(boxes, axis=(-3, -1))


def on_left(matrix, field):
    return jnp.einsum("ij,...jk->...ik", matrix, field, precision=lax.Precision.HIGHEST)


def on_right(field, matrix):
    return jnp.einsum("...ij,jk->...ik", field, matrix, precision=lax.Precision.HIGHEST)


def goldstein(looked):
    length = looked.shape[-1]
    positions = jnp.arange(length, dtype=jnp.int32)
    phase = positions[:, None] * positions[None, :] % length
    angle = phase.astype(jnp.float32) * (2.0 * math.pi / length)
    cosine = jnp.cos(angle)
    sine = jnp.sin(angle)
    real_in = looked[..., 0, :, :]
    imag_in = looked[..., 1, :, :]
    half_real = on_left(cosine, real_in) + on_left(sine, imag_in)
    half_imag = on_left(cosine, imag_in) - on_left(sine, real_in)
    spec_real = on_right(half_real, cosine) + on_right(half_imag, sine)
    spec_imag = on_right(half_imag, cosine) - on_right(half_real, sine)
    weight = (spec_real * spec_real + spec_imag * spec_imag + 1e-06) ** 0.25
    weight = weight / jnp.mean(weight, axis=(-2, -1), keepdims=True)
    spec_real = spec_real * weight
    spec_imag = spec_imag * weight
    back_real = on_left(cosine, spec_real) - on_left(sine, spec_imag)
    back_imag = on_left(cosine, spec_imag) + on_left(sine, spec_real)
    out_real = on_right(back_real, cosine) - on_right(back_imag, sine)
    out_imag = on_right(back_imag, cosine) + on_right(back_real, sine)
    scale = 1.0 / (length * length)
    return jnp.stack([out_real * scale, out_imag * scale], axis=-3)


def partners_of(index, pair_width):
    order = jnp.arange(pair_width, dtype=jnp.int32)
    return order + (order >= index).astype(jnp.int32)


def local(coregistered_sweeps, shard_opening_height, shard_goal_patch, shard_patch_place):
    earth_patch_total_size = lax.axis_size("ground")
    pair_count = lax.axis_size("pair")
    piece_count = shard_opening_height.shape[0]
    place_allowance = max(
        2, (2 * piece_count + earth_patch_total_size - 1) // earth_patch_total_size
    )
    sweep_resident = coregistered_sweeps[0, 0]
    target = shard_goal_patch[:, 0]
    hits = (target[:, None] == jnp.arange(earth_patch_total_size, dtype=jnp.int32)[None, :]).astype(
        jnp.int32
    )
    order = jnp.arange(piece_count, dtype=jnp.int32)
    before = (order[None, :] < order[:, None]).astype(jnp.bfloat16)
    earlier = jnp.dot(before, hits.astype(jnp.bfloat16), preferred_element_type=jnp.float32).astype(jnp.int32)
    rank = jnp.sum(earlier * hits, axis=1)
    position = target * place_allowance + rank
    matches = (
        position[None, :]
        == jnp.arange(earth_patch_total_size * place_allowance, dtype=jnp.int32)[:, None]
    ).astype(jnp.int32)
    tiles_filled = jnp.sum(matches, axis=1) > 0
    sweep_height_offset = (
        jnp.sum(matches * shard_opening_height[None, :], axis=1)[:, None] + jnp.arange(SHARD_HEIGHT, dtype=jnp.int32)[None, :]
    )
    wanted = jnp.where(tiles_filled[:, None], sweep_height_offset, -1).reshape(-1)
    picked = wanted[:, None] == jnp.arange(sweep_resident.shape[0], dtype=jnp.int32)[None, :]
    pieces_to_send = jnp.dot(
        picked.astype(jnp.bfloat16),
        sweep_resident.reshape(sweep_resident.shape[0], -1),
        preferred_element_type=jnp.float32,
    ).astype(jnp.bfloat16)
    labels = jnp.sum(matches * (shard_patch_place + 1)[None, :], axis=1).astype(jnp.bfloat16)
    received_pieces, arrived_labels = (
        lax.all_to_all(
            pieces_to_send.reshape(
                earth_patch_total_size, place_allowance, SHARD_HEIGHT, 2, SWEEP_WIDTH
            ),
            "ground",
            split_axis=0,
            concat_axis=0,
            tiled=True,
        ),
        lax.all_to_all(
            labels.reshape(earth_patch_total_size, place_allowance),
            "ground",
            split_axis=0,
            concat_axis=0,
            tiled=True,
        ),
    )
    pieces_flattened = received_pieces.reshape(
        earth_patch_total_size * place_allowance, SHARD_HEIGHT * 2 * SWEEP_WIDTH
    )
    slot_labels = (jnp.arange(SLOTS, dtype=jnp.int32) + 1).astype(jnp.bfloat16)
    selector = arrived_labels.reshape(-1)[None, :] == slot_labels[:, None]
    totals = jnp.dot(
        selector.astype(jnp.bfloat16), pieces_flattened, preferred_element_type=jnp.float32
    )
    counts = jnp.sum(selector.astype(jnp.float32), axis=1)
    smoothed_pixel_mean = (totals / jnp.maximum(counts, 1.0)[:, None]).astype(jnp.bfloat16)
    ground_tile = (
        smoothed_pixel_mean.reshape(PATCH_SHARD_LEVEL, 2, SHARD_HEIGHT, 2, SWEEP_WIDTH)
        .transpose(0, 2, 3, 1, 4)
        .reshape(TILE_ROWS, 2, TILE_COLS)
    )
    pair_width = pair_count - 1
    own_refs = partners_of(lax.axis_index("pair"), pair_width)
    piece = lax.all_gather(ground_tile[None], "pair", axis=0, tiled=True)
    looked_piece = multilook(piece, ground_tile[None])
    indices = jnp.arange(piece.shape[0], dtype=jnp.int32)
    selection = (own_refs[:, None] == indices[None, :]).astype(jnp.float32)
    looked = jnp.einsum("kn,nabc->kabc", selection, looked_piece, precision=lax.Precision.HIGHEST)
    return goldstein(looked)[None, :, None]


CAP_VMEM = 58 * 1024 * 1024
MESH = pl.DeviceIdType.MESH
EXACT = lax.Precision.HIGHEST
COLS = 16
LANES = 128


def fused_kernel(
    sweep_hbm, opening_hbm, goal_hbm, place_hbm, part_hbm, widen_hbm, row_dft_hbm, left_hbm, back_hbm,
    out,
    sweep, ints, part, widen, row_dft, left, back_mat, outgoing, arrived, meta_out, meta, tops, rows, gathered,
    chosen, scale, sums, looked_out, looked_in, folded,
    load_sem, part_sem, send_sem, recv_sem, meta_send, meta_recv, top_sem, look_send, look_recv, gate,
):
    me = lax.axis_index("ground")
    mine = lax.axis_index("pair")
    tile_count = meta.shape[0]
    piece_count = ints.shape[2]
    device_count = 2 * tile_count
    level_count = tile_count // 4
    level = me // 4
    spot = lax.rem(me, 4)
    self_id = me * 2 + mine
    barrier = pltpu.get_barrier_semaphore()

    loads = [
        pltpu.make_async_copy(source, sink, load_sem.at[at])
        for at, (source, sink) in enumerate(
            [
                (sweep_hbm, sweep),
                (opening_hbm, ints.at[0]),
                (goal_hbm, ints.at[1]),
                (place_hbm, ints.at[2]),
                (widen_hbm, widen),
                (row_dft_hbm, row_dft),
                (left_hbm, left),
                (back_hbm, back_mat),
            ]
        )
    ]

    def spot_of(step):
        return lax.rem(spot // 2 + step // 2, 2) * 2 + lax.rem(spot + step, 2)

    parts = [
        pltpu.make_async_copy(part_hbm.at[spot_of(step)], part.at[step], part_sem.at[step]) for step in range(4)
    ]
    for copy in [loads[0], parts[0]] + loads[1:4] + parts[1:] + loads[4:]:
        copy.start()

    above = device_count - 8 * level

    def greet(step, carry):
        number = 8 * level + lax.rem(self_id - 8 * level + step, above)
        pl.semaphore_signal(
            barrier, inc=1, device_id={"ground": number // 2, "pair": lax.rem(number, 2)}, device_id_type=MESH
        )
        return carry

    lax.fori_loop(1, above, greet, 0)
    pl.semaphore_wait(barrier, 8 * level + 7)
    for plane in range(level_count - 1):

        @pl.when(plane < level)
        def _():
            pl.semaphore_signal(
                gate.at[level], inc=1, device_id={"ground": plane * 4 + spot, "pair": mine}, device_id_type=MESH
            )

    def block(step, plane, other):
        return pltpu.make_async_remote_copy(
            src_ref=outgoing.at[(step * 2 + other) * level_count + plane],
            dst_ref=arrived.at[me, mine],
            send_sem=send_sem,
            recv_sem=recv_sem.at[me],
            device_id={"ground": plane * 4 + spot_of(step), "pair": other},
            device_id_type=MESH,
        )

    def label(target):
        return pltpu.make_async_remote_copy(
            src_ref=meta_out,
            dst_ref=meta.at[me],
            send_sem=meta_send,
            recv_sem=meta_recv,
            device_id={"ground": target, "pair": mine},
            device_id_type=MESH,
        )

    def labels(plane):
        for step in range(4):
            label(plane * 4 + spot_of(step)).start()

    for copy in loads[1:4]:
        copy.wait()
    meta_out[...] = jnp.concatenate([ints[0] * 2, ints[1] * SLOTS + ints[2]], axis=1)
    meta[me] = meta_out[...]
    loads[0].wait()

    for step in range(4):
        parts[step].wait()
        for at in range(level_count):
            if step == 0:
                for row in range(8):
                    folded[at, :, row * LANES:(row + 1) * LANES] = sweep[
                        row * 64:(row + 1) * 64, :, at * LANES:(at + 1) * LANES
                    ].reshape(LANES, LANES)
            moved = jnp.dot(folded[at], part[step], preferred_element_type=jnp.float32).astype(jnp.bfloat16)
            outgoing[step * 2 * level_count + at] = moved[:, :LANES]
            outgoing[(step * 2 + 1) * level_count + at] = moved[:, LANES:]
        for plane in range(level_count - 1):

            @pl.when(plane < level)
            def _():
                if step == 0:
                    labels(plane)
                for other in range(2):
                    block(step, plane, other).start()

        if step == 0:
            for turn in range(1, 4):
                label(level * 4 + spot_of(turn)).start()
            block(step, level, 1 - mine).start()
            arrived[me, mine] = outgoing[mine * level_count + level]
        else:
            for other in range(2):
                block(step, level, other).start()
        for plane in (1, 3, 2):

            @pl.when(plane > level)
            def _():
                opening_step = 0 if plane < level_count - 1 else 1
                if step == opening_step:
                    pl.semaphore_wait(gate.at[plane], 1)
                    labels(plane)
                if step >= opening_step:
                    for turn in range(0 if step == opening_step else step, step + 1):
                        for other in range(2):
                            block(turn, plane, other).start()

    pltpu.make_async_remote_copy(
        src_ref=meta.at[pl.ds(0, tile_count - 1)],
        dst_ref=meta.at[pl.ds(0, tile_count - 1)],
        send_sem=meta_send,
        recv_sem=meta_recv,
        device_id={"ground": me, "pair": 1 - mine},
        device_id_type=MESH,
    ).wait()
    to_scalars = pltpu.make_async_copy(meta, tops, top_sem)
    to_scalars.start()
    for copy in loads[4:]:
        copy.wait()

    near = level + 1 - 2 * lax.rem(level, 2)
    cross = 2 - 2 * (level // 2)
    order = [(plane, step) for step in range(4) for plane in (level, near, 3 - 3 * (level // 2), 2 - level // 2)]
    sources = [plane * 4 + spot_of(step) for plane, step in order]

    lane1 = lax.broadcasted_iota(jnp.int32, (1, LANES), 1)
    width = tile_count * piece_count
    for at in range(tile_count // 2):
        keys = jnp.where(lane1 < 64, pltpu.roll(meta[sources[2 * at]], 64, 1), meta[sources[2 * at + 1]])
        slots = lax.broadcasted_iota(jnp.int32, (tile_count * SLOTS, LANES), 0)
        chosen[:, at * LANES:(at + 1) * LANES] = jnp.where(slots == keys, 1.0, 0.0).astype(jnp.bfloat16)
    count = jnp.dot(chosen[...], jnp.ones((width, LANES), jnp.bfloat16), preferred_element_type=jnp.float32)
    scale[...] = 1.0 / jnp.maximum(count, 1.0)
    to_scalars.wait()

    lane8 = lax.broadcasted_iota(jnp.int32, (8, LANES), 1)
    cuts = (8, 12)
    early = cuts[-1] * piece_count

    def columns(pair_row, first, last):
        return jnp.concatenate(
            [gathered[(2 * pair_row + part) * width + first:(2 * pair_row + part) * width + last] for part in range(2)],
            axis=1,
        ).astype(jnp.bfloat16)

    for position, source in enumerate(sources):
        if position == 0:
            pltpu.make_async_remote_copy(
                src_ref=outgoing.at[0],
                dst_ref=arrived.at[me, 1 - mine],
                send_sem=send_sem,
                recv_sem=recv_sem.at[me],
                device_id={"ground": me, "pair": 1 - mine},
                device_id_type=MESH,
            ).wait_recv()
        else:
            pltpu.make_async_remote_copy(
                src_ref=arrived.at[source],
                dst_ref=arrived.at[source],
                send_sem=send_sem,
                recv_sem=recv_sem.at[source],
                device_id={"ground": source, "pair": mine},
                device_id_type=MESH,
            ).wait_recv()
        both = jnp.concatenate([arrived[source, 0], arrived[source, 1]], axis=1)
        for quarter in range(4):
            spread = jnp.dot(both, widen[quarter], preferred_element_type=jnp.float32)
            rows[quarter * 256:quarter * 256 + LANES] = spread[:, :LANES]
            rows[quarter * 256 + LANES:quarter * 256 + 256] = spread[:, LANES:]

        for piece in range(piece_count):
            top = tops[source, 0, piece]
            value = rows[pl.ds(top, 8), :]
            for shift in range(1, 4):
                value = jnp.where(lane8 < shift * 32, value, rows[pl.ds(top + 8 * shift, 8), :])
            gathered[pl.ds(position * piece_count + piece, 8, stride=width), :] = value
        if position + 1 in cuts:
            last = (position + 1) * piece_count
            first = 0 if position + 1 == cuts[0] else cuts[cuts.index(position + 1) - 1] * piece_count
            for pair_row in range(4):
                part_sum = jnp.dot(
                    chosen[:, first:last], columns(pair_row, first, last), preferred_element_type=jnp.float32
                )
                sums[pair_row] = part_sum if first == 0 else sums[pair_row] + part_sum

    same = jnp.zeros((tile_count * SLOTS, LANES), jnp.float32)
    crossed = same
    for pair_row in range(4):
        total = sums[pair_row] + jnp.dot(
            chosen[:, early:], columns(pair_row, early, width), preferred_element_type=jnp.float32
        )
        real = (total[:, :LANES] * scale[...]).astype(jnp.bfloat16).astype(jnp.float32)
        imag = (total[:, LANES:] * scale[...]).astype(jnp.bfloat16).astype(jnp.float32)
        real_other = pltpu.roll(real, LANES - COLS, 1)
        imag_other = pltpu.roll(imag, LANES - COLS, 1)
        same = same + real * real_other + imag * imag_other
        crossed = crossed + imag_other * real - real_other * imag
    lane = lax.broadcasted_iota(jnp.int32, same.shape, 1)
    merged = jnp.where(lane % 32 < COLS, same, pltpu.roll(crossed, COLS, 1))
    high = merged.astype(jnp.bfloat16)
    low = (merged - high.astype(jnp.float32)).astype(jnp.bfloat16)
    row8 = lax.broadcasted_iota(jnp.int32, (8, LANES), 0)
    pool = jnp.where(lane8 // COLS == (row8 % 4) * 2 + row8 // 4, 1.0 / (LOOK_ROWS * LOOK_COLS), 0.0)
    pool = pool.astype(jnp.bfloat16)
    pooled = lax.dot_general(
        jnp.concatenate([pool, pool], axis=1),
        jnp.concatenate([high, low], axis=1),
        (((1,), (1,)), ((), ())),
        preferred_element_type=jnp.float32,
    )
    for group in range(tile_count // 4):
        piece = pooled[:, group * LANES:(group + 1) * LANES]
        turned = piece
        for shift in range(1, 4):
            moved = pltpu.roll(pltpu.roll(piece, LANES - 32 * shift, 1), 2 * shift, 0)
            turned = jnp.where((row8 // 2 - lane8 // 32 + 4) % 4 == shift, moved, turned)
        for inner in range(4):
            looked_out[group * 4 + inner] = turned[2 * inner:2 * inner + 2]

    away = level // 2
    for plane in (3 - 3 * away, 2 - away, near, level):
        for step in (3, 2, 1, 0):
            target = plane * 4 + spot_of(step)
            for other in (1 - mine, mine):
                if plane is level and step == 0 and other is mine:
                    continue
                pltpu.make_async_remote_copy(
                    src_ref=looked_out.at[target],
                    dst_ref=looked_in.at[self_id],
                    send_sem=look_send,
                    recv_sem=look_recv,
                    device_id={"ground": target, "pair": other},
                    device_id_type=MESH,
                ).start()
    looked_in[self_id] = looked_out[me]
    pltpu.make_async_remote_copy(
        src_ref=outgoing.at[pl.ds(0, device_count - 1)],
        dst_ref=outgoing.at[pl.ds(0, device_count - 1)],
        send_sem=send_sem,
        recv_sem=recv_sem.at[0],
        device_id={"ground": me, "pair": 1 - mine},
        device_id_type=MESH,
    ).wait_send()
    pltpu.make_async_remote_copy(
        src_ref=looked_in.at[pl.ds(0, device_count - 1)],
        dst_ref=looked_in.at[pl.ds(0, device_count - 1)],
        send_sem=look_send,
        recv_sem=look_recv,
        device_id={"ground": me, "pair": 1 - mine},
        device_id_type=MESH,
    ).wait()

    def split(value):
        first = value.astype(jnp.bfloat16)
        return first, (value - first.astype(jnp.float32)).astype(jnp.bfloat16)

    flip = 1.0 - 2.0 * mine.astype(jnp.float32)
    lanes = lax.broadcasted_iota(jnp.int32, (device_count, LANES), 1)
    sign = jnp.where(lanes < 64, 1.0, flip)
    field = jnp.concatenate([looked_in[:, 0, :] * sign, looked_in[:, 1, :] * sign], axis=1)
    first, second = split(field)
    field = jnp.dot(
        jnp.concatenate([first, second, first], axis=1), row_dft[...], preferred_element_type=jnp.float32
    )
    field = jnp.concatenate([field[:, :LANES], field[:, LANES:]], axis=0)
    length = out.shape[1]
    turn = jnp.where(lax.broadcasted_iota(jnp.int32, (length, 2 * length), 1) < length, 1.0, -1.0)
    first, second = split(field)
    both = jnp.dot(
        left[...], jnp.concatenate([first, second, first], axis=0), preferred_element_type=jnp.float32
    )
    spectrum = both[:length] + turn * pltpu.roll(both[length:], length, 1)
    power = spectrum * spectrum
    power = power + pltpu.roll(power, length, 1)
    weight = jnp.sqrt(jnp.sqrt(power + 1e-06))
    mean = jnp.sum(weight) * (1.0 / (2 * length * length))
    spectrum = spectrum * (weight / mean)
    first, second = split(spectrum)
    both = jnp.dot(
        left[...], jnp.concatenate([first, second, first], axis=0), preferred_element_type=jnp.float32
    )
    back = both[:length] - turn * pltpu.roll(both[length:], length, 1)
    first, second = split(back)
    result = lax.dot_general(
        back_mat[...],
        jnp.concatenate([first, second, first], axis=1),
        (((1,), (1,)), ((), ())),
        preferred_element_type=jnp.float32,
    ) * (1.0 / (length * length))
    out[0] = result[:length]
    out[1] = result[length:]


def constants():
    row = np.arange(1024)
    col = np.arange(256)
    lane, group = row % 128, row // 128
    part = np.stack(
        [
            (lane[:, None] // 32 == spot)
            & (col[None, :] // 128 == lane[:, None] // 16 % 2)
            & (col[None, :] % 128 // 16 == group[:, None])
            & (col[None, :] % 16 == lane[:, None] % 16)
            for spot in range(4)
        ]
    ).astype(jnp.bfloat16)
    row = np.arange(256)
    widen = np.stack(
        [
            (row[:, None] // 128 == col[None, :] // 16 % 2)
            & (row[:, None] % 128 // 16 == 2 * quarter + col[None, :] // 128)
            & (row[:, None] % 16 == col[None, :] % 16)
            for quarter in range(4)
        ]
    ).astype(jnp.bfloat16)
    low, high, slot = row // 128, row % 128 // 32, row % 32
    kind, box = (2 * high + low) // 4, (2 * high + low) % 4
    line = slot // 2 * 4 + box
    out_side, out_kind, frequency = col // 128, col // 64 % 2, col % 64
    angle = (line[:, None] * frequency[None, :] % 64) * (2.0 * math.pi / 64)
    mixed = np.where(
        kind[:, None] == out_kind[None, :],
        np.cos(angle),
        np.where(kind[:, None] == 0, -np.sin(angle), np.sin(angle)),
    )
    row_dft = np.where(slot[:, None] % 2 == out_side[None, :], mixed, 0.0)
    column = np.arange(64)
    angle = (column[:, None] * column[None, :] % 64) * (2.0 * math.pi / 64)
    cosine, sine = np.cos(angle), np.sin(angle)
    left = np.concatenate([cosine, sine], 0)
    back = np.block([[cosine, -sine], [sine, cosine]])

    def parts_of(value, axis):
        first = value.astype(np.float32).astype(jnp.bfloat16)
        second = (value - first.astype(np.float64)).astype(np.float32).astype(jnp.bfloat16)
        return np.concatenate([first, first, second], axis)

    return part, widen, parts_of(row_dft, 0), parts_of(left, 1), parts_of(back, 1)


def local_pair(coregistered_sweeps, shard_opening_height, shard_goal_patch, shard_patch_place):
    tile_count = lax.axis_size("ground")
    level_count = tile_count // 4
    tables = constants()
    vmem = pl.BlockSpec(memory_space=pltpu.VMEM)
    anyplace = pl.BlockSpec(memory_space=pltpu.HBM)
    dma = pltpu.SemaphoreType.DMA
    filtered = pl.pallas_call(
        fused_kernel,
        out_shape=pltpu.VMEM((2, 64, 64), jnp.float32),
        in_specs=[anyplace] * 9,
        out_specs=vmem,
        scratch_shapes=[
            pltpu.VMEM((512, 2, 512), jnp.bfloat16),
            pltpu.VMEM((3, 1, 64), jnp.int32),
            pltpu.VMEM((4, 1024, 256), jnp.bfloat16),
            pltpu.VMEM((4, 256, 256), jnp.bfloat16),
            pltpu.VMEM((3 * 256, 256), jnp.bfloat16),
            pltpu.VMEM((128, 3 * 64), jnp.bfloat16),
            pltpu.VMEM((128, 3 * 128), jnp.bfloat16),
            pltpu.VMEM((2 * tile_count, 128, 128), jnp.bfloat16),
            pltpu.VMEM((tile_count, 2, 128, 128), jnp.bfloat16),
            pltpu.VMEM((1, 128), jnp.int32),
            pltpu.VMEM((tile_count, 1, 128), jnp.int32),
            pltpu.SMEM((tile_count, 1, 128), jnp.int32),
            pltpu.VMEM((1024, 128), jnp.float32),
            pltpu.VMEM((8 * tile_count * 64, 128), jnp.float32),
            pltpu.VMEM((tile_count * SLOTS, tile_count * 64), jnp.bfloat16),
            pltpu.VMEM((tile_count * SLOTS, 128), jnp.float32),
            pltpu.VMEM((4, tile_count * SLOTS, 256), jnp.float32),
            pltpu.VMEM((tile_count, 2, 128), jnp.float32),
            pltpu.VMEM((2 * tile_count, 2, 128), jnp.float32),
            pltpu.VMEM((4, 128, 1024), jnp.bfloat16),
            dma((8,)),
            dma((4,)),
            dma,
            dma((tile_count,)),
            dma,
            dma,
            dma,
            dma,
            dma,
            pltpu.SemaphoreType.REGULAR((level_count,)),
        ],
        compiler_params=pltpu.CompilerParams(
            collective_id=0, has_side_effects=True, vmem_limit_bytes=CAP_VMEM
        ),
    )(
        coregistered_sweeps[0, 0],
        shard_opening_height.reshape(1, -1),
        shard_goal_patch.reshape(1, -1),
        shard_patch_place.reshape(1, -1),
        *tables,
    )
    return filtered[None, None, None]


def solution(mesh):
    placed = (P("pair", "ground", None, None, None), P("ground"), P("ground", None), P("ground"))
    return jax.shard_map(
        local_pair if dict(mesh.shape) == {"ground": 16, "pair": 2} else local,
        mesh=mesh,
        in_specs=placed,
        out_specs=P("pair", None, "ground", None, None, None),
        check_vma=False,
    )
```

```python
import functools
import math

import jax
import jax.numpy as jnp
import numpy as np
from jax import lax
from jax.experimental import pallas as pl
from jax.experimental.pallas import tpu as pltpu
from jax.sharding import PartitionSpec as P

LOOK_ROWS = 4
LOOK_COLS = 16
SHARD_HEIGHT = 16
TILE_ROWS = 256
TILE_COLS = 1024
SWEEP_WIDTH = 512
PATCH_SHARD_LEVEL = 16
SLOTS = 32


def multilook(reference_tiles, secondary_tiles):
    first = reference_tiles.astype(jnp.float32)
    second = secondary_tiles.astype(jnp.float32)
    real_part = first[..., 0, :] * second[..., 0, :] + first[..., 1, :] * second[..., 1, :]
    imag_part = first[..., 1, :] * second[..., 0, :] - first[..., 0, :] * second[..., 1, :]
    joined = jnp.stack([real_part, imag_part], axis=-3)
    leading = joined.shape[:-2]
    row_count = joined.shape[-2]
    col_count = joined.shape[-1]
    boxes = joined.reshape(
        leading + (row_count // LOOK_ROWS, LOOK_ROWS, col_count // LOOK_COLS, LOOK_COLS)
    )
    return jnp.mean(boxes, axis=(-3, -1))


def on_left(matrix, field):
    return jnp.einsum("ij,...jk->...ik", matrix, field, precision=lax.Precision.HIGHEST)


def on_right(field, matrix):
    return jnp.einsum("...ij,jk->...ik", field, matrix, precision=lax.Precision.HIGHEST)


def goldstein(looked):
    length = looked.shape[-1]
    positions = jnp.arange(length, dtype=jnp.int32)
    phase = positions[:, None] * positions[None, :] % length
    angle = phase.astype(jnp.float32) * (2.0 * math.pi / length)
    cosine = jnp.cos(angle)
    sine = jnp.sin(angle)
    real_in = looked[..., 0, :, :]
    imag_in = looked[..., 1, :, :]
    half_real = on_left(cosine, real_in) + on_left(sine, imag_in)
    half_imag = on_left(cosine, imag_in) - on_left(sine, real_in)
    spec_real = on_right(half_real, cosine) + on_right(half_imag, sine)
    spec_imag = on_right(half_imag, cosine) - on_right(half_real, sine)
    weight = (spec_real * spec_real + spec_imag * spec_imag + 1e-06) ** 0.25
    weight = weight / jnp.mean(weight, axis=(-2, -1), keepdims=True)
    spec_real = spec_real * weight
    spec_imag = spec_imag * weight
    back_real = on_left(cosine, spec_real) - on_left(sine, spec_imag)
    back_imag = on_left(cosine, spec_imag) + on_left(sine, spec_real)
    out_real = on_right(back_real, cosine) - on_right(back_imag, sine)
    out_imag = on_right(back_imag, cosine) + on_right(back_real, sine)
    scale = 1.0 / (length * length)
    return jnp.stack([out_real * scale, out_imag * scale], axis=-3)


def partners_of(index, pair_width):
    order = jnp.arange(pair_width, dtype=jnp.int32)
    return order + (order >= index).astype(jnp.int32)


def local(coregistered_sweeps, shard_opening_height, shard_goal_patch, shard_patch_place):
    earth_patch_total_size = lax.axis_size("ground")
    pair_count = lax.axis_size("pair")
    piece_count = shard_opening_height.shape[0]
    place_allowance = max(
        2, (2 * piece_count + earth_patch_total_size - 1) // earth_patch_total_size
    )
    sweep_resident = coregistered_sweeps[0, 0]
    target = shard_goal_patch[:, 0]
    hits = (target[:, None] == jnp.arange(earth_patch_total_size, dtype=jnp.int32)[None, :]).astype(
        jnp.int32
    )
    order = jnp.arange(piece_count, dtype=jnp.int32)
    before = (order[None, :] < order[:, None]).astype(jnp.bfloat16)
    earlier = jnp.dot(before, hits.astype(jnp.bfloat16), preferred_element_type=jnp.float32).astype(jnp.int32)
    rank = jnp.sum(earlier * hits, axis=1)
    position = target * place_allowance + rank
    matches = (
        position[None, :]
        == jnp.arange(earth_patch_total_size * place_allowance, dtype=jnp.int32)[:, None]
    ).astype(jnp.int32)
    tiles_filled = jnp.sum(matches, axis=1) > 0
    sweep_height_offset = (
        jnp.sum(matches * shard_opening_height[None, :], axis=1)[:, None] + jnp.arange(SHARD_HEIGHT, dtype=jnp.int32)[None, :]
    )
    wanted = jnp.where(tiles_filled[:, None], sweep_height_offset, -1).reshape(-1)
    picked = wanted[:, None] == jnp.arange(sweep_resident.shape[0], dtype=jnp.int32)[None, :]
    pieces_to_send = jnp.dot(
        picked.astype(jnp.bfloat16),
        sweep_resident.reshape(sweep_resident.shape[0], -1),
        preferred_element_type=jnp.float32,
    ).astype(jnp.bfloat16)
    labels = jnp.sum(matches * (shard_patch_place + 1)[None, :], axis=1).astype(jnp.bfloat16)
    received_pieces, arrived_labels = (
        lax.all_to_all(
            pieces_to_send.reshape(
                earth_patch_total_size, place_allowance, SHARD_HEIGHT, 2, SWEEP_WIDTH
            ),
            "ground",
            split_axis=0,
            concat_axis=0,
            tiled=True,
        ),
        lax.all_to_all(
            labels.reshape(earth_patch_total_size, place_allowance),
            "ground",
            split_axis=0,
            concat_axis=0,
            tiled=True,
        ),
    )
    pieces_flattened = received_pieces.reshape(
        earth_patch_total_size * place_allowance, SHARD_HEIGHT * 2 * SWEEP_WIDTH
    )
    slot_labels = (jnp.arange(SLOTS, dtype=jnp.int32) + 1).astype(jnp.bfloat16)
    selector = arrived_labels.reshape(-1)[None, :] == slot_labels[:, None]
    totals = jnp.dot(
        selector.astype(jnp.bfloat16), pieces_flattened, preferred_element_type=jnp.float32
    )
    counts = jnp.sum(selector.astype(jnp.float32), axis=1)
    smoothed_pixel_mean = (totals / jnp.maximum(counts, 1.0)[:, None]).astype(jnp.bfloat16)
    ground_tile = (
        smoothed_pixel_mean.reshape(PATCH_SHARD_LEVEL, 2, SHARD_HEIGHT, 2, SWEEP_WIDTH)
        .transpose(0, 2, 3, 1, 4)
        .reshape(TILE_ROWS, 2, TILE_COLS)
    )
    pair_width = pair_count - 1
    own_refs = partners_of(lax.axis_index("pair"), pair_width)
    piece = lax.all_gather(ground_tile[None], "pair", axis=0, tiled=True)
    looked_piece = multilook(piece, ground_tile[None])
    indices = jnp.arange(piece.shape[0], dtype=jnp.int32)
    selection = (own_refs[:, None] == indices[None, :]).astype(jnp.float32)
    looked = jnp.einsum("kn,nabc->kabc", selection, looked_piece, precision=lax.Precision.HIGHEST)
    return goldstein(looked)[None, :, None]


CAP_VMEM = 58 * 1024 * 1024
MESH = pl.DeviceIdType.MESH
EXACT = lax.Precision.HIGHEST
COLS = 16
LANES = 128


def fused_kernel(
    sweep_hbm, opening_hbm, goal_hbm, place_hbm, part_hbm, widen_hbm, row_dft_hbm, left_hbm, back_hbm,
    out,
    sweep, ints, part, widen, row_dft, left, back_mat, outgoing, arrived, meta_out, meta, tops, rows, gathered,
    chosen, scale, sums, looked_out, looked_in, folded,
    load_sem, part_sem, send_sem, recv_sem, meta_send, meta_recv, top_sem, look_send, look_recv, gate,
):
    me = lax.axis_index("ground")
    mine = lax.axis_index("pair")
    tile_count = meta.shape[0]
    piece_count = ints.shape[2]
    device_count = 2 * tile_count
    level_count = tile_count // 4
    level = me // 4
    spot = lax.rem(me, 4)
    self_id = me * 2 + mine
    barrier = pltpu.get_barrier_semaphore()

    loads = [
        pltpu.make_async_copy(source, sink, load_sem.at[at])
        for at, (source, sink) in enumerate(
            [
                (sweep_hbm, sweep),
                (opening_hbm, ints.at[0]),
                (goal_hbm, ints.at[1]),
                (place_hbm, ints.at[2]),
                (widen_hbm, widen),
                (row_dft_hbm, row_dft),
                (left_hbm, left),
                (back_hbm, back_mat),
            ]
        )
    ]

    def spot_of(step):
        return lax.rem(spot // 2 + step // 2, 2) * 2 + lax.rem(spot + step, 2)

    parts = [
        pltpu.make_async_copy(part_hbm.at[spot_of(step)], part.at[step], part_sem.at[step]) for step in range(4)
    ]
    for copy in [loads[0], parts[0]] + loads[1:4] + parts[1:] + loads[4:]:
        copy.start()

    above = device_count - 8 * level

    def greet(step, carry):
        number = 8 * level + lax.rem(self_id - 8 * level + step, above)
        pl.semaphore_signal(
            barrier, inc=1, device_id={"ground": number // 2, "pair": lax.rem(number, 2)}, device_id_type=MESH
        )
        return carry

    lax.fori_loop(1, above, greet, 0)
    pl.semaphore_wait(barrier, 8 * level + 7)
    for plane in range(level_count - 1):

        @pl.when(plane < level)
        def _():
            pl.semaphore_signal(
                gate.at[level], inc=1, device_id={"ground": plane * 4 + spot, "pair": mine}, device_id_type=MESH
            )

    def block(step, plane, other):
        return pltpu.make_async_remote_copy(
            src_ref=outgoing.at[(step * 2 + other) * level_count + plane],
            dst_ref=arrived.at[me, mine],
            send_sem=send_sem,
            recv_sem=recv_sem.at[me],
            device_id={"ground": plane * 4 + spot_of(step), "pair": other},
            device_id_type=MESH,
        )

    def label(target):
        return pltpu.make_async_remote_copy(
            src_ref=meta_out,
            dst_ref=meta.at[me],
            send_sem=meta_send,
            recv_sem=meta_recv,
            device_id={"ground": target, "pair": mine},
            device_id_type=MESH,
        )

    def labels(plane):
        for step in range(4):
            label(plane * 4 + spot_of(step)).start()

    for copy in loads[1:4]:
        copy.wait()
    meta_out[...] = jnp.concatenate([ints[0] * 2, ints[1] * SLOTS + ints[2]], axis=1)
    meta[me] = meta_out[...]
    loads[0].wait()

    for step in range(4):
        parts[step].wait()
        for at in range(level_count):
            if step == 0:
                for row in range(8):
                    folded[at, :, row * LANES:(row + 1) * LANES] = sweep[
                        row * 64:(row + 1) * 64, :, at * LANES:(at + 1) * LANES
                    ].reshape(LANES, LANES)
            moved = jnp.dot(folded[at], part[step], preferred_element_type=jnp.float32).astype(jnp.bfloat16)
            outgoing[step * 2 * level_count + at] = moved[:, :LANES]
            outgoing[(step * 2 + 1) * level_count + at] = moved[:, LANES:]
        for plane in range(level_count - 1):

            @pl.when(plane < level)
            def _():
                if step == 0:
                    labels(plane)
                for other in range(2):
                    block(step, plane, other).start()

        if step == 0:
            for turn in range(1, 4):
                label(level * 4 + spot_of(turn)).start()
            block(step, level, 1 - mine).start()
            arrived[me, mine] = outgoing[mine * level_count + level]
        else:
            for other in range(2):
                block(step, level, other).start()
        for plane in (1, 3, 2):

            @pl.when(plane > level)
            def _():
                opening_step = 0 if plane < level_count - 1 else 1
                if step == opening_step:
                    pl.semaphore_wait(gate.at[plane], 1)
                    labels(plane)
                if step >= opening_step:
                    for turn in range(0 if step == opening_step else step, step + 1):
                        for other in range(2):
                            block(turn, plane, other).start()

    pltpu.make_async_remote_copy(
        src_ref=meta.at[pl.ds(0, tile_count - 1)],
        dst_ref=meta.at[pl.ds(0, tile_count - 1)],
        send_sem=meta_send,
        recv_sem=meta_recv,
        device_id={"ground": me, "pair": 1 - mine},
        device_id_type=MESH,
    ).wait()
    to_scalars = pltpu.make_async_copy(meta, tops, top_sem)
    to_scalars.start()
    for copy in loads[4:]:
        copy.wait()

    near = level + 1 - 2 * lax.rem(level, 2)
    cross = 2 - 2 * (level // 2)
    order = [(plane, step) for step in range(4) for plane in (level, near, 3 - 3 * (level // 2), 2 - level // 2)]
    sources = [plane * 4 + spot_of(step) for plane, step in order]

    lane1 = lax.broadcasted_iota(jnp.int32, (1, LANES), 1)
    width = tile_count * piece_count
    for at in range(tile_count // 2):
        keys = jnp.where(lane1 < 64, pltpu.roll(meta[sources[2 * at]], 64, 1), meta[sources[2 * at + 1]])
        slots = lax.broadcasted_iota(jnp.int32, (tile_count * SLOTS, LANES), 0)
        chosen[:, at * LANES:(at + 1) * LANES] = jnp.where(slots == keys, 1.0, 0.0).astype(jnp.bfloat16)
    count = jnp.dot(chosen[...], jnp.ones((width, LANES), jnp.bfloat16), preferred_element_type=jnp.float32)
    scale[...] = 1.0 / jnp.maximum(count, 1.0)
    to_scalars.wait()

    lane8 = lax.broadcasted_iota(jnp.int32, (8, LANES), 1)
    cuts = (8, 12)
    early = cuts[-1] * piece_count

    def columns(pair_row, first, last):
        return jnp.concatenate(
            [gathered[(2 * pair_row + part) * width + first:(2 * pair_row + part) * width + last] for part in range(2)],
            axis=1,
        ).astype(jnp.bfloat16)

    for position, source in enumerate(sources):
        if position == 0:
            pltpu.make_async_remote_copy(
                src_ref=outgoing.at[0],
                dst_ref=arrived.at[me, 1 - mine],
                send_sem=send_sem,
                recv_sem=recv_sem.at[me],
                device_id={"ground": me, "pair": 1 - mine},
                device_id_type=MESH,
            ).wait_recv()
        else:
            pltpu.make_async_remote_copy(
                src_ref=arrived.at[source],
                dst_ref=arrived.at[source],
                send_sem=send_sem,
                recv_sem=recv_sem.at[source],
                device_id={"ground": source, "pair": mine},
                device_id_type=MESH,
            ).wait_recv()
        both = jnp.concatenate([arrived[source, 0], arrived[source, 1]], axis=1)
        for quarter in range(4):
            spread = jnp.dot(both, widen[quarter], preferred_element_type=jnp.float32)
            rows[quarter * 256:quarter * 256 + LANES] = spread[:, :LANES]
            rows[quarter * 256 + LANES:quarter * 256 + 256] = spread[:, LANES:]

        for piece in range(piece_count):
            top = tops[source, 0, piece]
            value = rows[pl.ds(top, 8), :]
            for shift in range(1, 4):
                value = jnp.where(lane8 < shift * 32, value, rows[pl.ds(top + 8 * shift, 8), :])
            gathered[pl.ds(position * piece_count + piece, 8, stride=width), :] = value
        if position + 1 in cuts:
            last = (position + 1) * piece_count
            first = 0 if position + 1 == cuts[0] else cuts[cuts.index(position + 1) - 1] * piece_count
            for pair_row in range(4):
                part_sum = jnp.dot(
                    chosen[:, first:last], columns(pair_row, first, last), preferred_element_type=jnp.float32
                )
                sums[pair_row] = part_sum if first == 0 else sums[pair_row] + part_sum

    same = jnp.zeros((tile_count * SLOTS, LANES), jnp.float32)
    crossed = same
    for pair_row in range(4):
        total = sums[pair_row] + jnp.dot(
            chosen[:, early:], columns(pair_row, early, width), preferred_element_type=jnp.float32
        )
        real = (total[:, :LANES] * scale[...]).astype(jnp.bfloat16).astype(jnp.float32)
        imag = (total[:, LANES:] * scale[...]).astype(jnp.bfloat16).astype(jnp.float32)
        real_other = pltpu.roll(real, LANES - COLS, 1)
        imag_other = pltpu.roll(imag, LANES - COLS, 1)
        same = same + real * real_other + imag * imag_other
        crossed = crossed + imag_other * real - real_other * imag
    lane = lax.broadcasted_iota(jnp.int32, same.shape, 1)
    merged = jnp.where(lane % 32 < COLS, same, pltpu.roll(crossed, COLS, 1))
    high = merged.astype(jnp.bfloat16)
    low = (merged - high.astype(jnp.float32)).astype(jnp.bfloat16)
    row8 = lax.broadcasted_iota(jnp.int32, (8, LANES), 0)
    pool = jnp.where(lane8 // COLS == (row8 % 4) * 2 + row8 // 4, 1.0 / (LOOK_ROWS * LOOK_COLS), 0.0)
    pool = pool.astype(jnp.bfloat16)
    pooled = lax.dot_general(
        jnp.concatenate([pool, pool], axis=1),
        jnp.concatenate([high, low], axis=1),
        (((1,), (1,)), ((), ())),
        preferred_element_type=jnp.float32,
    )
    for group in range(tile_count // 4):
        piece = pooled[:, group * LANES:(group + 1) * LANES]
        turned = piece
        for shift in range(1, 4):
            moved = pltpu.roll(pltpu.roll(piece, LANES - 32 * shift, 1), 2 * shift, 0)
            turned = jnp.where((row8 // 2 - lane8 // 32 + 4) % 4 == shift, moved, turned)
        for inner in range(4):
            looked_out[group * 4 + inner] = turned[2 * inner:2 * inner + 2]

    away = level // 2
    for plane in (3 - 3 * away, 2 - away, near, level):
        for step in (3, 2, 1, 0):
            target = plane * 4 + spot_of(step)
            for other in (1 - mine, mine):
                if plane is level and step == 0 and other is mine:
                    continue
                pltpu.make_async_remote_copy(
                    src_ref=looked_out.at[target],
                    dst_ref=looked_in.at[self_id],
                    send_sem=look_send,
                    recv_sem=look_recv,
                    device_id={"ground": target, "pair": other},
                    device_id_type=MESH,
                ).start()
    looked_in[self_id] = looked_out[me]
    pltpu.make_async_remote_copy(
        src_ref=outgoing.at[pl.ds(0, device_count - 1)],
        dst_ref=outgoing.at[pl.ds(0, device_count - 1)],
        send_sem=send_sem,
        recv_sem=recv_sem.at[0],
        device_id={"ground": me, "pair": 1 - mine},
        device_id_type=MESH,
    ).wait_send()
    pltpu.make_async_remote_copy(
        src_ref=looked_in.at[pl.ds(0, device_count - 1)],
        dst_ref=looked_in.at[pl.ds(0, device_count - 1)],
        send_sem=look_send,
        recv_sem=look_recv,
        device_id={"ground": me, "pair": 1 - mine},
        device_id_type=MESH,
    ).wait()

    def split(value):
        first = value.astype(jnp.bfloat16)
        return first, (value - first.astype(jnp.float32)).astype(jnp.bfloat16)

    flip = 1.0 - 2.0 * mine.astype(jnp.float32)
    lanes = lax.broadcasted_iota(jnp.int32, (device_count, LANES), 1)
    sign = jnp.where(lanes < 64, 1.0, flip)
    field = jnp.concatenate([looked_in[:, 0, :] * sign, looked_in[:, 1, :] * sign], axis=1)
    first, second = split(field)
    field = jnp.dot(
        jnp.concatenate([first, second, first], axis=1), row_dft[...], preferred_element_type=jnp.float32
    )
    field = jnp.concatenate([field[:, :LANES], field[:, LANES:]], axis=0)
    length = out.shape[1]
    turn = jnp.where(lax.broadcasted_iota(jnp.int32, (length, 2 * length), 1) < length, 1.0, -1.0)
    first, second = split(field)
    both = jnp.dot(
        left[...], jnp.concatenate([first, second, first], axis=0), preferred_element_type=jnp.float32
    )
    spectrum = both[:length] + turn * pltpu.roll(both[length:], length, 1)
    power = spectrum * spectrum
    power = power + pltpu.roll(power, length, 1)
    weight = jnp.sqrt(jnp.sqrt(power + 1e-06))
    mean = jnp.sum(weight) * (1.0 / (2 * length * length))
    spectrum = spectrum * (weight / mean)
    first, second = split(spectrum)
    both = jnp.dot(
        left[...], jnp.concatenate([first, second, first], axis=0), preferred_element_type=jnp.float32
    )
    back = both[:length] - turn * pltpu.roll(both[length:], length, 1)
    first, second = split(back)
    result = lax.dot_general(
        back_mat[...],
        jnp.concatenate([first, second, first], axis=1),
        (((1,), (1,)), ((), ())),
        preferred_element_type=jnp.float32,
    ) * (1.0 / (length * length))
    out[0] = result[:length]
    out[1] = result[length:]


def constants():
    row = np.arange(1024)
    col = np.arange(256)
    lane, group = row % 128, row // 128
    part = np.stack(
        [
            (lane[:, None] // 32 == spot)
            & (col[None, :] // 128 == lane[:, None] // 16 % 2)
            & (col[None, :] % 128 // 16 == group[:, None])
            & (col[None, :] % 16 == lane[:, None] % 16)
            for spot in range(4)
        ]
    ).astype(jnp.bfloat16)
    row = np.arange(256)
    widen = np.stack(
        [
            (row[:, None] // 128 == col[None, :] // 16 % 2)
            & (row[:, None] % 128 // 16 == 2 * quarter + col[None, :] // 128)
            & (row[:, None] % 16 == col[None, :] % 16)
            for quarter in range(4)
        ]
    ).astype(jnp.bfloat16)
    low, high, slot = row // 128, row % 128 // 32, row % 32
    kind, box = (2 * high + low) // 4, (2 * high + low) % 4
    line = slot // 2 * 4 + box
    out_side, out_kind, frequency = col // 128, col // 64 % 2, col % 64
    angle = (line[:, None] * frequency[None, :] % 64) * (2.0 * math.pi / 64)
    mixed = np.where(
        kind[:, None] == out_kind[None, :],
        np.cos(angle),
        np.where(kind[:, None] == 0, -np.sin(angle), np.sin(angle)),
    )
    row_dft = np.where(slot[:, None] % 2 == out_side[None, :], mixed, 0.0)
    column = np.arange(64)
    angle = (column[:, None] * column[None, :] % 64) * (2.0 * math.pi / 64)
    cosine, sine = np.cos(angle), np.sin(angle)
    left = np.concatenate([cosine, sine], 0)
    back = np.block([[cosine, -sine], [sine, cosine]])

    def parts_of(value, axis):
        first = value.astype(np.float32).astype(jnp.bfloat16)
        second = (value - first.astype(np.float64)).astype(np.float32).astype(jnp.bfloat16)
        return np.concatenate([first, first, second], axis)

    return part, widen, parts_of(row_dft, 0), parts_of(left, 1), parts_of(back, 1)


def local_pair(coregistered_sweeps, shard_opening_height, shard_goal_patch, shard_patch_place):
    tile_count = lax.axis_size("ground")
    level_count = tile_count // 4
    tables = constants()
    vmem = pl.BlockSpec(memory_space=pltpu.VMEM)
    anyplace = pl.BlockSpec(memory_space=pltpu.HBM)
    dma = pltpu.SemaphoreType.DMA
    filtered = pl.pallas_call(
        fused_kernel,
        out_shape=pltpu.VMEM((2, 64, 64), jnp.float32),
        in_specs=[anyplace] * 9,
        out_specs=vmem,
        scratch_shapes=[
            pltpu.VMEM((512, 2, 512), jnp.bfloat16),
            pltpu.VMEM((3, 1, 64), jnp.int32),
            pltpu.VMEM((4, 1024, 256), jnp.bfloat16),
            pltpu.VMEM((4, 256, 256), jnp.bfloat16),
            pltpu.VMEM((3 * 256, 256), jnp.bfloat16),
            pltpu.VMEM((128, 3 * 64), jnp.bfloat16),
            pltpu.VMEM((128, 3 * 128), jnp.bfloat16),
            pltpu.VMEM((2 * tile_count, 128, 128), jnp.bfloat16),
            pltpu.VMEM((tile_count, 2, 128, 128), jnp.bfloat16),
            pltpu.VMEM((1, 128), jnp.int32),
            pltpu.VMEM((tile_count, 1, 128), jnp.int32),
            pltpu.SMEM((tile_count, 1, 128), jnp.int32),
            pltpu.VMEM((1024, 128), jnp.float32),
            pltpu.VMEM((9 * tile_count * 64, 128), jnp.float32),
            pltpu.VMEM((tile_count * SLOTS, tile_count * 64), jnp.bfloat16),
            pltpu.VMEM((tile_count * SLOTS, 128), jnp.float32),
            pltpu.VMEM((4, tile_count * SLOTS, 256), jnp.float32),
            pltpu.VMEM((tile_count, 2, 128), jnp.float32),
            pltpu.VMEM((2 * tile_count, 2, 128), jnp.float32),
            pltpu.VMEM((4, 128, 1024), jnp.bfloat16),
            dma((8,)),
            dma((4,)),
            dma,
            dma((tile_count,)),
            dma,
            dma,
            dma,
            dma,
            dma,
            pltpu.SemaphoreType.REGULAR((level_count,)),
        ],
        compiler_params=pltpu.CompilerParams(
            collective_id=0, has_side_effects=True, vmem_limit_bytes=CAP_VMEM
        ),
    )(
        coregistered_sweeps[0, 0],
        shard_opening_height.reshape(1, -1),
        shard_goal_patch.reshape(1, -1),
        shard_patch_place.reshape(1, -1),
        *tables,
    )
    return filtered[None, None, None]


def solution(mesh):
    placed = (P("pair", "ground", None, None, None), P("ground"), P("ground", None), P("ground"))
    return jax.shard_map(
        local_pair if dict(mesh.shape) == {"ground": 16, "pair": 2} else local,
        mesh=mesh,
        in_specs=placed,
        out_specs=P("pair", None, "ground", None, None, None),
        check_vma=False,
    )
```

```python
import functools
import math

import jax
import jax.numpy as jnp
import numpy as np
from jax import lax
from jax.experimental import pallas as pl
from jax.experimental.pallas import tpu as pltpu
from jax.sharding import PartitionSpec as P

LOOK_ROWS = 4
LOOK_COLS = 16
SHARD_HEIGHT = 16
TILE_ROWS = 256
TILE_COLS = 1024
SWEEP_WIDTH = 512
PATCH_SHARD_LEVEL = 16
SLOTS = 32


def multilook(reference_tiles, secondary_tiles):
    first = reference_tiles.astype(jnp.float32)
    second = secondary_tiles.astype(jnp.float32)
    real_part = first[..., 0, :] * second[..., 0, :] + first[..., 1, :] * second[..., 1, :]
    imag_part = first[..., 1, :] * second[..., 0, :] - first[..., 0, :] * second[..., 1, :]
    joined = jnp.stack([real_part, imag_part], axis=-3)
    leading = joined.shape[:-2]
    row_count = joined.shape[-2]
    col_count = joined.shape[-1]
    boxes = joined.reshape(
        leading + (row_count // LOOK_ROWS, LOOK_ROWS, col_count // LOOK_COLS, LOOK_COLS)
    )
    return jnp.mean(boxes, axis=(-3, -1))


def on_left(matrix, field):
    return jnp.einsum("ij,...jk->...ik", matrix, field, precision=lax.Precision.HIGHEST)


def on_right(field, matrix):
    return jnp.einsum("...ij,jk->...ik", field, matrix, precision=lax.Precision.HIGHEST)


def goldstein(looked):
    length = looked.shape[-1]
    positions = jnp.arange(length, dtype=jnp.int32)
    phase = positions[:, None] * positions[None, :] % length
    angle = phase.astype(jnp.float32) * (2.0 * math.pi / length)
    cosine = jnp.cos(angle)
    sine = jnp.sin(angle)
    real_in = looked[..., 0, :, :]
    imag_in = looked[..., 1, :, :]
    half_real = on_left(cosine, real_in) + on_left(sine, imag_in)
    half_imag = on_left(cosine, imag_in) - on_left(sine, real_in)
    spec_real = on_right(half_real, cosine) + on_right(half_imag, sine)
    spec_imag = on_right(half_imag, cosine) - on_right(half_real, sine)
    weight = (spec_real * spec_real + spec_imag * spec_imag + 1e-06) ** 0.25
    weight = weight / jnp.mean(weight, axis=(-2, -1), keepdims=True)
    spec_real = spec_real * weight
    spec_imag = spec_imag * weight
    back_real = on_left(cosine, spec_real) - on_left(sine, spec_imag)
    back_imag = on_left(cosine, spec_imag) + on_left(sine, spec_real)
    out_real = on_right(back_real, cosine) - on_right(back_imag, sine)
    out_imag = on_right(back_imag, cosine) + on_right(back_real, sine)
    scale = 1.0 / (length * length)
    return jnp.stack([out_real * scale, out_imag * scale], axis=-3)


def partners_of(index, pair_width):
    order = jnp.arange(pair_width, dtype=jnp.int32)
    return order + (order >= index).astype(jnp.int32)


def local(coregistered_sweeps, shard_opening_height, shard_goal_patch, shard_patch_place):
    earth_patch_total_size = lax.axis_size("ground")
    pair_count = lax.axis_size("pair")
    piece_count = shard_opening_height.shape[0]
    place_allowance = max(
        2, (2 * piece_count + earth_patch_total_size - 1) // earth_patch_total_size
    )
    sweep_resident = coregistered_sweeps[0, 0]
    target = shard_goal_patch[:, 0]
    hits = (target[:, None] == jnp.arange(earth_patch_total_size, dtype=jnp.int32)[None, :]).astype(
        jnp.int32
    )
    order = jnp.arange(piece_count, dtype=jnp.int32)
    before = (order[None, :] < order[:, None]).astype(jnp.bfloat16)
    earlier = jnp.dot(before, hits.astype(jnp.bfloat16), preferred_element_type=jnp.float32).astype(jnp.int32)
    rank = jnp.sum(earlier * hits, axis=1)
    position = target * place_allowance + rank
    matches = (
        position[None, :]
        == jnp.arange(earth_patch_total_size * place_allowance, dtype=jnp.int32)[:, None]
    ).astype(jnp.int32)
    tiles_filled = jnp.sum(matches, axis=1) > 0
    sweep_height_offset = (
        jnp.sum(matches * shard_opening_height[None, :], axis=1)[:, None] + jnp.arange(SHARD_HEIGHT, dtype=jnp.int32)[None, :]
    )
    wanted = jnp.where(tiles_filled[:, None], sweep_height_offset, -1).reshape(-1)
    picked = wanted[:, None] == jnp.arange(sweep_resident.shape[0], dtype=jnp.int32)[None, :]
    pieces_to_send = jnp.dot(
        picked.astype(jnp.bfloat16),
        sweep_resident.reshape(sweep_resident.shape[0], -1),
        preferred_element_type=jnp.float32,
    ).astype(jnp.bfloat16)
    labels = jnp.sum(matches * (shard_patch_place + 1)[None, :], axis=1).astype(jnp.bfloat16)
    received_pieces, arrived_labels = (
        lax.all_to_all(
            pieces_to_send.reshape(
                earth_patch_total_size, place_allowance, SHARD_HEIGHT, 2, SWEEP_WIDTH
            ),
            "ground",
            split_axis=0,
            concat_axis=0,
            tiled=True,
        ),
        lax.all_to_all(
            labels.reshape(earth_patch_total_size, place_allowance),
            "ground",
            split_axis=0,
            concat_axis=0,
            tiled=True,
        ),
    )
    pieces_flattened = received_pieces.reshape(
        earth_patch_total_size * place_allowance, SHARD_HEIGHT * 2 * SWEEP_WIDTH
    )
    slot_labels = (jnp.arange(SLOTS, dtype=jnp.int32) + 1).astype(jnp.bfloat16)
    selector = arrived_labels.reshape(-1)[None, :] == slot_labels[:, None]
    totals = jnp.dot(
        selector.astype(jnp.bfloat16), pieces_flattened, preferred_element_type=jnp.float32
    )
    counts = jnp.sum(selector.astype(jnp.float32), axis=1)
    smoothed_pixel_mean = (totals / jnp.maximum(counts, 1.0)[:, None]).astype(jnp.bfloat16)
    ground_tile = (
        smoothed_pixel_mean.reshape(PATCH_SHARD_LEVEL, 2, SHARD_HEIGHT, 2, SWEEP_WIDTH)
        .transpose(0, 2, 3, 1, 4)
        .reshape(TILE_ROWS, 2, TILE_COLS)
    )
    pair_width = pair_count - 1
    own_refs = partners_of(lax.axis_index("pair"), pair_width)
    piece = lax.all_gather(ground_tile[None], "pair", axis=0, tiled=True)
    looked_piece = multilook(piece, ground_tile[None])
    indices = jnp.arange(piece.shape[0], dtype=jnp.int32)
    selection = (own_refs[:, None] == indices[None, :]).astype(jnp.float32)
    looked = jnp.einsum("kn,nabc->kabc", selection, looked_piece, precision=lax.Precision.HIGHEST)
    return goldstein(looked)[None, :, None]


CAP_VMEM = 58 * 1024 * 1024
MESH = pl.DeviceIdType.MESH
EXACT = lax.Precision.HIGHEST
COLS = 16
LANES = 128


def fused_kernel(
    sweep_hbm, opening_hbm, goal_hbm, place_hbm, part_hbm, widen_hbm, row_dft_hbm, left_hbm, back_hbm,
    out,
    sweep, ints, part, widen, row_dft, left, back_mat, outgoing, arrived, meta_out, meta, tops, rows, gathered,
    chosen, scale, sums, looked_out, looked_in, folded,
    load_sem, part_sem, send_sem, recv_sem, meta_send, meta_recv, top_sem, look_send, look_recv, gate,
):
    me = lax.axis_index("ground")
    mine = lax.axis_index("pair")
    tile_count = meta.shape[0]
    piece_count = ints.shape[2]
    device_count = 2 * tile_count
    level_count = tile_count // 4
    level = me // 4
    spot = lax.rem(me, 4)
    self_id = me * 2 + mine
    barrier = pltpu.get_barrier_semaphore()

    loads = [
        pltpu.make_async_copy(source, sink, load_sem.at[at])
        for at, (source, sink) in enumerate(
            [
                (sweep_hbm, sweep),
                (opening_hbm, ints.at[0]),
                (goal_hbm, ints.at[1]),
                (place_hbm, ints.at[2]),
                (widen_hbm, widen),
                (row_dft_hbm, row_dft),
                (left_hbm, left),
                (back_hbm, back_mat),
            ]
        )
    ]

    def spot_of(step):
        return lax.rem(spot // 2 + step // 2, 2) * 2 + lax.rem(spot + step, 2)

    parts = [
        pltpu.make_async_copy(part_hbm.at[spot_of(step)], part.at[step], part_sem.at[step]) for step in range(4)
    ]

    above = device_count - 8 * level

    def greet(step, carry):
        number = 8 * level + lax.rem(self_id - 8 * level + step, above)
        pl.semaphore_signal(
            barrier, inc=1, device_id={"ground": number // 2, "pair": lax.rem(number, 2)}, device_id_type=MESH
        )
        return carry

    lax.fori_loop(1, above, greet, 0)
    for copy in [loads[0], parts[0]] + loads[1:4] + parts[1:] + loads[4:]:
        copy.start()
    pl.semaphore_wait(barrier, 8 * level + 7)
    for plane in range(level_count - 1):

        @pl.when(plane < level)
        def _():
            pl.semaphore_signal(
                gate.at[level], inc=1, device_id={"ground": plane * 4 + spot, "pair": mine}, device_id_type=MESH
            )

    def block(step, plane, other):
        return pltpu.make_async_remote_copy(
            src_ref=outgoing.at[(step * 2 + other) * level_count + plane],
            dst_ref=arrived.at[me, mine],
            send_sem=send_sem,
            recv_sem=recv_sem.at[me],
            device_id={"ground": plane * 4 + spot_of(step), "pair": other},
            device_id_type=MESH,
        )

    def label(target):
        return pltpu.make_async_remote_copy(
            src_ref=meta_out,
            dst_ref=meta.at[me],
            send_sem=meta_send,
            recv_sem=meta_recv,
            device_id={"ground": target, "pair": mine},
            device_id_type=MESH,
        )

    def labels(plane):
        for step in range(4):
            label(plane * 4 + spot_of(step)).start()

    for copy in loads[1:4]:
        copy.wait()
    meta_out[...] = jnp.concatenate([ints[0] * 2, ints[1] * SLOTS + ints[2]], axis=1)
    meta[me] = meta_out[...]
    loads[0].wait()

    for step in range(4):
        parts[step].wait()
        for at in range(level_count):
            if step == 0:
                for row in range(8):
                    folded[at, :, row * LANES:(row + 1) * LANES] = sweep[
                        row * 64:(row + 1) * 64, :, at * LANES:(at + 1) * LANES
                    ].reshape(LANES, LANES)
            moved = jnp.dot(folded[at], part[step], preferred_element_type=jnp.float32).astype(jnp.bfloat16)
            outgoing[step * 2 * level_count + at] = moved[:, :LANES]
            outgoing[(step * 2 + 1) * level_count + at] = moved[:, LANES:]
        for plane in range(level_count - 1):

            @pl.when(plane < level)
            def _():
                if step == 0:
                    labels(plane)
                for other in range(2):
                    block(step, plane, other).start()

        if step == 0:
            for turn in range(1, 4):
                label(level * 4 + spot_of(turn)).start()
            block(step, level, 1 - mine).start()
            arrived[me, mine] = outgoing[mine * level_count + level]
        else:
            for other in range(2):
                block(step, level, other).start()
        for plane in (1, 3, 2):

            @pl.when(plane > level)
            def _():
                opening_step = 0 if plane < level_count - 1 else 1
                if step == opening_step:
                    pl.semaphore_wait(gate.at[plane], 1)
                    labels(plane)
                if step >= opening_step:
                    for turn in range(0 if step == opening_step else step, step + 1):
                        for other in range(2):
                            block(turn, plane, other).start()

    pltpu.make_async_remote_copy(
        src_ref=meta.at[pl.ds(0, tile_count - 1)],
        dst_ref=meta.at[pl.ds(0, tile_count - 1)],
        send_sem=meta_send,
        recv_sem=meta_recv,
        device_id={"ground": me, "pair": 1 - mine},
        device_id_type=MESH,
    ).wait()
    to_scalars = pltpu.make_async_copy(meta, tops, top_sem)
    to_scalars.start()
    for copy in loads[4:]:
        copy.wait()

    near = level + 1 - 2 * lax.rem(level, 2)
    cross = 2 - 2 * (level // 2)
    order = [(plane, step) for step in range(4) for plane in (level, near, 3 - 3 * (level // 2), 2 - level // 2)]
    sources = [plane * 4 + spot_of(step) for plane, step in order]

    lane1 = lax.broadcasted_iota(jnp.int32, (1, LANES), 1)
    width = tile_count * piece_count
    for at in range(tile_count // 2):
        keys = jnp.where(lane1 < 64, pltpu.roll(meta[sources[2 * at]], 64, 1), meta[sources[2 * at + 1]])
        slots = lax.broadcasted_iota(jnp.int32, (tile_count * SLOTS, LANES), 0)
        chosen[:, at * LANES:(at + 1) * LANES] = jnp.where(slots == keys, 1.0, 0.0).astype(jnp.bfloat16)
    count = jnp.dot(chosen[...], jnp.ones((width, LANES), jnp.bfloat16), preferred_element_type=jnp.float32)
    scale[...] = 1.0 / jnp.maximum(count, 1.0)
    to_scalars.wait()

    lane8 = lax.broadcasted_iota(jnp.int32, (8, LANES), 1)
    cuts = (8, 12)
    early = cuts[-1] * piece_count

    def columns(pair_row, first, last):
        return jnp.concatenate(
            [gathered[(2 * pair_row + part) * width + first:(2 * pair_row + part) * width + last] for part in range(2)],
            axis=1,
        ).astype(jnp.bfloat16)

    for position, source in enumerate(sources):
        if position == 0:
            pltpu.make_async_remote_copy(
                src_ref=outgoing.at[0],
                dst_ref=arrived.at[me, 1 - mine],
                send_sem=send_sem,
                recv_sem=recv_sem.at[me],
                device_id={"ground": me, "pair": 1 - mine},
                device_id_type=MESH,
            ).wait_recv()
        else:
            pltpu.make_async_remote_copy(
                src_ref=arrived.at[source],
                dst_ref=arrived.at[source],
                send_sem=send_sem,
                recv_sem=recv_sem.at[source],
                device_id={"ground": source, "pair": mine},
                device_id_type=MESH,
            ).wait_recv()
        both = jnp.concatenate([arrived[source, 0], arrived[source, 1]], axis=1)
        for quarter in range(4):
            spread = jnp.dot(both, widen[quarter], preferred_element_type=jnp.float32)
            rows[quarter * 256:quarter * 256 + LANES] = spread[:, :LANES]
            rows[quarter * 256 + LANES:quarter * 256 + 256] = spread[:, LANES:]

        for piece in range(piece_count):
            top = tops[source, 0, piece]
            value = rows[pl.ds(top, 8), :]
            for shift in range(1, 4):
                value = jnp.where(lane8 < shift * 32, value, rows[pl.ds(top + 8 * shift, 8), :])
            gathered[pl.ds(position * piece_count + piece, 8, stride=width), :] = value
        if position + 1 in cuts:
            last = (position + 1) * piece_count
            first = 0 if position + 1 == cuts[0] else cuts[cuts.index(position + 1) - 1] * piece_count
            for pair_row in range(4):
                part_sum = jnp.dot(
                    chosen[:, first:last], columns(pair_row, first, last), preferred_element_type=jnp.float32
                )
                sums[pair_row] = part_sum if first == 0 else sums[pair_row] + part_sum

    same = jnp.zeros((tile_count * SLOTS, LANES), jnp.float32)
    crossed = same
    for pair_row in range(4):
        total = sums[pair_row] + jnp.dot(
            chosen[:, early:], columns(pair_row, early, width), preferred_element_type=jnp.float32
        )
        real = (total[:, :LANES] * scale[...]).astype(jnp.bfloat16).astype(jnp.float32)
        imag = (total[:, LANES:] * scale[...]).astype(jnp.bfloat16).astype(jnp.float32)
        real_other = pltpu.roll(real, LANES - COLS, 1)
        imag_other = pltpu.roll(imag, LANES - COLS, 1)
        same = same + real * real_other + imag * imag_other
        crossed = crossed + imag_other * real - real_other * imag
    lane = lax.broadcasted_iota(jnp.int32, same.shape, 1)
    merged = jnp.where(lane % 32 < COLS, same, pltpu.roll(crossed, COLS, 1))
    high = merged.astype(jnp.bfloat16)
    low = (merged - high.astype(jnp.float32)).astype(jnp.bfloat16)
    row8 = lax.broadcasted_iota(jnp.int32, (8, LANES), 0)
    pool = jnp.where(lane8 // COLS == (row8 % 4) * 2 + row8 // 4, 1.0 / (LOOK_ROWS * LOOK_COLS), 0.0)
    pool = pool.astype(jnp.bfloat16)
    pooled = lax.dot_general(
        jnp.concatenate([pool, pool], axis=1),
        jnp.concatenate([high, low], axis=1),
        (((1,), (1,)), ((), ())),
        preferred_element_type=jnp.float32,
    )
    for group in range(tile_count // 4):
        piece = pooled[:, group * LANES:(group + 1) * LANES]
        turned = piece
        for shift in range(1, 4):
            moved = pltpu.roll(pltpu.roll(piece, LANES - 32 * shift, 1), 2 * shift, 0)
            turned = jnp.where((row8 // 2 - lane8 // 32 + 4) % 4 == shift, moved, turned)
        for inner in range(4):
            looked_out[group * 4 + inner] = turned[2 * inner:2 * inner + 2]

    away = level // 2
    for plane in (3 - 3 * away, 2 - away, near, level):
        for step in (3, 2, 1, 0):
            target = plane * 4 + spot_of(step)
            for other in (1 - mine, mine):
                if plane is level and step == 0 and other is mine:
                    continue
                pltpu.make_async_remote_copy(
                    src_ref=looked_out.at[target],
                    dst_ref=looked_in.at[self_id],
                    send_sem=look_send,
                    recv_sem=look_recv,
                    device_id={"ground": target, "pair": other},
                    device_id_type=MESH,
                ).start()
    looked_in[self_id] = looked_out[me]
    pltpu.make_async_remote_copy(
        src_ref=outgoing.at[pl.ds(0, device_count - 1)],
        dst_ref=outgoing.at[pl.ds(0, device_count - 1)],
        send_sem=send_sem,
        recv_sem=recv_sem.at[0],
        device_id={"ground": me, "pair": 1 - mine},
        device_id_type=MESH,
    ).wait_send()
    pltpu.make_async_remote_copy(
        src_ref=looked_in.at[pl.ds(0, device_count - 1)],
        dst_ref=looked_in.at[pl.ds(0, device_count - 1)],
        send_sem=look_send,
        recv_sem=look_recv,
        device_id={"ground": me, "pair": 1 - mine},
        device_id_type=MESH,
    ).wait()

    def split(value):
        first = value.astype(jnp.bfloat16)
        return first, (value - first.astype(jnp.float32)).astype(jnp.bfloat16)

    flip = 1.0 - 2.0 * mine.astype(jnp.float32)
    lanes = lax.broadcasted_iota(jnp.int32, (device_count, LANES), 1)
    sign = jnp.where(lanes < 64, 1.0, flip)
    field = jnp.concatenate([looked_in[:, 0, :] * sign, looked_in[:, 1, :] * sign], axis=1)
    first, second = split(field)
    field = jnp.dot(
        jnp.concatenate([first, second, first], axis=1), row_dft[...], preferred_element_type=jnp.float32
    )
    field = jnp.concatenate([field[:, :LANES], field[:, LANES:]], axis=0)
    length = out.shape[1]
    turn = jnp.where(lax.broadcasted_iota(jnp.int32, (length, 2 * length), 1) < length, 1.0, -1.0)
    first, second = split(field)
    both = jnp.dot(
        left[...], jnp.concatenate([first, second, first], axis=0), preferred_element_type=jnp.float32
    )
    spectrum = both[:length] + turn * pltpu.roll(both[length:], length, 1)
    power = spectrum * spectrum
    power = power + pltpu.roll(power, length, 1)
    weight = jnp.sqrt(jnp.sqrt(power + 1e-06))
    mean = jnp.sum(weight) * (1.0 / (2 * length * length))
    spectrum = spectrum * (weight / mean)
    first, second = split(spectrum)
    both = jnp.dot(
        left[...], jnp.concatenate([first, second, first], axis=0), preferred_element_type=jnp.float32
    )
    back = both[:length] - turn * pltpu.roll(both[length:], length, 1)
    first, second = split(back)
    result = lax.dot_general(
        back_mat[...],
        jnp.concatenate([first, second, first], axis=1),
        (((1,), (1,)), ((), ())),
        preferred_element_type=jnp.float32,
    ) * (1.0 / (length * length))
    out[0] = result[:length]
    out[1] = result[length:]


def constants():
    row = np.arange(1024)
    col = np.arange(256)
    lane, group = row % 128, row // 128
    part = np.stack(
        [
            (lane[:, None] // 32 == spot)
            & (col[None, :] // 128 == lane[:, None] // 16 % 2)
            & (col[None, :] % 128 // 16 == group[:, None])
            & (col[None, :] % 16 == lane[:, None] % 16)
            for spot in range(4)
        ]
    ).astype(jnp.bfloat16)
    row = np.arange(256)
    widen = np.stack(
        [
            (row[:, None] // 128 == col[None, :] // 16 % 2)
            & (row[:, None] % 128 // 16 == 2 * quarter + col[None, :] // 128)
            & (row[:, None] % 16 == col[None, :] % 16)
            for quarter in range(4)
        ]
    ).astype(jnp.bfloat16)
    low, high, slot = row // 128, row % 128 // 32, row % 32
    kind, box = (2 * high + low) // 4, (2 * high + low) % 4
    line = slot // 2 * 4 + box
    out_side, out_kind, frequency = col // 128, col // 64 % 2, col % 64
    angle = (line[:, None] * frequency[None, :] % 64) * (2.0 * math.pi / 64)
    mixed = np.where(
        kind[:, None] == out_kind[None, :],
        np.cos(angle),
        np.where(kind[:, None] == 0, -np.sin(angle), np.sin(angle)),
    )
    row_dft = np.where(slot[:, None] % 2 == out_side[None, :], mixed, 0.0)
    column = np.arange(64)
    angle = (column[:, None] * column[None, :] % 64) * (2.0 * math.pi / 64)
    cosine, sine = np.cos(angle), np.sin(angle)
    left = np.concatenate([cosine, sine], 0)
    back = np.block([[cosine, -sine], [sine, cosine]])

    def parts_of(value, axis):
        first = value.astype(np.float32).astype(jnp.bfloat16)
        second = (value - first.astype(np.float64)).astype(np.float32).astype(jnp.bfloat16)
        return np.concatenate([first, first, second], axis)

    return part, widen, parts_of(row_dft, 0), parts_of(left, 1), parts_of(back, 1)


def local_pair(coregistered_sweeps, shard_opening_height, shard_goal_patch, shard_patch_place):
    tile_count = lax.axis_size("ground")
    level_count = tile_count // 4
    tables = constants()
    vmem = pl.BlockSpec(memory_space=pltpu.VMEM)
    anyplace = pl.BlockSpec(memory_space=pltpu.HBM)
    dma = pltpu.SemaphoreType.DMA
    filtered = pl.pallas_call(
        fused_kernel,
        out_shape=pltpu.VMEM((2, 64, 64), jnp.float32),
        in_specs=[anyplace] * 9,
        out_specs=vmem,
        scratch_shapes=[
            pltpu.VMEM((512, 2, 512), jnp.bfloat16),
            pltpu.VMEM((3, 1, 64), jnp.int32),
            pltpu.VMEM((4, 1024, 256), jnp.bfloat16),
            pltpu.VMEM((4, 256, 256), jnp.bfloat16),
            pltpu.VMEM((3 * 256, 256), jnp.bfloat16),
            pltpu.VMEM((128, 3 * 64), jnp.bfloat16),
            pltpu.VMEM((128, 3 * 128), jnp.bfloat16),
            pltpu.VMEM((2 * tile_count, 128, 128), jnp.bfloat16),
            pltpu.VMEM((tile_count, 2, 128, 128), jnp.bfloat16),
            pltpu.VMEM((1, 128), jnp.int32),
            pltpu.VMEM((tile_count, 1, 128), jnp.int32),
            pltpu.SMEM((tile_count, 1, 128), jnp.int32),
            pltpu.VMEM((1024, 128), jnp.float32),
            pltpu.VMEM((9 * tile_count * 64, 128), jnp.float32),
            pltpu.VMEM((tile_count * SLOTS, tile_count * 64), jnp.bfloat16),
            pltpu.VMEM((tile_count * SLOTS, 128), jnp.float32),
            pltpu.VMEM((4, tile_count * SLOTS, 256), jnp.float32),
            pltpu.VMEM((tile_count, 2, 128), jnp.float32),
            pltpu.VMEM((2 * tile_count, 2, 128), jnp.float32),
            pltpu.VMEM((4, 128, 1024), jnp.bfloat16),
            dma((8,)),
            dma((4,)),
            dma,
            dma((tile_count,)),
            dma,
            dma,
            dma,
            dma,
            dma,
            pltpu.SemaphoreType.REGULAR((level_count,)),
        ],
        compiler_params=pltpu.CompilerParams(
            collective_id=0, has_side_effects=True, vmem_limit_bytes=CAP_VMEM
        ),
    )(
        coregistered_sweeps[0, 0],
        shard_opening_height.reshape(1, -1),
        shard_goal_patch.reshape(1, -1),
        shard_patch_place.reshape(1, -1),
        *tables,
    )
    return filtered[None, None, None]


def solution(mesh):
    placed = (P("pair", "ground", None, None, None), P("ground"), P("ground", None), P("ground"))
    return jax.shard_map(
        local_pair if dict(mesh.shape) == {"ground": 16, "pair": 2} else local,
        mesh=mesh,
        in_specs=placed,
        out_specs=P("pair", None, "ground", None, None, None),
        check_vma=False,
    )
```

```python
import functools
import math

import jax
import jax.numpy as jnp
import numpy as np
from jax import lax
from jax.experimental import pallas as pl
from jax.experimental.pallas import tpu as pltpu
from jax.sharding import PartitionSpec as P

LOOK_ROWS = 4
LOOK_COLS = 16
SHARD_HEIGHT = 16
TILE_ROWS = 256
TILE_COLS = 1024
SWEEP_WIDTH = 512
PATCH_SHARD_LEVEL = 16
SLOTS = 32


def multilook(reference_tiles, secondary_tiles):
    first = reference_tiles.astype(jnp.float32)
    second = secondary_tiles.astype(jnp.float32)
    real_part = first[..., 0, :] * second[..., 0, :] + first[..., 1, :] * second[..., 1, :]
    imag_part = first[..., 1, :] * second[..., 0, :] - first[..., 0, :] * second[..., 1, :]
    joined = jnp.stack([real_part, imag_part], axis=-3)
    leading = joined.shape[:-2]
    row_count = joined.shape[-2]
    col_count = joined.shape[-1]
    boxes = joined.reshape(
        leading + (row_count // LOOK_ROWS, LOOK_ROWS, col_count // LOOK_COLS, LOOK_COLS)
    )
    return jnp.mean(boxes, axis=(-3, -1))


def on_left(matrix, field):
    return jnp.einsum("ij,...jk->...ik", matrix, field, precision=lax.Precision.HIGHEST)


def on_right(field, matrix):
    return jnp.einsum("...ij,jk->...ik", field, matrix, precision=lax.Precision.HIGHEST)


def goldstein(looked):
    length = looked.shape[-1]
    positions = jnp.arange(length, dtype=jnp.int32)
    phase = positions[:, None] * positions[None, :] % length
    angle = phase.astype(jnp.float32) * (2.0 * math.pi / length)
    cosine = jnp.cos(angle)
    sine = jnp.sin(angle)
    real_in = looked[..., 0, :, :]
    imag_in = looked[..., 1, :, :]
    half_real = on_left(cosine, real_in) + on_left(sine, imag_in)
    half_imag = on_left(cosine, imag_in) - on_left(sine, real_in)
    spec_real = on_right(half_real, cosine) + on_right(half_imag, sine)
    spec_imag = on_right(half_imag, cosine) - on_right(half_real, sine)
    weight = (spec_real * spec_real + spec_imag * spec_imag + 1e-06) ** 0.25
    weight = weight / jnp.mean(weight, axis=(-2, -1), keepdims=True)
    spec_real = spec_real * weight
    spec_imag = spec_imag * weight
    back_real = on_left(cosine, spec_real) - on_left(sine, spec_imag)
    back_imag = on_left(cosine, spec_imag) + on_left(sine, spec_real)
    out_real = on_right(back_real, cosine) - on_right(back_imag, sine)
    out_imag = on_right(back_imag, cosine) + on_right(back_real, sine)
    scale = 1.0 / (length * length)
    return jnp.stack([out_real * scale, out_imag * scale], axis=-3)


def partners_of(index, pair_width):
    order = jnp.arange(pair_width, dtype=jnp.int32)
    return order + (order >= index).astype(jnp.int32)


def local(coregistered_sweeps, shard_opening_height, shard_goal_patch, shard_patch_place):
    earth_patch_total_size = lax.axis_size("ground")
    pair_count = lax.axis_size("pair")
    piece_count = shard_opening_height.shape[0]
    place_allowance = max(
        2, (2 * piece_count + earth_patch_total_size - 1) // earth_patch_total_size
    )
    sweep_resident = coregistered_sweeps[0, 0]
    target = shard_goal_patch[:, 0]
    hits = (target[:, None] == jnp.arange(earth_patch_total_size, dtype=jnp.int32)[None, :]).astype(
        jnp.int32
    )
    order = jnp.arange(piece_count, dtype=jnp.int32)
    before = (order[None, :] < order[:, None]).astype(jnp.bfloat16)
    earlier = jnp.dot(before, hits.astype(jnp.bfloat16), preferred_element_type=jnp.float32).astype(jnp.int32)
    rank = jnp.sum(earlier * hits, axis=1)
    position = target * place_allowance + rank
    matches = (
        position[None, :]
        == jnp.arange(earth_patch_total_size * place_allowance, dtype=jnp.int32)[:, None]
    ).astype(jnp.int32)
    tiles_filled = jnp.sum(matches, axis=1) > 0
    sweep_height_offset = (
        jnp.sum(matches * shard_opening_height[None, :], axis=1)[:, None] + jnp.arange(SHARD_HEIGHT, dtype=jnp.int32)[None, :]
    )
    wanted = jnp.where(tiles_filled[:, None], sweep_height_offset, -1).reshape(-1)
    picked = wanted[:, None] == jnp.arange(sweep_resident.shape[0], dtype=jnp.int32)[None, :]
    pieces_to_send = jnp.dot(
        picked.astype(jnp.bfloat16),
        sweep_resident.reshape(sweep_resident.shape[0], -1),
        preferred_element_type=jnp.float32,
    ).astype(jnp.bfloat16)
    labels = jnp.sum(matches * (shard_patch_place + 1)[None, :], axis=1).astype(jnp.bfloat16)
    received_pieces, arrived_labels = (
        lax.all_to_all(
            pieces_to_send.reshape(
                earth_patch_total_size, place_allowance, SHARD_HEIGHT, 2, SWEEP_WIDTH
            ),
            "ground",
            split_axis=0,
            concat_axis=0,
            tiled=True,
        ),
        lax.all_to_all(
            labels.reshape(earth_patch_total_size, place_allowance),
            "ground",
            split_axis=0,
            concat_axis=0,
            tiled=True,
        ),
    )
    pieces_flattened = received_pieces.reshape(
        earth_patch_total_size * place_allowance, SHARD_HEIGHT * 2 * SWEEP_WIDTH
    )
    slot_labels = (jnp.arange(SLOTS, dtype=jnp.int32) + 1).astype(jnp.bfloat16)
    selector = arrived_labels.reshape(-1)[None, :] == slot_labels[:, None]
    totals = jnp.dot(
        selector.astype(jnp.bfloat16), pieces_flattened, preferred_element_type=jnp.float32
    )
    counts = jnp.sum(selector.astype(jnp.float32), axis=1)
    smoothed_pixel_mean = (totals / jnp.maximum(counts, 1.0)[:, None]).astype(jnp.bfloat16)
    ground_tile = (
        smoothed_pixel_mean.reshape(PATCH_SHARD_LEVEL, 2, SHARD_HEIGHT, 2, SWEEP_WIDTH)
        .transpose(0, 2, 3, 1, 4)
        .reshape(TILE_ROWS, 2, TILE_COLS)
    )
    pair_width = pair_count - 1
    own_refs = partners_of(lax.axis_index("pair"), pair_width)
    piece = lax.all_gather(ground_tile[None], "pair", axis=0, tiled=True)
    looked_piece = multilook(piece, ground_tile[None])
    indices = jnp.arange(piece.shape[0], dtype=jnp.int32)
    selection = (own_refs[:, None] == indices[None, :]).astype(jnp.float32)
    looked = jnp.einsum("kn,nabc->kabc", selection, looked_piece, precision=lax.Precision.HIGHEST)
    return goldstein(looked)[None, :, None]


CAP_VMEM = 58 * 1024 * 1024
MESH = pl.DeviceIdType.MESH
EXACT = lax.Precision.HIGHEST
COLS = 16
LANES = 128


def fused_kernel(
    sweep_hbm, opening_hbm, goal_hbm, place_hbm, part_hbm, widen_hbm, row_dft_hbm, left_hbm, back_hbm,
    out,
    sweep, ints, part, widen, row_dft, left, back_mat, outgoing, arrived, meta_out, meta, tops, rows, gathered,
    chosen, scale, sums, looked_out, looked_in, folded,
    load_sem, part_sem, send_sem, recv_sem, meta_send, meta_recv, top_sem, look_send, look_recv, gate,
):
    me = lax.axis_index("ground")
    mine = lax.axis_index("pair")
    tile_count = meta.shape[0]
    piece_count = ints.shape[2]
    device_count = 2 * tile_count
    level_count = tile_count // 4
    level = me // 4
    spot = lax.rem(me, 4)
    self_id = me * 2 + mine
    barrier = pltpu.get_barrier_semaphore()

    loads = [
        pltpu.make_async_copy(source, sink, load_sem.at[at])
        for at, (source, sink) in enumerate(
            [
                (sweep_hbm, sweep),
                (opening_hbm, ints.at[0]),
                (goal_hbm, ints.at[1]),
                (place_hbm, ints.at[2]),
                (widen_hbm, widen),
                (row_dft_hbm, row_dft),
                (left_hbm, left),
                (back_hbm, back_mat),
            ]
        )
    ]

    def spot_of(step):
        return lax.rem(spot // 2 + step // 2, 2) * 2 + lax.rem(spot + step, 2)

    parts = [
        pltpu.make_async_copy(part_hbm.at[spot_of(step)], part.at[step], part_sem.at[step]) for step in range(4)
    ]

    above = device_count - 8 * level

    def greet(step, carry):
        number = 8 * level + jnp.where(step < 8, lax.rem(self_id - 8 * level + step, 8), step)
        pl.semaphore_signal(
            barrier, inc=1, device_id={"ground": number // 2, "pair": lax.rem(number, 2)}, device_id_type=MESH
        )
        return carry

    lax.fori_loop(1, above, greet, 0)
    for copy in [loads[0], parts[0]] + loads[1:4] + parts[1:] + loads[4:]:
        copy.start()
    pl.semaphore_wait(barrier, 8 * level + 7)
    for plane in range(level_count - 1):

        @pl.when(plane < level)
        def _():
            pl.semaphore_signal(
                gate.at[level], inc=1, device_id={"ground": plane * 4 + spot, "pair": mine}, device_id_type=MESH
            )

    def block(step, plane, other):
        return pltpu.make_async_remote_copy(
            src_ref=outgoing.at[(step * 2 + other) * level_count + plane],
            dst_ref=arrived.at[me, mine],
            send_sem=send_sem,
            recv_sem=recv_sem.at[me],
            device_id={"ground": plane * 4 + spot_of(step), "pair": other},
            device_id_type=MESH,
        )

    def label(target):
        return pltpu.make_async_remote_copy(
            src_ref=meta_out,
            dst_ref=meta.at[me],
            send_sem=meta_send,
            recv_sem=meta_recv,
            device_id={"ground": target, "pair": mine},
            device_id_type=MESH,
        )

    def labels(plane):
        for step in range(4):
            label(plane * 4 + spot_of(step)).start()

    for copy in loads[1:4]:
        copy.wait()
    meta_out[...] = jnp.concatenate([ints[0] * 2, ints[1] * SLOTS + ints[2]], axis=1)
    meta[me] = meta_out[...]
    loads[0].wait()

    for step in range(4):
        parts[step].wait()
        for at in range(level_count):
            if step == 0:
                for row in range(8):
                    folded[at, :, row * LANES:(row + 1) * LANES] = sweep[
                        row * 64:(row + 1) * 64, :, at * LANES:(at + 1) * LANES
                    ].reshape(LANES, LANES)
            moved = jnp.dot(folded[at], part[step], preferred_element_type=jnp.float32).astype(jnp.bfloat16)
            outgoing[step * 2 * level_count + at] = moved[:, :LANES]
            outgoing[(step * 2 + 1) * level_count + at] = moved[:, LANES:]
        for plane in range(level_count - 1):

            @pl.when(plane < level)
            def _():
                if step == 0:
                    labels(plane)
                for other in range(2):
                    block(step, plane, other).start()

        if step == 0:
            for turn in range(1, 4):
                label(level * 4 + spot_of(turn)).start()
            block(step, level, 1 - mine).start()
            arrived[me, mine] = outgoing[mine * level_count + level]
        else:
            for other in range(2):
                block(step, level, other).start()
        for plane in (1, 3, 2):

            @pl.when(plane > level)
            def _():
                opening_step = 0 if plane < level_count - 1 else 1
                if step == opening_step:
                    pl.semaphore_wait(gate.at[plane], 1)
                    labels(plane)
                if step >= opening_step:
                    for turn in range(0 if step == opening_step else step, step + 1):
                        for other in range(2):
                            block(turn, plane, other).start()

    pltpu.make_async_remote_copy(
        src_ref=meta.at[pl.ds(0, tile_count - 1)],
        dst_ref=meta.at[pl.ds(0, tile_count - 1)],
        send_sem=meta_send,
        recv_sem=meta_recv,
        device_id={"ground": me, "pair": 1 - mine},
        device_id_type=MESH,
    ).wait()
    to_scalars = pltpu.make_async_copy(meta, tops, top_sem)
    to_scalars.start()
    for copy in loads[4:]:
        copy.wait()

    near = level + 1 - 2 * lax.rem(level, 2)
    cross = 2 - 2 * (level // 2)
    order = [(plane, step) for step in range(4) for plane in (level, near, 3 - 3 * (level // 2), 2 - level // 2)]
    sources = [plane * 4 + spot_of(step) for plane, step in order]

    lane1 = lax.broadcasted_iota(jnp.int32, (1, LANES), 1)
    width = tile_count * piece_count
    for at in range(tile_count // 2):
        keys = jnp.where(lane1 < 64, pltpu.roll(meta[sources[2 * at]], 64, 1), meta[sources[2 * at + 1]])
        slots = lax.broadcasted_iota(jnp.int32, (tile_count * SLOTS, LANES), 0)
        chosen[:, at * LANES:(at + 1) * LANES] = jnp.where(slots == keys, 1.0, 0.0).astype(jnp.bfloat16)
    count = jnp.dot(chosen[...], jnp.ones((width, LANES), jnp.bfloat16), preferred_element_type=jnp.float32)
    scale[...] = 1.0 / jnp.maximum(count, 1.0)
    to_scalars.wait()

    lane8 = lax.broadcasted_iota(jnp.int32, (8, LANES), 1)
    cuts = (8, 12)
    early = cuts[-1] * piece_count

    def columns(pair_row, first, last):
        return jnp.concatenate(
            [gathered[(2 * pair_row + part) * width + first:(2 * pair_row + part) * width + last] for part in range(2)],
            axis=1,
        ).astype(jnp.bfloat16)

    for position, source in enumerate(sources):
        if position == 0:
            pltpu.make_async_remote_copy(
                src_ref=outgoing.at[0],
                dst_ref=arrived.at[me, 1 - mine],
                send_sem=send_sem,
                recv_sem=recv_sem.at[me],
                device_id={"ground": me, "pair": 1 - mine},
                device_id_type=MESH,
            ).wait_recv()
        else:
            pltpu.make_async_remote_copy(
                src_ref=arrived.at[source],
                dst_ref=arrived.at[source],
                send_sem=send_sem,
                recv_sem=recv_sem.at[source],
                device_id={"ground": source, "pair": mine},
                device_id_type=MESH,
            ).wait_recv()
        both = jnp.concatenate([arrived[source, 0], arrived[source, 1]], axis=1)
        for quarter in range(4):
            spread = jnp.dot(both, widen[quarter], preferred_element_type=jnp.float32)
            rows[quarter * 256:quarter * 256 + LANES] = spread[:, :LANES]
            rows[quarter * 256 + LANES:quarter * 256 + 256] = spread[:, LANES:]

        for piece in range(piece_count):
            top = tops[source, 0, piece]
            value = rows[pl.ds(top, 8), :]
            for shift in range(1, 4):
                value = jnp.where(lane8 < shift * 32, value, rows[pl.ds(top + 8 * shift, 8), :])
            gathered[pl.ds(position * piece_count + piece, 8, stride=width), :] = value
        if position + 1 in cuts:
            last = (position + 1) * piece_count
            first = 0 if position + 1 == cuts[0] else cuts[cuts.index(position + 1) - 1] * piece_count
            for pair_row in range(4):
                part_sum = jnp.dot(
                    chosen[:, first:last], columns(pair_row, first, last), preferred_element_type=jnp.float32
                )
                sums[pair_row] = part_sum if first == 0 else sums[pair_row] + part_sum

    same = jnp.zeros((tile_count * SLOTS, LANES), jnp.float32)
    crossed = same
    for pair_row in range(4):
        total = sums[pair_row] + jnp.dot(
            chosen[:, early:], columns(pair_row, early, width), preferred_element_type=jnp.float32
        )
        real = (total[:, :LANES] * scale[...]).astype(jnp.bfloat16).astype(jnp.float32)
        imag = (total[:, LANES:] * scale[...]).astype(jnp.bfloat16).astype(jnp.float32)
        real_other = pltpu.roll(real, LANES - COLS, 1)
        imag_other = pltpu.roll(imag, LANES - COLS, 1)
        same = same + real * real_other + imag * imag_other
        crossed = crossed + imag_other * real - real_other * imag
    lane = lax.broadcasted_iota(jnp.int32, same.shape, 1)
    merged = jnp.where(lane % 32 < COLS, same, pltpu.roll(crossed, COLS, 1))
    high = merged.astype(jnp.bfloat16)
    low = (merged - high.astype(jnp.float32)).astype(jnp.bfloat16)
    row8 = lax.broadcasted_iota(jnp.int32, (8, LANES), 0)
    pool = jnp.where(lane8 // COLS == (row8 % 4) * 2 + row8 // 4, 1.0 / (LOOK_ROWS * LOOK_COLS), 0.0)
    pool = pool.astype(jnp.bfloat16)
    pooled = lax.dot_general(
        jnp.concatenate([pool, pool], axis=1),
        jnp.concatenate([high, low], axis=1),
        (((1,), (1,)), ((), ())),
        preferred_element_type=jnp.float32,
    )
    for group in range(tile_count // 4):
        piece = pooled[:, group * LANES:(group + 1) * LANES]
        turned = piece
        for shift in range(1, 4):
            moved = pltpu.roll(pltpu.roll(piece, LANES - 32 * shift, 1), 2 * shift, 0)
            turned = jnp.where((row8 // 2 - lane8 // 32 + 4) % 4 == shift, moved, turned)
        for inner in range(4):
            looked_out[group * 4 + inner] = turned[2 * inner:2 * inner + 2]

    away = level // 2
    for plane in (3 - 3 * away, 2 - away, near, level):
        for step in (3, 2, 1, 0):
            target = plane * 4 + spot_of(step)
            for other in (1 - mine, mine):
                if plane is level and step == 0 and other is mine:
                    continue
                pltpu.make_async_remote_copy(
                    src_ref=looked_out.at[target],
                    dst_ref=looked_in.at[self_id],
                    send_sem=look_send,
                    recv_sem=look_recv,
                    device_id={"ground": target, "pair": other},
                    device_id_type=MESH,
                ).start()
    looked_in[self_id] = looked_out[me]
    pltpu.make_async_remote_copy(
        src_ref=outgoing.at[pl.ds(0, device_count - 1)],
        dst_ref=outgoing.at[pl.ds(0, device_count - 1)],
        send_sem=send_sem,
        recv_sem=recv_sem.at[0],
        device_id={"ground": me, "pair": 1 - mine},
        device_id_type=MESH,
    ).wait_send()
    pltpu.make_async_remote_copy(
        src_ref=looked_in.at[pl.ds(0, device_count - 1)],
        dst_ref=looked_in.at[pl.ds(0, device_count - 1)],
        send_sem=look_send,
        recv_sem=look_recv,
        device_id={"ground": me, "pair": 1 - mine},
        device_id_type=MESH,
    ).wait()

    def split(value):
        first = value.astype(jnp.bfloat16)
        return first, (value - first.astype(jnp.float32)).astype(jnp.bfloat16)

    flip = 1.0 - 2.0 * mine.astype(jnp.float32)
    lanes = lax.broadcasted_iota(jnp.int32, (device_count, LANES), 1)
    sign = jnp.where(lanes < 64, 1.0, flip)
    field = jnp.concatenate([looked_in[:, 0, :] * sign, looked_in[:, 1, :] * sign], axis=1)
    first, second = split(field)
    field = jnp.dot(
        jnp.concatenate([first, second, first], axis=1), row_dft[...], preferred_element_type=jnp.float32
    )
    field = jnp.concatenate([field[:, :LANES], field[:, LANES:]], axis=0)
    length = out.shape[1]
    turn = jnp.where(lax.broadcasted_iota(jnp.int32, (length, 2 * length), 1) < length, 1.0, -1.0)
    first, second = split(field)
    both = jnp.dot(
        left[...], jnp.concatenate([first, second, first], axis=0), preferred_element_type=jnp.float32
    )
    spectrum = both[:length] + turn * pltpu.roll(both[length:], length, 1)
    power = spectrum * spectrum
    power = power + pltpu.roll(power, length, 1)
    weight = jnp.sqrt(jnp.sqrt(power + 1e-06))
    mean = jnp.sum(weight) * (1.0 / (2 * length * length))
    spectrum = spectrum * (weight / mean)
    first, second = split(spectrum)
    both = jnp.dot(
        left[...], jnp.concatenate([first, second, first], axis=0), preferred_element_type=jnp.float32
    )
    back = both[:length] - turn * pltpu.roll(both[length:], length, 1)
    first, second = split(back)
    result = lax.dot_general(
        back_mat[...],
        jnp.concatenate([first, second, first], axis=1),
        (((1,), (1,)), ((), ())),
        preferred_element_type=jnp.float32,
    ) * (1.0 / (length * length))
    out[0] = result[:length]
    out[1] = result[length:]


def constants():
    row = np.arange(1024)
    col = np.arange(256)
    lane, group = row % 128, row // 128
    part = np.stack(
        [
            (lane[:, None] // 32 == spot)
            & (col[None, :] // 128 == lane[:, None] // 16 % 2)
            & (col[None, :] % 128 // 16 == group[:, None])
            & (col[None, :] % 16 == lane[:, None] % 16)
            for spot in range(4)
        ]
    ).astype(jnp.bfloat16)
    row = np.arange(256)
    widen = np.stack(
        [
            (row[:, None] // 128 == col[None, :] // 16 % 2)
            & (row[:, None] % 128 // 16 == 2 * quarter + col[None, :] // 128)
            & (row[:, None] % 16 == col[None, :] % 16)
            for quarter in range(4)
        ]
    ).astype(jnp.bfloat16)
    low, high, slot = row // 128, row % 128 // 32, row % 32
    kind, box = (2 * high + low) // 4, (2 * high + low) % 4
    line = slot // 2 * 4 + box
    out_side, out_kind, frequency = col // 128, col // 64 % 2, col % 64
    angle = (line[:, None] * frequency[None, :] % 64) * (2.0 * math.pi / 64)
    mixed = np.where(
        kind[:, None] == out_kind[None, :],
        np.cos(angle),
        np.where(kind[:, None] == 0, -np.sin(angle), np.sin(angle)),
    )
    row_dft = np.where(slot[:, None] % 2 == out_side[None, :], mixed, 0.0)
    column = np.arange(64)
    angle = (column[:, None] * column[None, :] % 64) * (2.0 * math.pi / 64)
    cosine, sine = np.cos(angle), np.sin(angle)
    left = np.concatenate([cosine, sine], 0)
    back = np.block([[cosine, -sine], [sine, cosine]])

    def parts_of(value, axis):
        first = value.astype(np.float32).astype(jnp.bfloat16)
        second = (value - first.astype(np.float64)).astype(np.float32).astype(jnp.bfloat16)
        return np.concatenate([first, first, second], axis)

    return part, widen, parts_of(row_dft, 0), parts_of(left, 1), parts_of(back, 1)


def local_pair(coregistered_sweeps, shard_opening_height, shard_goal_patch, shard_patch_place):
    tile_count = lax.axis_size("ground")
    level_count = tile_count // 4
    tables = constants()
    vmem = pl.BlockSpec(memory_space=pltpu.VMEM)
    anyplace = pl.BlockSpec(memory_space=pltpu.HBM)
    dma = pltpu.SemaphoreType.DMA
    filtered = pl.pallas_call(
        fused_kernel,
        out_shape=pltpu.VMEM((2, 64, 64), jnp.float32),
        in_specs=[anyplace] * 9,
        out_specs=vmem,
        scratch_shapes=[
            pltpu.VMEM((512, 2, 512), jnp.bfloat16),
            pltpu.VMEM((3, 1, 64), jnp.int32),
            pltpu.VMEM((4, 1024, 256), jnp.bfloat16),
            pltpu.VMEM((4, 256, 256), jnp.bfloat16),
            pltpu.VMEM((3 * 256, 256), jnp.bfloat16),
            pltpu.VMEM((128, 3 * 64), jnp.bfloat16),
            pltpu.VMEM((128, 3 * 128), jnp.bfloat16),
            pltpu.VMEM((2 * tile_count, 128, 128), jnp.bfloat16),
            pltpu.VMEM((tile_count, 2, 128, 128), jnp.bfloat16),
            pltpu.VMEM((1, 128), jnp.int32),
            pltpu.VMEM((tile_count, 1, 128), jnp.int32),
            pltpu.SMEM((tile_count, 1, 128), jnp.int32),
            pltpu.VMEM((1024, 128), jnp.float32),
            pltpu.VMEM((9 * tile_count * 64, 128), jnp.float32),
            pltpu.VMEM((tile_count * SLOTS, tile_count * 64), jnp.bfloat16),
            pltpu.VMEM((tile_count * SLOTS, 128), jnp.float32),
            pltpu.VMEM((4, tile_count * SLOTS, 256), jnp.float32),
            pltpu.VMEM((tile_count, 2, 128), jnp.float32),
            pltpu.VMEM((2 * tile_count, 2, 128), jnp.float32),
            pltpu.VMEM((4, 128, 1024), jnp.bfloat16),
            dma((8,)),
            dma((4,)),
            dma,
            dma((tile_count,)),
            dma,
            dma,
            dma,
            dma,
            dma,
            pltpu.SemaphoreType.REGULAR((level_count,)),
        ],
        compiler_params=pltpu.CompilerParams(
            collective_id=0, has_side_effects=True, vmem_limit_bytes=CAP_VMEM
        ),
    )(
        coregistered_sweeps[0, 0],
        shard_opening_height.reshape(1, -1),
        shard_goal_patch.reshape(1, -1),
        shard_patch_place.reshape(1, -1),
        *tables,
    )
    return filtered[None, None, None]


def solution(mesh):
    placed = (P("pair", "ground", None, None, None), P("ground"), P("ground", None), P("ground"))
    return jax.shard_map(
        local_pair if dict(mesh.shape) == {"ground": 16, "pair": 2} else local,
        mesh=mesh,
        in_specs=placed,
        out_specs=P("pair", None, "ground", None, None, None),
        check_vma=False,
    )
```
